32 devices in a mesh: patch: 16 (over z, x, core), sec: 2 (over y).
Axes of the slice: x: 2, y: 2, z: 4, core: 2. Of those that a mesh axis runs over, the one named last changes fastest.
Arguments:
- concentration: float32 [16, 8, 128, 128], P('patch', 'sec'), may hold values from -1 to 1
- partner: int32 [16, 4], replicated, may hold values from 0 to 15, as said below
- face_id: int32 [16, 4], replicated, may hold values from 0 to 3, as said below
- flip: int32 [16, 4], replicated, may hold values from 0 to 1, as said below
Outputs:
- evolved: float32 [16, 8, 128, 128], P('patch', 'sec')
The draws below stay inside these ranges and needn't reach their ends.
Inputs may be any that keep to these rules, and one draw needn't show every extreme that they name: Across face f of patch p lies face face_id[p, f] of patch partner[p, f], and across that face lies face f of patch p again; the four partners of a patch are four different patches, none of them p itself. `face_id`: see partner. `flip`: equal on the two sides of an interface.
All inputs are finite; a program needn't handle non-finite values.
Results may differ from the reference program's by a relative error of at most 0.0001.
Values sent between devices are 32-bit elements; how exact they have to be, the bound alone decides.
No kernel may reach another device: no remote copies, remote signals or barrier semaphores. Data moves between devices by JAX's collectives and lax.ppermute only.
A program may use at most 64 MiB of HBM per device.

```python
import jax
import jax.numpy as jnp
from jax import lax

CP = 128
ITERS = 3
STEPS = 2
PATCHES = 16
CZT = 8


def interfaces(key):
    patch_count = PATCHES
    ordering = jax.random.permutation(jax.random.fold_in(key, 11), patch_count).astype(jnp.int32)
    position = jnp.argsort(ordering).astype(jnp.int32)
    stride = jax.random.randint(jax.random.fold_in(key, 12), (), 2, patch_count // 2).astype(jnp.int32)
    subkeys = jax.random.split(jax.random.fold_in(key, 13), patch_count)
    labels = jax.vmap(lambda subkey: jax.random.permutation(subkey, 4))(subkeys).astype(jnp.int32)
    flip_bits = jax.random.randint(jax.random.fold_in(key, 14), (2, patch_count), 0, 2).astype(jnp.int32)
    flip_bits = flip_bits.at[0, 0].set(1).at[1, 0].set(0)
    ahead_one = ordering[(position + 1) % patch_count]
    behind_one = ordering[(position - 1) % patch_count]
    ahead_far = ordering[(position + stride) % patch_count]
    behind_far = ordering[(position - stride) % patch_count]
    role_partner = jnp.stack([ahead_one, behind_one, ahead_far, behind_far], axis=1)
    back_role = jnp.array([1, 0, 3, 2], dtype=jnp.int32)
    role_face = labels[role_partner, back_role[None, :]]
    role_flip = jnp.stack([flip_bits[0, position], flip_bits[0, (position - 1) % patch_count], flip_bits[1, position], flip_bits[1, (position - stride) % patch_count]], axis=1)
    row_ids = jnp.broadcast_to(jnp.arange(patch_count, dtype=jnp.int32)[:, None], (patch_count, 4))
    empty = jnp.zeros((patch_count, 4), jnp.int32)
    partner = empty.at[row_ids, labels].set(role_partner)
    face_id = empty.at[row_ids, labels].set(role_face)
    flip = empty.at[row_ids, labels].set(role_flip)
    return (partner, face_id, flip)


def draw_partner(key, part):
    return interfaces(key)[0]


def draw_face_id(key, part):
    return interfaces(key)[1]


def draw_flip(key, part):
    return interfaces(key)[2]


def draw_concentration(key, part):
    serial = jnp.arange(PATCHES, dtype=jnp.float32)[:, None] * CZT + jnp.arange(CZT, dtype=jnp.float32)[None, :]
    fraction = serial / (PATCHES * CZT - 1.0)
    amplitude = (0.3 * jnp.exp(jnp.log(3.0) * fraction))[:, :, None, None]
    shape = (PATCHES, CZT, CP, CP)
    noise = jax.random.uniform(key, shape, jnp.float32, -1.0, 1.0)
    values = amplitude * noise
    return values.astype(jnp.float32)


def setup_inputs(seed: int = 0) -> dict:
    seeds = jax.random.split(jax.random.key(seed), 5)
    return {
        "concentration": draw_concentration(jax.random.fold_in(seeds[4], 71), 0),
        "partner": draw_partner(jax.random.fold_in(seeds[4], 71), 0),
        "face_id": draw_face_id(jax.random.fold_in(seeds[4], 71), 0),
        "flip": draw_flip(jax.random.fold_in(seeds[4], 71), 0),
    }


MASS_BAND = (2416.0 / 5040.0, 1191.0 / 5040.0, 120.0 / 5040.0, 1.0 / 5040.0)
STIFF_BAND = (2.0 / 3.0, -0.125, -0.2, -1.0 / 120.0)
PENALTY = 2.0
TIME_STEP = 1.0
STABILIZER = 2.0
GRADIENT_ENERGY = 0.5


def banded_padded(padded, coefficients, along, length):
    summed = coefficients[0] * lax.slice_in_dim(padded, 3, 3 + length, axis=along)
    for offset in range(1, 4):
        lower = lax.slice_in_dim(padded, 3 - offset, 3 - offset + length, axis=along)
        upper = lax.slice_in_dim(padded, 3 + offset, 3 + offset + length, axis=along)
        summed = summed + coefficients[offset] * (lower + upper)
    return summed


def banded(field, coefficients, along):
    length = field.shape[along]
    widths = [(0, 0)] * field.ndim
    widths[along] = (3, 3)
    return banded_padded(jnp.pad(field, widths), coefficients, along, length)


def tensor_parts(mass_third, stiff_third, first_axis, second_axis):
    mass_both = banded(mass_third, MASS_BAND, second_axis)
    stiff_second = banded(mass_third, STIFF_BAND, second_axis)
    mixed_second = banded(stiff_third, MASS_BAND, second_axis)
    stiffness = banded(mass_both, STIFF_BAND, first_axis) + banded(stiff_second + mixed_second, MASS_BAND, first_axis)
    return mass_both, stiffness


def face_traces(field):
    return jnp.stack([field[..., 0, :], field[..., -1, :], field[..., :, 0], field[..., :, -1]], axis=field.ndim - 3)


def add_penalty(stiffness, mismatch, face_axis):
    pieces = [lax.index_in_dim(mismatch, number, face_axis, keepdims=False) for number in range(4)]
    stiffness = stiffness.at[..., 0, :].add(PENALTY * pieces[0])
    stiffness = stiffness.at[..., -1, :].add(PENALTY * pieces[1])
    stiffness = stiffness.at[..., :, 0].add(PENALTY * pieces[2])
    stiffness = stiffness.at[..., :, -1].add(PENALTY * pieces[3])
    return stiffness


def stiffness_full(field, partner, face_id, flip, with_mass):
    mass_third = banded(field, MASS_BAND, 1)
    stiff_third = banded(field, STIFF_BAND, 1)
    mass_both, stiffness = tensor_parts(mass_third, stiff_third, 2, 3)
    traces = face_traces(field)
    others = traces[partner, face_id]
    others = jnp.where(flip[:, :, None, None] == 1, others[..., ::-1], others)
    stiffness = add_penalty(stiffness, traces - others, 1)
    mass_full = banded(mass_both, MASS_BAND, 2) if with_mass else None
    return mass_full, stiffness


def reference(concentration, partner, face_id, flip):
    def operate(direction):
        mass_full, stiff_one = stiffness_full(direction, partner, face_id, flip, True)
        unused, stiff_two = stiffness_full(stiff_one, partner, face_id, flip, False)
        return mass_full + (TIME_STEP * STABILIZER) * stiff_one + (TIME_STEP * GRADIENT_ENERGY) * stiff_two

    iterate = concentration
    for section in range(STEPS):
        current = iterate
        unused, curvature = stiffness_full(current, partner, face_id, flip, False)
        potential = current * current * current - current + GRADIENT_ENERGY * curvature
        unused, flux = stiffness_full(potential, partner, face_id, flip, False)
        residual = -TIME_STEP * flux
        direction = residual
        norm_now = jnp.sum(residual * residual)
        for iteration in range(ITERS):
            image = operate(direction)
            step_size = norm_now / jnp.sum(direction * image)
            iterate = iterate + step_size * direction
            if iteration + 1 < ITERS:
                residual = residual - step_size * image
                norm_next = jnp.sum(residual * residual)
                direction = residual + (norm_next / norm_now) * direction
                norm_now = norm_next
    return iterate
```

```python
import functools

import jax
import jax.numpy as jnp
import numpy as np
from jax import lax
from jax.experimental import pallas as pl
from jax.experimental.pallas import tpu as pltpu
from jax.sharding import PartitionSpec as P

STEPS = 2
MASS_BAND = (2416.0 / 5040.0, 1191.0 / 5040.0, 120.0 / 5040.0, 1.0 / 5040.0)
STIFF_BAND = (2.0 / 3.0, -0.125, -0.2, -1.0 / 120.0)
PENALTY = 2.0
TIME_STEP = 1.0
STABILIZER = 2.0
GRADIENT_ENERGY = 0.5
HALF = TIME_STEP * GRADIENT_ENERGY
TWICE = TIME_STEP * STABILIZER
EXACT = lax.Precision.HIGHEST
LANES = 128
TABLE = 8


def band_matrix(band, size):
    out = np.zeros((size, size), np.float32)
    for offset, value in enumerate(band):
        for row in range(size - offset):
            out[row, row + offset] = value
            out[row + offset, row] = value
    return out


def dot(left, right):
    return jnp.dot(left, right, precision=EXACT, preferred_element_type=jnp.float32)


def constants(depth):
    mass, stiff = band_matrix(MASS_BAND, LANES), band_matrix(STIFF_BAND, LANES)
    zero = np.zeros_like(mass)
    right = np.block([[mass, stiff], [zero, mass]])
    left = np.block([[stiff, mass], [mass, zero]])
    reverse = np.ascontiguousarray(np.eye(LANES, dtype=np.float32)[::-1])
    four = np.eye(4, dtype=np.float32)
    third = np.concatenate(
        [
            np.kron(four, band_matrix(MASS_BAND, depth)),
            np.kron(four, band_matrix(STIFF_BAND, depth)),
        ],
        axis=1,
    )
    return right, left, reverse, third


class Body:
    def __init__(self, depth, patches, tables, consts, scratch):
        self.depth, self.patches, self.tables = depth, patches, tables
        self.right, self.left, self.reverse, self.third = consts
        self.pair, self.strip, self.turned = scratch
        self.me = tables[12 * patches]
        self.lane = lax.broadcasted_iota(jnp.int32, (depth, LANES), 1)
        self.first, self.last = self.lane == 0, self.lane == LANES - 1

    def partner(self, patch, face):
        return self.tables[patch * 4 + face]

    def face_id(self, patch, face):
        return self.tables[4 * self.patches + patch * 4 + face]

    def flip(self, patch, face):
        return self.tables[8 * self.patches + patch * 4 + face]

    def stiff0(self, layer, store, mass=None):
        depth = self.depth
        for z in range(depth):
            middle = layer(z)
            massed, stiffed = MASS_BAND[0] * middle, STIFF_BAND[0] * middle
            for offset in (1, 2, 3):
                near = [layer(k) for k in (z - offset, z + offset) if 0 <= k < depth]
                if near:
                    both = near[0] if len(near) == 1 else near[0] + near[1]
                    massed = massed + MASS_BAND[offset] * both
                    stiffed = stiffed + STIFF_BAND[offset] * both
            mixed = dot(jnp.concatenate([massed, stiffed], axis=1), self.right[...])
            self.pair[:LANES, z * LANES : (z + 1) * LANES] = mixed[:, :LANES]
            self.pair[LANES:, z * LANES : (z + 1) * LANES] = mixed[:, LANES:]
        rows = LANES if mass is None else 2 * LANES
        for z in range(depth):
            both = dot(self.left[:rows], self.pair[:, z * LANES : (z + 1) * LANES])
            store(z, both[:LANES])
            if mass is not None:
                mass(z, both[LANES:])

    def strips(self, field):
        depth = self.depth
        lane = lax.broadcasted_iota(jnp.int32, (LANES, LANES), 1)
        rows0 = [field[:, d, :] for d in range(4)]
        rows1 = [field[:, LANES - 1 - d, :] for d in range(4)]
        pieces = [[] for _ in range(8)]
        for start in range(0, depth, 8):
            stacked = jnp.zeros((LANES, LANES), jnp.float32)
            for j in range(8):
                rolled = pltpu.roll(field[start + j], (8 * j + 4) % LANES, 1)
                stacked = jnp.where((lane >> 3) == j, rolled, stacked)
            self.strip[...] = jnp.transpose(stacked)
            for i in range(8):
                pieces[i].append(self.strip[pl.ds(i, 8, stride=8), :])
        columns = [jnp.concatenate(p, axis=0) if len(p) > 1 else p[0] for p in pieces]
        return [rows0, rows1, columns[4:], columns[3::-1]]

    def traces(self, field):
        return [strip[0] for strip in self.strips(field)]

    def jumps(self, mine, other):
        return [PENALTY * (a - b) for a, b in zip(mine, other)]

    def add_faces(self, field, jump):
        depth = self.depth
        lane = lax.broadcasted_iota(jnp.int32, (LANES, LANES), 1)
        edge = (lane == 0) | (lane == LANES - 1)
        for start in range(0, depth, 8):
            self.turned[pl.ds(0, 8, stride=2), :] = jump[3][start : start + 8]
            self.turned[pl.ds(1, 8, stride=2), :] = jump[2][start : start + 8]
            stood = jnp.transpose(self.turned[...])
            for j in range(8):
                rolled = pltpu.roll(stood, (LANES - 2 * j - 1) % LANES, 1)
                z = start + j
                field[z] = field[z] + jnp.where(edge, rolled, 0.0)
        field[:, 0, :] = field[:, 0, :] + jump[0]
        field[:, LANES - 1, :] = field[:, LANES - 1, :] + jump[1]

    def slab(self, stiffs, masses):
        n = 4 * self.depth
        both = dot(
            jnp.concatenate([jnp.concatenate(masses, 0), jnp.concatenate(stiffs, 0)], 0),
            self.right[:LANES],
        )
        lower = both[n:, :LANES] + both[:n, LANES:]
        out = dot(self.third[...], jnp.concatenate([lower, both[:n, :LANES]], 0))
        return [out[f * self.depth : (f + 1) * self.depth] for f in range(4)]

    def depth_sum(self, strip, band):
        out = band[0] * strip[0]
        for d in (1, 2, 3):
            out = out + band[d] * strip[d]
        return out

    def corner_table(self, trace, inner=None):
        table = jnp.zeros((self.depth, LANES), jnp.float32)
        ends = (0, LANES - 1)
        if inner is not None:
            arms = dot(jnp.concatenate(trace, 0), self.right[:LANES])
        for rs in range(2):
            for cs in range(2):
                slot = TABLE * (2 * rs + cs)
                values = [(trace[rs], ends[cs])]
                if inner is not None:
                    values.append((inner[rs], ends[cs]))
                    for face, end in ((rs, ends[cs]), (2 + cs, ends[rs])):
                        part = arms[face * self.depth : (face + 1) * self.depth]
                        values.append((part[:, :LANES], end))
                        values.append((part[:, LANES:], end))
                for kind, (value, end) in enumerate(values):
                    rolled = pltpu.roll(value, (slot + kind - end) % LANES, 1)
                    table = jnp.where(self.lane == slot + kind, rolled, table)
        return table

    def send(self, payload, groups, table):
        depth = self.depth
        for f in range(4):
            to = self.partner(self.me, f)
            for i, group in enumerate(groups):
                payload[to, i * depth : (i + 1) * depth, :] = group[f]
        if table is not None:
            at = len(groups) * depth
            for to in range(self.patches):
                payload[to, at : at + depth, :] = table

    def received(self, recv, count):
        depth = self.depth
        rows = count * depth
        raw = [recv[self.partner(self.me, f), :rows, :] for f in range(4)]
        turned = dot(jnp.concatenate(raw, 0), self.reverse[...])
        out = []
        for f in range(4):
            flipped = self.flip(self.me, f) == 1
            out.append(jnp.where(flipped, turned[f * rows : (f + 1) * rows], raw[f]))
        return [[out[f][i * depth : (i + 1) * depth] for f in range(4)] for i in range(count)]

    def corner(self, face, side):
        q, f1 = self.partner(self.me, face), self.face_id(self.me, face)
        eq = side ^ self.flip(self.me, face)
        s1 = f1 & 1
        upright = f1 < 2
        f2 = jnp.where(upright, 2 + eq, eq)
        kq = jnp.where(upright, 2 * s1 + eq, 2 * eq + s1)
        tq = jnp.where(upright, 4, 2)
        r, g = self.partner(q, f2), self.face_id(q, f2)
        s2 = s1 ^ self.flip(q, f2)
        flat = g < 2
        k = jnp.where(flat, 2 * (g & 1) + s2, 2 * s2 + (g & 1))
        t = jnp.where(flat, 2, 4)
        g2 = jnp.where(flat, 2 + s2, s2)
        r2, h = self.partner(r, g2), self.face_id(r, g2)
        s4 = (g & 1) ^ self.flip(r, g2)
        k2 = jnp.where(h < 2, 2 * (h & 1) + s4, 2 * s4 + (h & 1))
        return (q, kq, tq), (r, k, t), (r2, k2)

    def look(self, recv, at, patch, lane, side):
        end = side * (LANES - 1)
        shift = (end + LANES - lane) & (LANES - 1)
        return pltpu.roll(recv[patch, at : at + self.depth, :], shift, 1)

    def ends(self, low, high):
        return jnp.where(self.first, low, jnp.where(self.last, high, 0.0))

    def other_stiff(self, recv, at, mine, theirs, inner, corners):
        out = []
        for f in range(4):
            across = self.ends(
                *[
                    self.look(recv, at, corners[f][s][1][0], TABLE * corners[f][s][1][1], s)
                    for s in range(2)
                ]
            )
            edge = self.first | self.last
            value = inner[f] + PENALTY * (theirs[f] - mine[f])
            out.append(value + jnp.where(edge, PENALTY * (theirs[f] - across), 0.0))
        return out

    def corners(self):
        return [[self.corner(f, s) for s in range(2)] for f in range(4)]


def stack(values):
    return jnp.concatenate(values, 0)


def unstack(ref, depth):
    return [ref[f * depth : (f + 1) * depth, :] for f in range(4)]


def start_kernel(depth, patches, tables, right, left, reverse, third, c, v0, payload, *scratch):
    body = Body(depth, patches, tables, (right, left, reverse, third), scratch)
    body.stiff0(lambda z: c[z], lambda z, x: v0.__setitem__(z, x))
    trace = body.traces(c)
    body.send(payload, [trace, body.traces(v0)], body.corner_table(trace))


def flux_tail(body, sc, current, other_c, other_sc, r0, v1, m1, payload, potential):
    depth = body.depth
    for z in range(depth):
        x = current[z]
        potential[z] = x * x * x - x + GRADIENT_ENERGY * sc[z]
    other = [x * x * x - x + GRADIENT_ENERGY * s for x, s in zip(other_c, other_sc)]
    body.stiff0(lambda z: potential[z], lambda z, x: r0.__setitem__(z, x))
    body.add_faces(r0, body.jumps(body.traces(potential), other))
    for z in range(depth):
        r0[z] = -TIME_STEP * r0[z]
    body.stiff0(
        lambda z: r0[z],
        lambda z, x: v1.__setitem__(z, x),
        lambda z, x: m1.__setitem__(z, x),
    )
    trace = body.traces(r0)
    body.send(payload, [trace, body.traces(v1)], body.corner_table(trace))


def first_kernel(depth, patches, tables, right, left, reverse, third, c, v0, recv,
                 sc, r0, v1, m1, sides, payload, potential, *scratch):
    body = Body(depth, patches, tables, (right, left, reverse, third), scratch)
    other, inner = body.received(recv, 2)
    mine = body.traces(c)
    sc[...] = v0[...]
    body.add_faces(sc, body.jumps(mine, other))
    other_s = body.other_stiff(recv, 2 * depth, mine, other, inner, body.corners())
    sides[0] = stack(other)
    sides[1] = stack(other_s)
    flux_tail(body, sc, c, other, other_s, r0, v1, m1, payload, potential)


def second_kernel(depth, patches, tables, right, left, reverse, third, r0, v1, m1, recv,
                  u1, y, v2, m2, sides, payload, *scratch):
    body = Body(depth, patches, tables, (right, left, reverse, third), scratch)
    other, inner = body.received(recv, 2)
    mine = body.traces(r0)
    u1[...] = v1[...]
    body.add_faces(u1, body.jumps(mine, other))
    other_s = body.other_stiff(recv, 2 * depth, mine, other, inner, body.corners())
    sides[0] = stack(other)
    sides[1] = stack(other_s)
    body.stiff0(lambda z: u1[z], lambda z, x: y.__setitem__(z, x))
    body.add_faces(y, body.jumps(body.traces(u1), other_s))
    for z in range(depth):
        y[z] = m1[z] + TWICE * u1[z] + HALF * y[z]
    body.stiff0(
        lambda z: y[z],
        lambda z, x: v2.__setitem__(z, x),
        lambda z, x: m2.__setitem__(z, x),
    )
    trace = body.traces(y)
    strips = body.strips(v2)
    inner = [s[0] for s in strips]
    twice = body.slab(
        [body.depth_sum(s, STIFF_BAND) for s in strips],
        [body.depth_sum(s, MASS_BAND) for s in strips],
    )
    image = [m + TWICE * a + HALF * b for m, a, b in zip(body.traces(m2), inner, twice)]
    body.send(payload, [trace, inner, image], body.corner_table(trace, inner))


def third_kernel(depth, patches, tables, right, left, reverse, third, r0, y, v2, m2, recv,
                 u2, w, zf, sides, payload, mw, *scratch):
    body = Body(depth, patches, tables, (right, left, reverse, third), scratch)
    at = 3 * depth
    other, inner, image = body.received(recv, 3)
    corners = body.corners()
    mine = body.traces(y)
    u2[...] = v2[...]
    body.add_faces(u2, body.jumps(mine, other))
    other_s = body.other_stiff(recv, at, mine, other, inner, corners)
    mine_s = body.traces(u2)
    masses, stiffs, far = [], [], []
    for f in range(4):
        arm_m, arm_k, across = [], [], []
        for s in range(2):
            (q, kq, tq), (r, k, t), (r2, k2) = corners[f][s]
            look = functools.partial(body.look, recv, at, side=s)
            arm_m.append(look(q, TABLE * kq + tq) - look(r, TABLE * k + t))
            arm_k.append(look(q, TABLE * kq + tq + 1) - look(r, TABLE * k + t + 1))
            value = look(r, TABLE * k)
            across.append(
                look(r, TABLE * k + 1)
                + PENALTY * (value - other[f])
                + PENALTY * (value - look(r2, TABLE * k2))
            )
        jump = PENALTY * (other[f] - mine[f])
        masses.append(MASS_BAND[0] * jump + PENALTY * body.ends(*arm_m))
        stiffs.append(STIFF_BAND[0] * jump + PENALTY * body.ends(*arm_k))
        far.append(body.ends(*across))
    pushed = body.slab(stiffs, masses)
    edge = body.first | body.last
    other_w = []
    for f in range(4):
        again = pushed[f] + PENALTY * (other_s[f] - mine_s[f])
        again = again + jnp.where(edge, PENALTY * (other_s[f] - far[f]), 0.0)
        other_w.append(image[f] + TWICE * (other_s[f] - inner[f]) + HALF * again)
    sides[0] = stack(other)
    sides[1] = stack(other_s)
    sides[2] = stack(other_w)
    body.stiff0(lambda z: u2[z], lambda z, x: w.__setitem__(z, x))
    body.add_faces(w, body.jumps(mine_s, other_s))
    for z in range(depth):
        w[z] = m2[z] + TWICE * u2[z] + HALF * w[z]
    body.stiff0(
        lambda z: w[z],
        lambda z, x: zf.__setitem__(z, x),
        lambda z, x: mw.__setitem__(z, x),
    )
    body.add_faces(zf, body.jumps(body.traces(w), other_w))
    sums = [jnp.zeros((8, LANES), jnp.float32)] * 6
    for z in range(depth):
        a, b, x, s = r0[z], y[z], w[z], zf[z]
        last = x * (mw[z] + TWICE * s) + HALF * (s * s)
        for i, product in enumerate((a * a, a * b, b * b, b * x, x * x, last)):
            sums[i] = sums[i] + jnp.sum(product.reshape(LANES // 8, 8, LANES), axis=0)
    moments = [jnp.sum(s, axis=0, keepdims=True) for s in sums]
    moments = jnp.concatenate(moments + [jnp.zeros((2, LANES), jnp.float32)], 0)
    trace = body.traces(zf)
    for f in range(4):
        payload[body.partner(body.me, f), 8 : 8 + depth, :] = trace[f]
    for to in range(patches):
        payload[to, :8, :] = moments


def weights(patches, recv):
    total = recv[0, :8, :]
    for p in range(1, patches):
        total = total + recv[p, :8, :]
    total = jnp.sum(total, axis=1, keepdims=True)
    m0, m1, m2, m3, m4, m5 = [total[i : i + 1] for i in range(6)]
    a0 = m0 / m1
    rr1 = m0 - 2.0 * a0 * m1 + a0 * a0 * m2
    p0, p1 = 1.0 + rr1 / m0, -a0
    a1 = rr1 / (p0 * p0 * m1 + 2.0 * p0 * p1 * m2 + p1 * p1 * m3)
    q1, q2 = -a0 - a1 * p0, -a1 * p1
    rr2 = m0 + q1 * q1 * m2 + q2 * q2 * m4 + 2.0 * (q1 * m1 + q2 * m2 + q1 * q2 * m3)
    b1 = rr2 / rr1
    s0, s1, s2 = 1.0 + b1 * p0, q1 + b1 * p1, q2
    a2 = rr2 / (
        s0 * s0 * m1
        + s1 * s1 * m3
        + s2 * s2 * m5
        + 2.0 * (s0 * s1 * m2 + s0 * s2 * m3 + s1 * s2 * m4)
    )
    return a0 + a1 * p0 + a2 * s0, a1 * p1 + a2 * s1, a2 * s2


def next_kernel(depth, patches, tables, right, left, reverse, third,
                c, r0, y, w, sc, u1, u2, zf, side_c, side_r, side_y, recv,
                cn, rn, v1, m1, payload, scn, potential, *scratch):
    body = Body(depth, patches, tables, (right, left, reverse, third), scratch)
    x0, x1, x2 = weights(patches, recv)
    for z in range(depth):
        cn[z] = c[z] + x0 * r0[z] + x1 * y[z] + x2 * w[z]
        scn[z] = sc[z] + x0 * u1[z] + x1 * u2[z] + x2 * zf[z]
    raw = [recv[body.partner(body.me, f), 8 : 8 + depth, :] for f in range(4)]
    turned = dot(stack(raw), reverse[...])
    side_z = []
    for f in range(4):
        flipped = body.flip(body.me, f) == 1
        side_z.append(jnp.where(flipped, turned[f * depth : (f + 1) * depth], raw[f]))
    other, other_s = [], []
    for f in range(4):
        at = slice(f * depth, (f + 1) * depth)
        other.append(side_c[0, at] + x0 * side_r[0, at] + x1 * side_y[0, at] + x2 * side_y[2, at])
        other_s.append(side_c[1, at] + x0 * side_r[1, at] + x1 * side_y[1, at] + x2 * side_z[f])
    flux_tail(body, scn, cn, other, other_s, rn, v1, m1, payload, potential)


def last_kernel(depth, patches, sec, c, r0, y, w, recv, out):
    x0, x1, x2 = weights(patches, recv)
    rows = out.shape[0]
    for z in range(rows):
        k = sec[0] * rows + z
        out[z] = c[k] + x0 * r0[k] + x1 * y[k] + x2 * w[k]


def shards(patches, concentration, partner, face_id, flip):
    c = lax.all_gather(concentration[0], "sec", axis=0, tiled=True)
    depth = c.shape[0]
    me = lax.axis_index("patch").astype(jnp.int32)
    sec = lax.axis_index("sec").astype(jnp.int32)[None]
    tables = jnp.concatenate([partner.reshape(-1), face_id.reshape(-1), flip.reshape(-1), me[None]])
    consts = [jnp.asarray(x) for x in constants(depth)]
    field = jax.ShapeDtypeStruct((depth, LANES, LANES), jnp.float32)

    def sides(count):
        return jax.ShapeDtypeStruct((count, 4 * depth, LANES), jnp.float32)

    def load(rows):
        return jax.ShapeDtypeStruct((patches, rows, LANES), jnp.float32)

    def call(kernel, outs, *args, fields=0):
        scratch = [pltpu.VMEM((depth, LANES, LANES), jnp.float32)] * fields + [
            pltpu.VMEM((2 * LANES, depth * LANES), jnp.float32),
            pltpu.VMEM((LANES, LANES), jnp.float32),
            pltpu.VMEM((LANES, LANES), jnp.float32),
        ]
        space = pl.BlockSpec(memory_space=pltpu.VMEM)
        return pl.pallas_call(
            functools.partial(kernel, depth, patches),
            out_shape=outs,
            in_specs=[pl.BlockSpec(memory_space=pltpu.SMEM)] + [space] * (len(consts) + len(args)),
            out_specs=[space] * len(outs),
            scratch_shapes=scratch,
            compiler_params=pltpu.CompilerParams(vmem_limit_bytes=48 << 20),
        )(tables, *consts, *args)

    def swap(payload):
        return lax.all_to_all(payload, "patch", 0, 0)

    v0, payload = call(start_kernel, [field, load(3 * depth)], c)
    sc, r0, v1, m1, side_c, payload = call(
        first_kernel, [field] * 4 + [sides(2), load(3 * depth)], c, v0, swap(payload), fields=1
    )
    for step in range(STEPS):
        u1, y, v2, m2, side_r, payload = call(
            second_kernel, [field] * 4 + [sides(2), load(4 * depth)], r0, v1, m1, swap(payload)
        )
        u2, w, zf, side_y, payload = call(
            third_kernel,
            [field] * 3 + [sides(3), load(8 + depth)],
            r0, y, v2, m2, swap(payload),
            fields=1,
        )
        if step + 1 == STEPS:
            break
        c, r0, v1, m1, payload = call(
            next_kernel,
            [field] * 4 + [load(3 * depth)],
            c, r0, y, w, sc, u1, u2, zf, side_c, side_r, side_y, swap(payload),
            fields=2,
        )
    rows = concentration.shape[1]
    space = pl.BlockSpec(memory_space=pltpu.VMEM)
    out = pl.pallas_call(
        functools.partial(last_kernel, depth, patches),
        out_shape=jax.ShapeDtypeStruct((rows, LANES, LANES), jnp.float32),
        in_specs=[pl.BlockSpec(memory_space=pltpu.SMEM)] + [space] * 5,
        out_specs=space,
        compiler_params=pltpu.CompilerParams(vmem_limit_bytes=48 << 20),
    )(sec, c, r0, y, w, swap(payload[:, :8, :]))
    return out[None]


def solution(mesh):
    placed = (P("patch", "sec", None, None), P(), P(), P())
    return jax.shard_map(
        functools.partial(shards, mesh.shape["patch"]),
        mesh=mesh,
        in_specs=placed,
        out_specs=P("patch", "sec", None, None),
        check_vma=False,
    )
```

```python
import functools

import jax
import jax.numpy as jnp
import numpy as np
from jax import lax
from jax.experimental import pallas as pl
from jax.experimental.pallas import tpu as pltpu
from jax.sharding import PartitionSpec as P

STEPS = 2
MASS_BAND = (2416.0 / 5040.0, 1191.0 / 5040.0, 120.0 / 5040.0, 1.0 / 5040.0)
STIFF_BAND = (2.0 / 3.0, -0.125, -0.2, -1.0 / 120.0)
SCALE = 5040.0
MASS_HIGH, MASS_LOW = (2416.0, 1192.0, 120.0, 1.0), (0.0, -1.0, 0.0, 0.0)
STIFF_HIGH, STIFF_LOW = (3360.0, -632.0, -1008.0, -42.0), (0.0, 2.0, 0.0, 0.0)
PENALTY = 2.0
TIME_STEP = 1.0
STABILIZER = 2.0
GRADIENT_ENERGY = 0.5
HALF = TIME_STEP * GRADIENT_ENERGY
TWICE = TIME_STEP * STABILIZER
EXACT = lax.Precision.HIGHEST
LANES = 128
PAD = 8
TABLE = 8
SUMS = 32


def band_matrix(band, size):
    out = np.zeros((size, size), np.float32)
    for offset, value in enumerate(band):
        for row in range(size - offset):
            out[row, row + offset] = value
            out[row + offset, row] = value
    return out


def dot(left, right):
    return jnp.dot(left, right, precision=EXACT, preferred_element_type=jnp.float32)


def right_matrix(mass_band, stiff_band):
    mass, stiff = band_matrix(mass_band, LANES), band_matrix(stiff_band, LANES)
    return np.block([[mass, stiff], [np.zeros_like(mass), mass]])


def constants(depth):
    high = right_matrix(MASS_HIGH, STIFF_HIGH).astype(jnp.bfloat16)
    low = right_matrix(MASS_LOW, STIFF_LOW).astype(jnp.bfloat16)
    plain = right_matrix(MASS_BAND, STIFF_BAND)[:LANES]
    reverse = np.ascontiguousarray(np.eye(LANES, dtype=np.float32)[::-1])
    four = np.eye(4, dtype=np.float32)
    third = np.concatenate(
        [
            np.kron(four, band_matrix(MASS_BAND, depth)),
            np.kron(four, band_matrix(STIFF_BAND, depth)),
        ],
        axis=1,
    )
    return high, low, plain, reverse, third


class Body:
    def __init__(self, sizes, refs):
        self.depth, self.patches, self.slabs = sizes
        self.tables, self.consts, self.scratch = refs[:3], refs[3:8], refs[8:]
        self.high, self.low, self.plain, self.reverse, self.third = self.consts
        self.near, self.strip, self.turned, self.stood = self.scratch
        self.me = lax.axis_index("patch")
        self.lane = lax.broadcasted_iota(jnp.int32, (self.depth, LANES), 1)
        self.first, self.last = self.lane == 0, self.lane == LANES - 1
        self.wide = lax.broadcasted_iota(jnp.int32, (LANES, LANES), 1)
        self.edge = (self.wide == 0) | (self.wide == LANES - 1)

    def partner(self, patch, face):
        return self.tables[0][patch, face]

    def face_id(self, patch, face):
        return self.tables[1][patch, face]

    def flip(self, patch, face):
        return self.tables[2][patch, face]

    def split(self, value):
        pieces = []
        for last in (False, False, True):
            piece = value.astype(jnp.bfloat16)
            pieces.append(piece)
            if not last:
                value = value - piece.astype(jnp.float32)
        return pieces

    def stiff0(self, layer, finish):
        depth = self.depth
        zeros = jnp.zeros((PAD, LANES), jnp.float32)
        for i in range(4):
            self.near[i, :PAD] = zeros
            self.near[i, PAD + LANES :] = zeros
        for z in range(depth):
            middle = layer(z)
            massed = (MASS_BAND[0] / SCALE) * middle
            stiffed = (STIFF_BAND[0] / SCALE) * middle
            for offset in (1, 2, 3):
                near = [layer(k) for k in (z - offset, z + offset) if 0 <= k < depth]
                if near:
                    both = near[0] if len(near) == 1 else near[0] + near[1]
                    massed = massed + (MASS_BAND[offset] / SCALE) * both
                    stiffed = stiffed + (STIFF_BAND[offset] / SCALE) * both
            pieces = self.split(jnp.concatenate([massed, stiffed], axis=1))
            mixed = None
            for matrix, parts in ((self.high, pieces), (self.low, pieces[:2])):
                for piece in parts:
                    term = jnp.dot(piece, matrix[...], preferred_element_type=jnp.float32)
                    mixed = term if mixed is None else mixed + term
            a, b = 2 * (z % 2), 2 * (z % 2) + 1
            self.near[a, PAD : PAD + LANES] = mixed[:, :LANES]
            self.near[b, PAD : PAD + LANES] = mixed[:, LANES:]
            stiff = STIFF_BAND[0] * mixed[:, :LANES] + MASS_BAND[0] * mixed[:, LANES:]
            mass = MASS_BAND[0] * mixed[:, :LANES]
            for o in (1, 2, 3):
                low, high = slice(PAD - o, PAD - o + LANES), slice(PAD + o, PAD + o + LANES)
                both = self.near[a, low] + self.near[a, high]
                stiff = stiff + STIFF_BAND[o] * both
                stiff = stiff + MASS_BAND[o] * (self.near[b, low] + self.near[b, high])
                mass = mass + MASS_BAND[o] * both
            finish(z, stiff, mass)

    def strips(self, field, count=4):
        depth = field.shape[0]
        group = min(depth, 8)
        rows0 = [field[:, d, :] for d in range(count)]
        rows1 = [field[:, LANES - 1 - d, :] for d in range(count)]
        wanted = list(range(4 - count, 4 + count))
        pieces = {i: [] for i in wanted}
        for start in range(0, depth, group):
            stacked = jnp.zeros((LANES, LANES), jnp.float32)
            for j in range(group):
                rolled = pltpu.roll(field[start + j], (8 * j + 4) % LANES, 1)
                stacked = jnp.where((self.wide >> 3) == j, rolled, stacked)
            self.strip[...] = jnp.transpose(stacked)
            for i in wanted:
                pieces[i].append(self.strip[pl.ds(i, group, stride=8), :])
        columns = {i: jnp.concatenate(p, axis=0) if len(p) > 1 else p[0] for i, p in pieces.items()}
        return [
            rows0,
            rows1,
            [columns[4 + d] for d in range(count)],
            [columns[3 - d] for d in range(count)],
        ]

    def traces(self, field):
        return [strip[0] for strip in self.strips(field, 1)]

    def jumps(self, mine, other):
        return [PENALTY * (a - b) for a, b in zip(mine, other)]

    def stand(self, jump):
        for start in range(0, self.depth, 8):
            self.turned[pl.ds(0, 8, stride=2), :] = jump[3][start : start + 8]
            self.turned[pl.ds(1, 8, stride=2), :] = jump[2][start : start + 8]
            self.stood[start // 8] = jnp.transpose(self.turned[...])

    def column(self, z):
        rolled = pltpu.roll(self.stood[z // 8], (LANES - 2 * (z % 8) - 1) % LANES, 1)
        return jnp.where(self.edge, rolled, 0.0)

    def add_rows(self, field, jump, factor):
        field[:, 0, :] = field[:, 0, :] + factor * jump[0]
        field[:, LANES - 1, :] = field[:, LANES - 1, :] + factor * jump[1]

    def stiff_trace(self, inner, jump):
        out = []
        for f in range(4):
            side = f & 1
            low, high = (2, 3) if f < 2 else (0, 1)
            at = side * (LANES - 1)
            ends = []
            for face, end in ((low, 0), (high, LANES - 1)):
                shift = (end - at) % LANES
                ends.append(pltpu.roll(jump[face], shift, 1) if shift else jump[face])
            out.append(inner[f] + jump[f] + self.ends(*ends))
        return out

    def slab(self, stiffs, masses, plain=None):
        n = 4 * self.depth
        rows = [stack(masses), stack(stiffs)] + ([] if plain is None else [stack(plain)])
        both = dot(stack(rows), self.plain[...])
        lower = both[n : 2 * n, :LANES] + both[:n, LANES:]
        if plain is not None:
            lower = lower + both[2 * n :, :LANES]
        out = dot(self.third[...], stack([lower, both[:n, :LANES]]))
        return unstack(out, self.depth)

    def depth_sum(self, strip, band):
        out = band[0] * strip[0]
        for d in (1, 2, 3):
            out = out + band[d] * strip[d]
        return out

    def corner_table(self, trace, inner=None):
        table = jnp.zeros((self.depth, LANES), jnp.float32)
        ends = (0, LANES - 1)
        if inner is not None:
            arms = dot(stack(trace), self.plain[...])
        for rs in range(2):
            for cs in range(2):
                slot = TABLE * (2 * rs + cs)
                values = [(trace[rs], ends[cs])]
                if inner is not None:
                    values.append((inner[rs], ends[cs]))
                    for face, end in ((rs, ends[cs]), (2 + cs, ends[rs])):
                        part = arms[face * self.depth : (face + 1) * self.depth]
                        values.append((part[:, :LANES], end))
                        values.append((part[:, LANES:], end))
                for kind, (value, end) in enumerate(values):
                    shift = (slot + kind - end) % LANES
                    rolled = pltpu.roll(value, shift, 1) if shift else value
                    table = jnp.where(self.lane == slot + kind, rolled, table)
        return table

    def send(self, payload, groups, table, copies=1):
        depth = self.depth
        at = len(groups) * depth
        for f in range(4):
            to = self.partner(self.me, f) * copies
            for i, group in enumerate(groups):
                for s in range(copies):
                    payload[to + s, i * depth : (i + 1) * depth, :] = group[f]
        for to in range(self.patches * copies):
            payload[to, at : at + depth, :] = table

    def take(self, recv, patch, lo, hi):
        copies = recv.shape[0] // self.patches
        out = recv[patch * copies, lo:hi, :]
        for s in range(1, copies):
            out = out + recv[patch * copies + s, lo:hi, :]
        return out

    def received(self, recv, count, at=0):
        depth = self.depth
        rows = count * depth
        raw = [self.take(recv, self.partner(self.me, f), at, at + rows) for f in range(4)]
        turned = dot(stack(raw), self.reverse[...])
        out = []
        for f in range(4):
            flipped = self.flip(self.me, f) == 1
            out.append(jnp.where(flipped, turned[f * rows : (f + 1) * rows], raw[f]))
        return [[out[f][i * depth : (i + 1) * depth] for f in range(4)] for i in range(count)]

    def corner(self, face, side):
        q, f1 = self.partner(self.me, face), self.face_id(self.me, face)
        eq = side ^ self.flip(self.me, face)
        s1 = f1 & 1
        upright = f1 < 2
        f2 = jnp.where(upright, 2 + eq, eq)
        kq = jnp.where(upright, 2 * s1 + eq, 2 * eq + s1)
        tq = jnp.where(upright, 4, 2)
        r, g = self.partner(q, f2), self.face_id(q, f2)
        s2 = s1 ^ self.flip(q, f2)
        flat = g < 2
        k = jnp.where(flat, 2 * (g & 1) + s2, 2 * s2 + (g & 1))
        t = jnp.where(flat, 2, 4)
        g2 = jnp.where(flat, 2 + s2, s2)
        r2, h = self.partner(r, g2), self.face_id(r, g2)
        s4 = (g & 1) ^ self.flip(r, g2)
        k2 = jnp.where(h < 2, 2 * (h & 1) + s4, 2 * s4 + (h & 1))
        return (q, kq, tq), (r, k, t), (r2, k2)

    def corners(self):
        return [[self.corner(f, s) for s in range(2)] for f in range(4)]

    def look(self, recv, at, patch, lane, side):
        shift = (side * (LANES - 1) + LANES - lane) & (LANES - 1)
        return pltpu.roll(self.take(recv, patch, at, at + self.depth), shift, 1)

    def ends(self, low, high):
        return jnp.where(self.first, low, jnp.where(self.last, high, 0.0))

    def other_stiff(self, recv, at, mine, theirs, inner, corners):
        out = []
        edge = self.first | self.last
        for f in range(4):
            across = []
            for s in range(2):
                r, k, t = corners[f][s][1]
                across.append(self.look(recv, at, r, TABLE * k, s))
            value = inner[f] + PENALTY * (theirs[f] - mine[f])
            far = PENALTY * (theirs[f] - self.ends(*across))
            out.append(value + jnp.where(edge, far, 0.0))
        return out


def stack(values):
    return jnp.concatenate(values, 0)


def unstack(value, depth):
    return [value[f * depth : (f + 1) * depth] for f in range(4)]


def cubic(x, s):
    return x * x * x - x + GRADIENT_ENERGY * s


def start_kernel(sizes, own, payload, *refs):
    body = Body(sizes, refs)
    rows = own.shape[0]
    layer = lax.broadcasted_iota(jnp.int32, (body.depth, LANES), 0)
    low = lax.axis_index("sec") * rows
    here = (layer >= low) & (layer < low + rows)

    def place(value):
        return jnp.where(here, stack([value] * body.slabs), 0.0)

    strips = body.strips(own)
    trace = [place(s[0]) for s in strips]
    inner = body.slab(
        [place(body.depth_sum(s, STIFF_BAND)) for s in strips],
        [place(body.depth_sum(s, MASS_BAND)) for s in strips],
    )
    body.send(payload, [trace, inner], body.corner_table(trace), body.slabs)


def flux_tail(body, current, mine, other, r0, v1, m1, tr, tv, payload, potential):
    jump = body.jumps(mine, other)
    body.stand(jump)

    def residual(z, stiff, mass):
        r0[z] = -TIME_STEP * (stiff + body.column(z))

    body.stiff0(lambda z: potential[z], residual)
    body.add_rows(r0, jump, -TIME_STEP)

    def image(z, stiff, mass):
        v1[z] = stiff
        m1[z] = mass

    body.stiff0(lambda z: r0[z], image)
    trace, inner = body.traces(r0), body.traces(v1)
    tr[...], tv[...] = stack(trace), stack(inner)
    body.send(payload, [trace, inner], body.corner_table(trace))


def first_kernel(sizes, recv, *refs):
    slabs, refs = refs[: sizes[2]], refs[sizes[2] :]
    c, sc, r0, v1, m1, tc, tr, tv, sides, payload, potential = refs[:11]
    body = Body(sizes, refs[11:])
    depth, count = body.depth, body.slabs
    rows = depth // count
    sec = lax.axis_index("sec")
    for k, slab in enumerate(slabs):
        c[pl.ds(lax.rem(sec + k, count) * rows, rows)] = slab[...]
    other, inner = body.received(recv, 2)
    mine = body.traces(c)
    jump = body.jumps(mine, other)
    body.stand(jump)

    def curve(z, stiff, mass):
        sc[z] = stiff + body.column(z)

    body.stiff0(lambda z: c[z], curve)
    body.add_rows(sc, jump, 1.0)
    for z in range(depth):
        potential[z] = cubic(c[z], sc[z])
    mine_s = body.traces(sc)
    other_s = body.other_stiff(recv, 2 * depth, mine, other, inner, body.corners())
    tc[0], tc[1] = stack(mine), stack(mine_s)
    sides[0], sides[1] = stack(other), stack(other_s)
    mine_p = [cubic(x, s) for x, s in zip(mine, mine_s)]
    other_p = [cubic(x, s) for x, s in zip(other, other_s)]
    flux_tail(body, c, mine_p, other_p, r0, v1, m1, tr, tv, payload, potential)


def second_kernel(sizes, r0, v1, m1, tr, tv, recv, u1, y, v2, m2, ty, tv2, tu, sides, payload,
                  *refs):
    body = Body(sizes, refs)
    depth = body.depth
    other, inner = body.received(recv, 2)
    mine = unstack(tr, depth)
    jump = body.jumps(mine, other)
    body.stand(jump)
    for z in range(depth):
        u1[z] = v1[z] + body.column(z)
    body.add_rows(u1, jump, 1.0)
    mine_s = body.stiff_trace(unstack(tv, depth), jump)
    other_s = body.other_stiff(recv, 2 * depth, mine, other, inner, body.corners())
    tu[...] = stack(mine_s)
    sides[0], sides[1] = stack(other), stack(other_s)
    jump = body.jumps(mine_s, other_s)
    body.stand(jump)

    def image(z, stiff, mass):
        y[z] = m1[z] + TWICE * u1[z] + HALF * (stiff + body.column(z))

    body.stiff0(lambda z: u1[z], image)
    body.add_rows(y, jump, HALF)
    sums = [[], [], []]

    def again(z, stiff, mass):
        v2[z] = stiff
        m2[z] = mass
        a, b = r0[z], y[z]
        for i, product in enumerate((a * a, a * b, b * b)):
            sums[i].append(jnp.sum(product, axis=0, keepdims=True))

    body.stiff0(lambda z: y[z], again)
    strips_y, strips = body.strips(y), body.strips(v2)
    trace, inner = [s[0] for s in strips_y], [s[0] for s in strips]
    ty[...], tv2[...] = stack(trace), stack(inner)
    mixed = body.slab(
        [HALF * body.depth_sum(s, STIFF_BAND) for s in strips],
        [HALF * body.depth_sum(s, MASS_BAND) for s in strips],
        [body.depth_sum(s, MASS_BAND) for s in strips_y],
    )
    outer = [TWICE * a + b for a, b in zip(inner, mixed)]
    table = body.corner_table(trace, inner)
    for i in range(3):
        total = jnp.sum(stack(sums[i]), axis=1, keepdims=True)
        table = jnp.where(body.lane == SUMS + i, total, table)
    body.send(payload, [trace, inner, outer], table)


def third_kernel(sizes, last, r0, y, v2, m2, ty, tv2, recv, *refs):
    if last:
        t, base, payload, u2, zf, mt = refs[:6]
        body = Body(sizes, refs[6:])
    else:
        t, base, u2, zf, tt, tu2, tz, sides, payload, mt = refs[:10]
        body = Body(sizes, refs[10:])
    depth, patches = body.depth, body.patches
    at = 3 * depth
    known = recv[0, at : at + depth, :]
    for p in range(1, patches):
        known = known + recv[p, at : at + depth, :]
    known = jnp.sum(known, axis=0, keepdims=True)
    m0, m1, m2s = [known[:, SUMS + i : SUMS + i + 1] for i in range(3)]
    a0 = m0 / m1
    other, inner, outer = body.received(recv, 3)
    corners = body.corners()
    mine = unstack(ty, depth)
    jump = body.jumps(mine, other)
    body.stand(jump)
    for z in range(depth):
        u2[z] = v2[z] + body.column(z)
    body.add_rows(u2, jump, 1.0)
    mine_s = body.stiff_trace(unstack(tv2, depth), jump)
    other_s = body.other_stiff(recv, at, mine, other, inner, corners)
    masses, stiffs, far = [], [], []
    for f in range(4):
        arm_m, arm_k, across = [], [], []
        for s in range(2):
            (q, kq, tq), (r, k, kind), (r2, k2) = corners[f][s]
            look = functools.partial(body.look, recv, at, side=s)
            arm_m.append(look(q, TABLE * kq + tq) - look(r, TABLE * k + kind))
            arm_k.append(look(q, TABLE * kq + tq + 1) - look(r, TABLE * k + kind + 1))
            value = look(r, TABLE * k)
            across.append(
                look(r, TABLE * k + 1)
                + PENALTY * (value - other[f])
                + PENALTY * (value - look(r2, TABLE * k2))
            )
        theirs = PENALTY * (other[f] - mine[f])
        masses.append(MASS_BAND[0] * theirs + PENALTY * body.ends(*arm_m))
        stiffs.append(STIFF_BAND[0] * theirs + PENALTY * body.ends(*arm_k))
        far.append(body.ends(*across))
    pushed = body.slab(stiffs, masses)
    edge = body.first | body.last
    other_t = []
    for f in range(4):
        again = pushed[f] + PENALTY * (other_s[f] - mine_s[f])
        again = again + jnp.where(edge, PENALTY * (other_s[f] - far[f]), 0.0)
        image = outer[f] + TWICE * (other_s[f] - inner[f]) + HALF * again
        other_t.append(other[f] - a0 * image)
    jump = body.jumps(mine_s, other_s)
    body.stand(jump)

    def turn(z, stiff, mass):
        t[z] = y[z] - a0 * (m2[z] + TWICE * u2[z] + HALF * (stiff + body.column(z)))

    body.stiff0(lambda z: u2[z], turn)
    body.add_rows(t, jump, -HALF * a0)
    mine_t = body.traces(t)
    jump = body.jumps(mine_t, other_t)
    body.stand(jump)

    def image(z, stiff, mass):
        zf[z] = stiff + body.column(z)
        mt[z] = mass

    body.stiff0(lambda z: t[z], image)
    body.add_rows(zf, jump, 1.0)
    sums = [jnp.zeros((8, LANES), jnp.float32)] * 6
    for z in range(depth):
        b, x, s = y[z], t[z], zf[z]
        a = r0[z] - a0 * b
        energy = x * (mt[z] + TWICE * s) + HALF * (s * s)
        for i, product in enumerate((a * a, a * x, a * b, x * x, x * b, energy)):
            sums[i] = sums[i] + jnp.sum(product.reshape(LANES // 8, 8, LANES), axis=0)
    moments = jnp.zeros((1, LANES), jnp.float32)
    lane = lax.broadcasted_iota(jnp.int32, (1, LANES), 1)
    for i, value in enumerate(sums):
        value = jnp.sum(jnp.sum(value, axis=0, keepdims=True), axis=1, keepdims=True)
        moments = jnp.where(lane == i, value, moments)
    for i, value in enumerate((a0, m0, m1, m2s)):
        base[i : i + 1, :] = jnp.broadcast_to(value, (1, LANES))
    for to in range(patches):
        payload[to, :1, :] = moments
    if not last:
        trace = body.traces(zf)
        tt[...], tu2[...], tz[...] = stack(mine_t), stack(mine_s), stack(trace)
        sides[0], sides[1], sides[2] = stack(other), stack(other_s), stack(other_t)
        for f in range(4):
            payload[body.partner(body.me, f), 8 : 8 + depth, :] = trace[f]


def weights(patches, base, recv):
    total = recv[0, :1, :]
    for p in range(1, patches):
        total = total + recv[p, :1, :]
    a0, m0, m1, m2 = [base[i : i + 1, :1] for i in range(4)]
    rr1, g1, g2, tt, ty, tat = [total[:, i : i + 1] for i in range(6)]
    b0 = rr1 / m0
    a1 = rr1 / (g1 + 2.0 * b0 * g2 + b0 * b0 * m1)
    rr2 = rr1 - 2.0 * a1 * (g1 + b0 * g2) + a1 * a1 * (tt + 2.0 * b0 * ty + b0 * b0 * m2)
    b1 = rr2 / rr1
    shift = a1 * b0 / a0
    c1, c0, c2 = 1.0 + b1 + shift, b1 * b0 - shift, -a1
    a2 = rr2 / (
        c1 * c1 * g1
        + c0 * c0 * m1
        + c2 * c2 * tat
        + 2.0 * (c1 * c0 * g2 + c1 * c2 * tt + c0 * c2 * ty)
    )
    return a0 + a1 * (1.0 + b0) + a2 * (c1 + c0), -a0 * (a1 + a2 * c1), a2 * c2


def next_kernel(sizes, c, r0, y, t, sc, u1, u2, zf, tc, tr, tu, ty, tu2, tt, tz,
                side_c, side_r, side_y, base, recv,
                cn, rn, v1, m1, trn, tvn, payload, potential, *refs):
    body = Body(sizes, refs)
    depth = body.depth
    x = weights(body.patches, base, recv)

    def mix(*values):
        return values[0] + x[0] * values[1] + x[1] * values[2] + x[2] * values[3]

    for z in range(depth):
        cn[z] = mix(c[z], r0[z], y[z], t[z])
        potential[z] = cubic(cn[z], mix(sc[z], u1[z], u2[z], zf[z]))
    (side_z,) = body.received(recv, 1, 8)
    mine = cubic(
        mix(tc[0], tr[...], ty[...], tt[...]), mix(tc[1], tu[...], tu2[...], tz[...])
    )
    other = cubic(
        mix(side_c[0], side_r[0], side_y[0], side_y[2]),
        mix(side_c[1], side_r[1], side_y[1], stack(side_z)),
    )
    flux_tail(body, cn, unstack(mine, depth), unstack(other, depth),
              rn, v1, m1, trn, tvn, payload, potential)


def last_kernel(patches, c, r0, y, t, base, recv, out):
    x0, x1, x2 = weights(patches, base, recv)
    rows = out.shape[0]
    low = lax.axis_index("sec") * rows
    for z in range(rows):
        k = low + z
        out[z] = c[k] + x0 * r0[k] + x1 * y[k] + x2 * t[k]


def shards(patches, slabs, concentration, partner, face_id, flip):
    own = concentration[0]
    rows = own.shape[0]
    depth = rows * slabs
    halves = [own]
    for k in range(1, slabs):
        halves.append(lax.ppermute(own, "sec", [((i + k) % slabs, i) for i in range(slabs)]))
    consts = [jnp.asarray(x) for x in constants(depth)]
    tables = [partner, face_id, flip]
    vmem, smem = pl.BlockSpec(memory_space=pltpu.VMEM), pl.BlockSpec(memory_space=pltpu.SMEM)
    params = pltpu.CompilerParams(vmem_limit_bytes=48 << 20)

    def shape(*dims):
        return jax.ShapeDtypeStruct(dims, jnp.float32)

    field, trace, base = shape(depth, LANES, LANES), shape(4 * depth, LANES), shape(8, LANES)

    def sides(count):
        return shape(count, 4 * depth, LANES)

    def load(count):
        return shape(patches, count, LANES)

    def call(kernel, outs, *args, fields=0):
        count = len(args)
        inside = [pltpu.VMEM((depth, LANES, LANES), jnp.float32)] * fields
        shared = [
            pltpu.VMEM((4, LANES + 2 * PAD, LANES), jnp.float32),
            pltpu.VMEM((LANES, LANES), jnp.float32),
            pltpu.VMEM((LANES, LANES), jnp.float32),
            pltpu.VMEM((-(-depth // 8), LANES, LANES), jnp.float32),
        ]

        def run(*refs):
            common, rest = refs[:8], refs[8:]
            cut = len(rest) - len(shared)
            kernel((depth, patches, slabs), *rest[:cut], *common, *rest[cut:])

        return pl.pallas_call(
            run,
            out_shape=outs,
            in_specs=[smem] * 3 + [vmem] * (len(consts) + count),
            out_specs=[vmem] * len(outs),
            scratch_shapes=inside + shared,
            compiler_params=params,
            name=kernel.__name__ if hasattr(kernel, "__name__") else "third_kernel",
        )(*tables, *consts, *args)

    def swap(payload, axes="patch"):
        return lax.all_to_all(payload, axes, 0, 0)

    (payload,) = call(start_kernel, [shape(patches * slabs, 3 * depth, LANES)], own)
    c, sc, r0, v1, m1, tc, tr, tv, side_c, payload = call(
        first_kernel,
        [field] * 5 + [sides(2), trace, trace, sides(2), load(3 * depth)],
        swap(payload, ("patch", "sec")), *halves,
        fields=1,
    )
    for step in range(STEPS):
        u1, y, v2, m2, ty, tv2, tu, side_r, payload = call(
            second_kernel,
            [field] * 4 + [trace] * 3 + [sides(2), load(4 * depth)],
            r0, v1, m1, tr, tv, swap(payload),
        )
        last = step + 1 == STEPS
        outs = [field, base]
        if last:
            outs += [load(1)]
        else:
            outs += [field] * 2 + [trace] * 3 + [sides(3), load(8 + depth)]
        t, base_now, *rest = call(
            lambda sizes, *refs, last=last: third_kernel(sizes, last, *refs),
            outs,
            r0, y, v2, m2, ty, tv2, swap(payload),
            fields=3 if last else 1,
        )
        if last:
            (payload,) = rest
            break
        u2, zf, tt, tu2, tz, side_y, payload = rest
        c, r0, v1, m1, tr, tv, payload = call(
            next_kernel,
            [field] * 4 + [trace] * 2 + [load(3 * depth)],
            c, r0, y, t, sc, u1, u2, zf, tc, tr, tu, ty, tu2, tt, tz,
            side_c, side_r, side_y, base_now, swap(payload),
            fields=1,
        )
    out = pl.pallas_call(
        functools.partial(last_kernel, patches),
        out_shape=shape(rows, LANES, LANES),
        in_specs=[vmem] * 6,
        out_specs=vmem,
        compiler_params=params,
    )(c, r0, y, t, base_now, swap(payload))
    return out[None]


def solution(mesh):
    placed = (P("patch", "sec", None, None), P(), P(), P())
    return jax.shard_map(
        functools.partial(shards, mesh.shape["patch"], mesh.shape["sec"]),
        mesh=mesh,
        in_specs=placed,
        out_specs=P("patch", "sec", None, None),
        check_vma=False,
    )
```

```python
import functools

import jax
import jax.numpy as jnp
import numpy as np
from jax import lax
from jax.experimental import pallas as pl
from jax.experimental.pallas import tpu as pltpu
from jax.sharding import PartitionSpec as P

STEPS = 2
MASS_BAND = (2416.0 / 5040.0, 1191.0 / 5040.0, 120.0 / 5040.0, 1.0 / 5040.0)
STIFF_BAND = (2.0 / 3.0, -0.125, -0.2, -1.0 / 120.0)
SCALE = 5040.0
MASS_HIGH, MASS_LOW = (2416.0, 1192.0, 120.0, 1.0), (0.0, -1.0, 0.0, 0.0)
STIFF_HIGH, STIFF_LOW = (3360.0, -632.0, -1008.0, -42.0), (0.0, 2.0, 0.0, 0.0)
PENALTY = 2.0
TIME_STEP = 1.0
STABILIZER = 2.0
GRADIENT_ENERGY = 0.5
HALF = TIME_STEP * GRADIENT_ENERGY
TWICE = TIME_STEP * STABILIZER
EXACT = lax.Precision.HIGHEST
LANES = 128
PAD = 8
KINDS = 6
SUMS = 4 * KINDS
NARROW, BROAD = 16, 32
COST = 1 << 34


def band_matrix(band, size):
    out = np.zeros((size, size), np.float32)
    for offset, value in enumerate(band):
        for row in range(size - offset):
            out[row, row + offset] = value
            out[row + offset, row] = value
    return out


def dot(left, right):
    return jnp.dot(left, right, precision=EXACT, preferred_element_type=jnp.float32)


def right_matrix(mass_band, stiff_band):
    mass, stiff = band_matrix(mass_band, LANES), band_matrix(stiff_band, LANES)
    return np.block([[mass, stiff], [np.zeros_like(mass), mass]])


def constants():
    high = right_matrix(MASS_HIGH, STIFF_HIGH).astype(jnp.bfloat16)
    low = right_matrix(MASS_LOW, STIFF_LOW).astype(jnp.bfloat16)
    return high, low


def banded(distance, band, inside=None):
    out = jnp.zeros(distance.shape, jnp.float32)
    for offset, value in enumerate(band):
        hit = distance == offset
        out = jnp.where(hit if inside is None else hit & inside, value, out)
    return out


class Body:
    def __init__(self, sizes, refs, copies=1):
        self.depth, self.patches, self.slabs = sizes
        self.copies = copies
        self.tables, refs = refs[:3], refs[3:]
        self.near, self.strip, self.turned, self.stood = refs[-4:]
        if len(refs) > 4:
            self.high, self.low = refs[:2]
        self.me = lax.axis_index("patch")
        self.lane = lax.broadcasted_iota(jnp.int32, (self.depth, LANES), 1)
        self.first, self.last = self.lane == 0, self.lane == LANES - 1
        self.wide = lax.broadcasted_iota(jnp.int32, (LANES, LANES), 1)
        self.edge = (self.wide == 0) | (self.wide == LANES - 1)
        row = lax.broadcasted_iota(jnp.int32, (LANES, LANES), 0)
        self.reverse = jnp.where(row + self.wide == LANES - 1, 1.0, 0.0)
        distance = jnp.abs(row - self.wide)
        self.plain = jnp.concatenate(
            [banded(distance, MASS_BAND), banded(distance, STIFF_BAND)], axis=1
        )
        n = 4 * self.depth
        row = lax.broadcasted_iota(jnp.int32, (n, 2 * n), 0)
        column = lax.broadcasted_iota(jnp.int32, (n, 2 * n), 1)
        left = column < n
        column = jnp.where(left, column, column - n)
        inside = row < 0
        for low in range(0, n, self.depth):
            top = low + self.depth
            inside = inside | ((row >= low) & (row < top) & (column >= low) & (column < top))
        distance = jnp.abs(row - column)
        self.third = banded(distance, MASS_BAND, inside & left) + banded(
            distance, STIFF_BAND, inside & ~left
        )

    def partner(self, patch, face):
        return self.tables[0][face, patch]

    def face_id(self, patch, face):
        return self.tables[1][face, patch]

    def flip(self, patch, face):
        return self.tables[2][face, patch]

    def split(self, value):
        pieces = []
        for last in (False, False, True):
            piece = value.astype(jnp.bfloat16)
            pieces.append(piece)
            if not last:
                value = value - piece.astype(jnp.float32)
        return pieces

    def stiff0(self, layer, finish):
        depth = self.depth
        zeros = jnp.zeros((PAD, LANES), jnp.float32)
        for i in range(4):
            self.near[i, :PAD] = zeros
            self.near[i, PAD + LANES :] = zeros
        for z in range(depth):
            middle = layer(z)
            massed = (MASS_BAND[0] / SCALE) * middle
            stiffed = (STIFF_BAND[0] / SCALE) * middle
            for offset in (1, 2, 3):
                near = [layer(k) for k in (z - offset, z + offset) if 0 <= k < depth]
                if near:
                    both = near[0] if len(near) == 1 else near[0] + near[1]
                    massed = massed + (MASS_BAND[offset] / SCALE) * both
                    stiffed = stiffed + (STIFF_BAND[offset] / SCALE) * both
            pieces = self.split(jnp.concatenate([massed, stiffed], axis=1))
            mixed = None
            for matrix, parts in ((self.high, pieces), (self.low, pieces[:2])):
                for piece in parts:
                    term = jnp.dot(piece, matrix[...], preferred_element_type=jnp.float32)
                    mixed = term if mixed is None else mixed + term
            a, b = 2 * (z % 2), 2 * (z % 2) + 1
            self.near[a, PAD : PAD + LANES] = mixed[:, :LANES]
            self.near[b, PAD : PAD + LANES] = mixed[:, LANES:]
            stiff = STIFF_BAND[0] * mixed[:, :LANES] + MASS_BAND[0] * mixed[:, LANES:]
            mass = MASS_BAND[0] * mixed[:, :LANES]
            for o in (1, 2, 3):
                low, high = slice(PAD - o, PAD - o + LANES), slice(PAD + o, PAD + o + LANES)
                both = self.near[a, low] + self.near[a, high]
                stiff = stiff + STIFF_BAND[o] * both
                stiff = stiff + MASS_BAND[o] * (self.near[b, low] + self.near[b, high])
                mass = mass + MASS_BAND[o] * both
            finish(z, stiff, mass)

    def strips(self, field, count=4):
        depth = field.shape[0]
        group = min(depth, 8)
        rows0 = [field[:, d, :] for d in range(count)]
        rows1 = [field[:, LANES - 1 - d, :] for d in range(count)]
        wanted = list(range(4 - count, 4 + count))
        pieces = {i: [] for i in wanted}
        for start in range(0, depth, group):
            stacked = jnp.zeros((LANES, LANES), jnp.float32)
            for j in range(group):
                rolled = pltpu.roll(field[start + j], (8 * j + 4) % LANES, 1)
                stacked = jnp.where((self.wide >> 3) == j, rolled, stacked)
            self.strip[...] = jnp.transpose(stacked)
            for i in wanted:
                pieces[i].append(self.strip[pl.ds(i, group, stride=8), :])
        columns = {i: jnp.concatenate(p, axis=0) if len(p) > 1 else p[0] for i, p in pieces.items()}
        return [
            rows0,
            rows1,
            [columns[4 + d] for d in range(count)],
            [columns[3 - d] for d in range(count)],
        ]

    def traces(self, field):
        return [strip[0] for strip in self.strips(field, 1)]

    def jumps(self, mine, other):
        return [PENALTY * (a - b) for a, b in zip(mine, other)]

    def stand(self, jump):
        for start in range(0, self.depth, 8):
            self.turned[pl.ds(0, 8, stride=2), :] = jump[3][start : start + 8]
            self.turned[pl.ds(1, 8, stride=2), :] = jump[2][start : start + 8]
            self.stood[start // 8] = jnp.transpose(self.turned[...])

    def column(self, z):
        rolled = pltpu.roll(self.stood[z // 8], (LANES - 2 * (z % 8) - 1) % LANES, 1)
        return jnp.where(self.edge, rolled, 0.0)

    def add_rows(self, field, jump, factor):
        field[:, 0, :] = field[:, 0, :] + factor * jump[0]
        field[:, LANES - 1, :] = field[:, LANES - 1, :] + factor * jump[1]

    def stiff_trace(self, inner, jump):
        out = []
        for f in range(4):
            side = f & 1
            low, high = (2, 3) if f < 2 else (0, 1)
            at = side * (LANES - 1)
            ends = []
            for face, end in ((low, 0), (high, LANES - 1)):
                shift = (end - at) % LANES
                ends.append(pltpu.roll(jump[face], shift, 1) if shift else jump[face])
            out.append(inner[f] + jump[f] + self.ends(*ends))
        return out

    def slab(self, stiffs, masses, plain=None):
        n = 4 * self.depth
        rows = [stack(masses), stack(stiffs)] + ([] if plain is None else [stack(plain)])
        both = dot(stack(rows), self.plain)
        lower = both[n : 2 * n, :LANES] + both[:n, LANES:]
        if plain is not None:
            lower = lower + both[2 * n :, :LANES]
        out = dot(self.third, stack([lower, both[:n, :LANES]]))
        return unstack(out, self.depth)

    def depth_sum(self, strip, band):
        out = band[0] * strip[0]
        for d in (1, 2, 3):
            out = out + band[d] * strip[d]
        return out

    def corner_table(self, trace, inner=None):
        table = jnp.zeros((self.depth, LANES), jnp.float32)
        ends = (0, LANES - 1)
        kinds = 1 if inner is None else KINDS
        if inner is not None:
            arms = dot(stack(trace), self.plain)
        for rs in range(2):
            for cs in range(2):
                slot = kinds * (2 * rs + cs)
                values = [(trace[rs], ends[cs])]
                if inner is not None:
                    values.append((inner[rs], ends[cs]))
                    for face, end in ((rs, ends[cs]), (2 + cs, ends[rs])):
                        part = arms[face * self.depth : (face + 1) * self.depth]
                        values.append((part[:, :LANES], end))
                        values.append((part[:, LANES:], end))
                for kind, (value, end) in enumerate(values):
                    shift = (slot + kind - end) % LANES
                    rolled = pltpu.roll(value, shift, 1) if shift else value
                    table = jnp.where(self.lane == slot + kind, rolled, table)
        return table

    def pack(self, table, width):
        count = width // NARROW
        rows = []
        for start in range(0, self.depth, 8):
            for low in range(count):
                total = None
                for i in range(low, 8, count):
                    layer = table[start + i : start + i + 1]
                    part = pltpu.roll(layer, LANES - NARROW * i, 1) if i else layer
                    total = part if total is None else total + part
                rows.append(total)
        return stack(rows) if len(rows) > 1 else rows[0]

    def send(self, payload, groups, packed):
        depth, copies = self.depth, self.copies
        rows = payload.shape[0] // (self.patches * copies)
        at = len(groups) * depth
        for f in range(4):
            to = self.partner(self.me, f) * copies
            for i, group in enumerate(groups):
                for s in range(copies):
                    payload[pl.ds((to + s) * rows + i * depth, depth), :] = group[f]
        for to in range(self.patches * copies):
            payload[to * rows + at : (to + 1) * rows, :] = packed

    def take(self, recv, patch, lo, count):
        rows = recv.shape[0] // (self.patches * self.copies)
        out = None
        for s in range(self.copies):
            part = recv[pl.ds((patch * self.copies + s) * rows + lo, count), :]
            out = part if out is None else out + part
        return out

    def received(self, recv, count, at=0):
        depth = self.depth
        rows = count * depth
        raw = [self.take(recv, self.partner(self.me, f), at, rows) for f in range(4)]
        turned = dot(stack(raw), self.reverse)
        out = []
        for f in range(4):
            flipped = self.flip(self.me, f) == 1
            out.append(jnp.where(flipped, turned[f * rows : (f + 1) * rows], raw[f]))
        return [[out[f][i * depth : (i + 1) * depth] for f in range(4)] for i in range(count)]

    def corner(self, face, side):
        q, f1 = self.partner(self.me, face), self.face_id(self.me, face)
        eq = side ^ self.flip(self.me, face)
        s1 = f1 & 1
        upright = f1 < 2
        f2 = jnp.where(upright, 2 + eq, eq)
        kq = jnp.where(upright, 2 * s1 + eq, 2 * eq + s1)
        tq = jnp.where(upright, 4, 2)
        r, g = self.partner(q, f2), self.face_id(q, f2)
        s2 = s1 ^ self.flip(q, f2)
        flat = g < 2
        k = jnp.where(flat, 2 * (g & 1) + s2, 2 * s2 + (g & 1))
        t = jnp.where(flat, 2, 4)
        g2 = jnp.where(flat, 2 + s2, s2)
        r2, h = self.partner(r, g2), self.face_id(r, g2)
        s4 = (g & 1) ^ self.flip(r, g2)
        k2 = jnp.where(h < 2, 2 * (h & 1) + s4, 2 * s4 + (h & 1))
        return (q, kq, tq), (r, k, t), (r2, k2)

    def corners(self):
        return [[self.corner(f, s) for s in range(2)] for f in range(4)]

    def look(self, recv, at, patch, lane, side, width):
        count = width // NARROW
        shift = (side * (LANES - 1) + LANES - lane) & (LANES - 1)
        packed = self.take(recv, patch, at, self.depth // 8 * count)
        odd = (lax.broadcasted_iota(jnp.int32, (8, LANES), 0) & 1) == 1
        out = []
        for k in range(0, self.depth // 8 * count, count):
            spread = jnp.broadcast_to(packed[k : k + 1], (8, LANES))
            if count == 2:
                spread = jnp.where(odd, packed[k + 1 : k + 2], spread)
            out.append(pltpu.roll(spread, 0, 1, stride=NARROW, stride_axis=0))
        return pltpu.roll(stack(out) if len(out) > 1 else out[0], shift, 1)

    def ends(self, low, high):
        return jnp.where(self.first, low, jnp.where(self.last, high, 0.0))

    def other_stiff(self, recv, at, mine, theirs, inner, corners, kinds, width):
        out = []
        edge = self.first | self.last
        for f in range(4):
            across = []
            for s in range(2):
                r, k, t = corners[f][s][1]
                across.append(self.look(recv, at, r, kinds * k, s, width))
            value = inner[f] + PENALTY * (theirs[f] - mine[f])
            far = PENALTY * (theirs[f] - self.ends(*across))
            out.append(value + jnp.where(edge, far, 0.0))
        return out


def stack(values):
    return jnp.concatenate(values, 0)


def unstack(value, depth):
    return [value[f * depth : (f + 1) * depth] for f in range(4)]


def cubic(x, s):
    return x * x * x - x + GRADIENT_ENERGY * s


def start_kernel(sizes, own, payload, *refs):
    body = Body(sizes, refs, sizes[2])
    rows = own.shape[0]
    layer = lax.broadcasted_iota(jnp.int32, (body.depth, LANES), 0)
    low = lax.axis_index("sec") * rows
    here = (layer >= low) & (layer < low + rows)

    def place(value):
        return jnp.where(here, stack([value] * body.slabs), 0.0)

    strips = body.strips(own)
    trace = [place(s[0]) for s in strips]
    inner = body.slab(
        [place(body.depth_sum(s, STIFF_BAND)) for s in strips],
        [place(body.depth_sum(s, MASS_BAND)) for s in strips],
    )
    body.send(payload, [trace, inner], body.pack(body.corner_table(trace), NARROW))


def flux_tail(body, current, mine, other, r0, v1, m1, tr, tv, payload, potential):
    jump = body.jumps(mine, other)
    body.stand(jump)

    def residual(z, stiff, mass):
        r0[z] = -TIME_STEP * (stiff + body.column(z))

    body.stiff0(lambda z: potential[z], residual)
    body.add_rows(r0, jump, -TIME_STEP)

    def image(z, stiff, mass):
        v1[z] = stiff
        m1[z] = mass

    body.stiff0(lambda z: r0[z], image)
    trace, inner = body.traces(r0), body.traces(v1)
    tr[...], tv[...] = stack(trace), stack(inner)
    body.copies = 1
    body.send(payload, [trace, inner], body.pack(body.corner_table(trace), NARROW))


def first_kernel(sizes, recv, *refs):
    slabs, refs = refs[: sizes[2]], refs[sizes[2] :]
    c, sc, r0, v1, m1, tc, tr, tv, sides, payload, potential = refs[:11]
    body = Body(sizes, refs[11:], sizes[2])
    depth, count = body.depth, body.slabs
    rows = depth // count
    sec = lax.axis_index("sec")
    for k, slab in enumerate(slabs):
        c[pl.ds(lax.rem(sec + k, count) * rows, rows)] = slab[...]
    other, inner = body.received(recv, 2)
    mine = body.traces(c)
    jump = body.jumps(mine, other)
    body.stand(jump)

    def curve(z, stiff, mass):
        sc[z] = stiff + body.column(z)

    body.stiff0(lambda z: c[z], curve)
    body.add_rows(sc, jump, 1.0)
    for z in range(depth):
        potential[z] = cubic(c[z], sc[z])
    mine_s = body.traces(sc)
    other_s = body.other_stiff(
        recv, 2 * depth, mine, other, inner, body.corners(), 1, NARROW
    )
    tc[0], tc[1] = stack(mine), stack(mine_s)
    sides[0], sides[1] = stack(other), stack(other_s)
    mine_p = [cubic(x, s) for x, s in zip(mine, mine_s)]
    other_p = [cubic(x, s) for x, s in zip(other, other_s)]
    flux_tail(body, c, mine_p, other_p, r0, v1, m1, tr, tv, payload, potential)


def second_kernel(sizes, r0, v1, m1, tr, tv, recv, u1, y, v2, m2, ty, tv2, tu, sides, payload,
                  *refs):
    body = Body(sizes, refs)
    depth = body.depth
    other, inner = body.received(recv, 2)
    mine = unstack(tr, depth)
    jump = body.jumps(mine, other)
    body.stand(jump)
    for z in range(depth):
        u1[z] = v1[z] + body.column(z)
    body.add_rows(u1, jump, 1.0)
    mine_s = body.stiff_trace(unstack(tv, depth), jump)
    other_s = body.other_stiff(
        recv, 2 * depth, mine, other, inner, body.corners(), 1, NARROW
    )
    tu[...] = stack(mine_s)
    sides[0], sides[1] = stack(other), stack(other_s)
    jump = body.jumps(mine_s, other_s)
    body.stand(jump)

    def image(z, stiff, mass):
        y[z] = m1[z] + TWICE * u1[z] + HALF * (stiff + body.column(z))

    body.stiff0(lambda z: u1[z], image)
    body.add_rows(y, jump, HALF)
    sums = [[], [], []]

    def again(z, stiff, mass):
        v2[z] = stiff
        m2[z] = mass
        a, b = r0[z], y[z]
        for i, product in enumerate((a * a, a * b, b * b)):
            sums[i].append(jnp.sum(product, axis=0, keepdims=True))

    body.stiff0(lambda z: y[z], again)
    strips_y, strips = body.strips(y), body.strips(v2)
    trace, inner = [s[0] for s in strips_y], [s[0] for s in strips]
    ty[...], tv2[...] = stack(trace), stack(inner)
    mixed = body.slab(
        [HALF * body.depth_sum(s, STIFF_BAND) for s in strips],
        [HALF * body.depth_sum(s, MASS_BAND) for s in strips],
        [body.depth_sum(s, MASS_BAND) for s in strips_y],
    )
    outer = [TWICE * a + b for a, b in zip(inner, mixed)]
    table = body.corner_table(trace, inner)
    for i in range(3):
        total = jnp.sum(stack(sums[i]), axis=1, keepdims=True)
        table = jnp.where(body.lane == SUMS + i, total, table)
    body.send(payload, [trace, inner, outer], body.pack(table, BROAD))


def third_kernel(sizes, last, r0, y, v2, m2, ty, tv2, recv, *refs):
    if last:
        t, base, payload, u2, zf, mt = refs[:6]
        body = Body(sizes, refs[6:])
    else:
        t, base, u2, zf, tt, tu2, tz, sides, payload, mt = refs[:10]
        body = Body(sizes, refs[10:])
    depth, patches = body.depth, body.patches
    at = 3 * depth
    packed = depth * BROAD // LANES
    known = recv[at : at + packed, :]
    for p in range(1, patches):
        known = known + recv[p * (at + packed) + at : (p + 1) * (at + packed), :]
    odd = lax.broadcasted_iota(jnp.int32, (packed, LANES), 0) & 1
    slot = lax.broadcasted_iota(jnp.int32, (packed, LANES), 1) + NARROW * odd
    slot = slot & (BROAD - 1)
    m0, m1, m2s = [
        jnp.sum(jnp.where(slot == SUMS + i, known, 0.0), keepdims=True) for i in range(3)
    ]
    a0 = m0 / m1
    other, inner, outer = body.received(recv, 3)
    corners = body.corners()
    mine = unstack(ty, depth)
    jump = body.jumps(mine, other)
    body.stand(jump)
    for z in range(depth):
        u2[z] = v2[z] + body.column(z)
    body.add_rows(u2, jump, 1.0)
    mine_s = body.stiff_trace(unstack(tv2, depth), jump)
    other_s = body.other_stiff(recv, at, mine, other, inner, corners, KINDS, BROAD)
    masses, stiffs, far = [], [], []
    for f in range(4):
        arm_m, arm_k, across = [], [], []
        for s in range(2):
            (q, kq, tq), (r, k, kind), (r2, k2) = corners[f][s]
            look = functools.partial(body.look, recv, at, side=s, width=BROAD)
            arm_m.append(look(q, KINDS * kq + tq) - look(r, KINDS * k + kind))
            arm_k.append(look(q, KINDS * kq + tq + 1) - look(r, KINDS * k + kind + 1))
            value = look(r, KINDS * k)
            across.append(
                look(r, KINDS * k + 1)
                + PENALTY * (value - other[f])
                + PENALTY * (value - look(r2, KINDS * k2))
            )
        theirs = PENALTY * (other[f] - mine[f])
        masses.append(MASS_BAND[0] * theirs + PENALTY * body.ends(*arm_m))
        stiffs.append(STIFF_BAND[0] * theirs + PENALTY * body.ends(*arm_k))
        far.append(body.ends(*across))
    pushed = body.slab(stiffs, masses)
    edge = body.first | body.last
    other_t = []
    for f in range(4):
        again = pushed[f] + PENALTY * (other_s[f] - mine_s[f])
        again = again + jnp.where(edge, PENALTY * (other_s[f] - far[f]), 0.0)
        image = outer[f] + TWICE * (other_s[f] - inner[f]) + HALF * again
        other_t.append(other[f] - a0 * image)
    jump = body.jumps(mine_s, other_s)
    body.stand(jump)

    def turn(z, stiff, mass):
        t[z] = y[z] - a0 * (m2[z] + TWICE * u2[z] + HALF * (stiff + body.column(z)))

    body.stiff0(lambda z: u2[z], turn)
    body.add_rows(t, jump, -HALF * a0)
    mine_t = body.traces(t)
    jump = body.jumps(mine_t, other_t)
    body.stand(jump)

    def image(z, stiff, mass):
        zf[z] = stiff + body.column(z)
        mt[z] = mass

    body.stiff0(lambda z: t[z], image)
    body.add_rows(zf, jump, 1.0)
    sums = [jnp.zeros((8, LANES), jnp.float32)] * 6
    for z in range(depth):
        b, x, s = y[z], t[z], zf[z]
        a = r0[z] - a0 * b
        energy = x * (mt[z] + TWICE * s) + HALF * (s * s)
        for i, product in enumerate((a * a, a * x, a * b, x * x, x * b, energy)):
            sums[i] = sums[i] + jnp.sum(product.reshape(LANES // 8, 8, LANES), axis=0)
    moments = jnp.zeros((1, LANES), jnp.float32)
    lane = lax.broadcasted_iota(jnp.int32, (1, LANES), 1)
    for i, value in enumerate(sums):
        value = jnp.sum(jnp.sum(value, axis=0, keepdims=True), axis=1, keepdims=True)
        moments = jnp.where(lane == i, value, moments)
    for i, value in enumerate((a0, m0, m1, m2s)):
        base[i : i + 1, :] = jnp.broadcast_to(value, (1, LANES))
    rows = payload.shape[0] // patches
    for to in range(patches):
        payload[to * rows : to * rows + 1, :] = moments
    if not last:
        trace = body.traces(zf)
        tt[...], tu2[...], tz[...] = stack(mine_t), stack(mine_s), stack(trace)
        sides[0], sides[1], sides[2] = stack(other), stack(other_s), stack(other_t)
        for f in range(4):
            payload[pl.ds(body.partner(body.me, f) * rows + 1, depth), :] = trace[f]


def weights(patches, base, recv):
    rows = recv.shape[0] // patches
    total = recv[:1, :]
    for p in range(1, patches):
        total = total + recv[p * rows : p * rows + 1, :]
    a0, m0, m1, m2 = [base[i : i + 1, :1] for i in range(4)]
    rr1, g1, g2, tt, ty, tat = [total[:, i : i + 1] for i in range(6)]
    b0 = rr1 / m0
    a1 = rr1 / (g1 + 2.0 * b0 * g2 + b0 * b0 * m1)
    rr2 = rr1 - 2.0 * a1 * (g1 + b0 * g2) + a1 * a1 * (tt + 2.0 * b0 * ty + b0 * b0 * m2)
    b1 = rr2 / rr1
    shift = a1 * b0 / a0
    c1, c0, c2 = 1.0 + b1 + shift, b1 * b0 - shift, -a1
    a2 = rr2 / (
        c1 * c1 * g1
        + c0 * c0 * m1
        + c2 * c2 * tat
        + 2.0 * (c1 * c0 * g2 + c1 * c2 * tt + c0 * c2 * ty)
    )
    return a0 + a1 * (1.0 + b0) + a2 * (c1 + c0), -a0 * (a1 + a2 * c1), a2 * c2


def next_kernel(sizes, c, r0, y, t, sc, u1, u2, zf, tc, tr, tu, ty, tu2, tt, tz,
                side_c, side_r, side_y, base, recv,
                cn, rn, v1, m1, trn, tvn, payload, potential, *refs):
    body = Body(sizes, refs)
    depth = body.depth
    x = weights(body.patches, base, recv)

    def mix(*values):
        return values[0] + x[0] * values[1] + x[1] * values[2] + x[2] * values[3]

    for z in range(depth):
        cn[z] = mix(c[z], r0[z], y[z], t[z])
        potential[z] = cubic(cn[z], mix(sc[z], u1[z], u2[z], zf[z]))
    (side_z,) = body.received(recv, 1, 1)
    mine = cubic(
        mix(tc[0], tr[...], ty[...], tt[...]), mix(tc[1], tu[...], tu2[...], tz[...])
    )
    other = cubic(
        mix(side_c[0], side_r[0], side_y[0], side_y[2]),
        mix(side_c[1], side_r[1], side_y[1], stack(side_z)),
    )
    flux_tail(body, cn, unstack(mine, depth), unstack(other, depth),
              rn, v1, m1, trn, tvn, payload, potential)


def last_kernel(patches, c, r0, y, t, base, recv, out):
    x0, x1, x2 = weights(patches, base, recv)
    rows = out.shape[0]
    low = lax.axis_index("sec") * rows
    for z in range(rows):
        k = low + z
        out[z] = c[k] + x0 * r0[k] + x1 * y[k] + x2 * t[k]


def shards(patches, slabs, concentration, partner, face_id, flip):
    own = concentration[0]
    rows = own.shape[0]
    depth = rows * slabs
    halves = [own]
    for k in range(1, slabs):
        halves.append(lax.ppermute(own, "sec", [((i + k) % slabs, i) for i in range(slabs)]))
    matrices = [jnp.asarray(x) for x in constants()]
    tables = [partner.T, face_id.T, flip.T]
    vmem, smem = pl.BlockSpec(memory_space=pltpu.VMEM), pl.BlockSpec(memory_space=pltpu.SMEM)
    params = pltpu.CompilerParams(vmem_limit_bytes=(4 + depth) << 20)

    def shape(*dims):
        return jax.ShapeDtypeStruct(dims, jnp.float32)

    field, trace, base = shape(depth, LANES, LANES), shape(4 * depth, LANES), shape(8, LANES)

    def sides(count):
        return shape(count, 4 * depth, LANES)

    def load(count):
        return shape(patches * count, LANES)

    def call(kernel, outs, *args, fields=0, consts=matrices, cost=None):
        count, head = len(args), 3 + len(consts)
        inside = [pltpu.VMEM((depth, LANES, LANES), jnp.float32)] * fields
        shared = [
            pltpu.VMEM((4, LANES + 2 * PAD, LANES), jnp.float32),
            pltpu.VMEM((LANES, LANES), jnp.float32),
            pltpu.VMEM((LANES, LANES), jnp.float32),
            pltpu.VMEM((-(-depth // 8), LANES, LANES), jnp.float32),
        ]

        def run(*refs):
            common, rest = refs[:head], refs[head:]
            cut = len(rest) - len(shared)
            kernel((depth, patches, slabs), *rest[:cut], *common, *rest[cut:])

        return pl.pallas_call(
            run,
            out_shape=outs,
            in_specs=[smem] * 3 + [vmem] * (len(consts) + count),
            out_specs=[vmem] * len(outs),
            scratch_shapes=inside + shared,
            compiler_params=params,
            cost_estimate=cost,
            name=kernel.__name__ if hasattr(kernel, "__name__") else "third_kernel",
        )(*tables, *consts, *args)

    def swap(payload, axes="patch", parts=patches):
        rows = payload.shape[0] // parts
        moved = lax.all_to_all(payload.reshape(parts, 1, rows * LANES), axes, 0, 0)
        return moved.reshape(parts * rows, LANES)

    narrow, broad = depth * NARROW // LANES, depth * BROAD // LANES
    (payload,) = call(
        start_kernel,
        [load(slabs * (2 * depth + narrow))],
        own,
        consts=[],
        cost=pl.CostEstimate(flops=COST, bytes_accessed=4 * own.size, transcendentals=0),
    )
    c, sc, r0, v1, m1, tc, tr, tv, side_c, payload = call(
        first_kernel,
        [field] * 5 + [sides(2), trace, trace, sides(2), load(2 * depth + narrow)],
        swap(payload, ("patch", "sec"), patches * slabs), *halves,
        fields=1,
    )
    for step in range(STEPS):
        u1, y, v2, m2, ty, tv2, tu, side_r, payload = call(
            second_kernel,
            [field] * 4 + [trace] * 3 + [sides(2), load(3 * depth + broad)],
            r0, v1, m1, tr, tv, swap(payload),
        )
        last = step + 1 == STEPS
        outs = [field, base]
        if last:
            outs += [load(1)]
        else:
            outs += [field] * 2 + [trace] * 3 + [sides(3), load(1 + depth)]
        t, base_now, *rest = call(
            lambda sizes, *refs, last=last: third_kernel(sizes, last, *refs),
            outs,
            r0, y, v2, m2, ty, tv2, swap(payload),
            fields=3 if last else 1,
        )
        if last:
            (payload,) = rest
            break
        u2, zf, tt, tu2, tz, side_y, payload = rest
        c, r0, v1, m1, tr, tv, payload = call(
            next_kernel,
            [field] * 4 + [trace] * 2 + [load(2 * depth + narrow)],
            c, r0, y, t, sc, u1, u2, zf, tc, tr, tu, ty, tu2, tt, tz,
            side_c, side_r, side_y, base_now, swap(payload),
            fields=1,
        )
    out = pl.pallas_call(
        functools.partial(last_kernel, patches),
        out_shape=shape(rows, LANES, LANES),
        in_specs=[vmem] * 6,
        out_specs=vmem,
        compiler_params=params,
    )(c, r0, y, t, base_now, swap(payload))
    return out[None]


def solution(mesh):
    placed = (P("patch", "sec", None, None), P(), P(), P())
    return jax.shard_map(
        functools.partial(shards, mesh.shape["patch"], mesh.shape["sec"]),
        mesh=mesh,
        in_specs=placed,
        out_specs=P("patch", "sec", None, None),
        check_vma=False,
    )
```

```python
import functools

import jax
import jax.numpy as jnp
import numpy as np
from jax import lax
from jax.experimental import pallas as pl
from jax.experimental.pallas import tpu as pltpu
from jax.sharding import PartitionSpec as P

STEPS = 2
MASS_BAND = (2416.0 / 5040.0, 1191.0 / 5040.0, 120.0 / 5040.0, 1.0 / 5040.0)
STIFF_BAND = (2.0 / 3.0, -0.125, -0.2, -1.0 / 120.0)
SCALE = 5040.0
MASS_HIGH, MASS_LOW = (2416.0, 1192.0, 120.0, 1.0), (0.0, -1.0, 0.0, 0.0)
STIFF_HIGH, STIFF_LOW = (3360.0, -632.0, -1008.0, -42.0), (0.0, 2.0, 0.0, 0.0)
PENALTY = 2.0
TIME_STEP = 1.0
STABILIZER = 2.0
GRADIENT_ENERGY = 0.5
HALF = TIME_STEP * GRADIENT_ENERGY
TWICE = TIME_STEP * STABILIZER
EXACT = lax.Precision.HIGHEST
LANES = 128
PAD = 8
KINDS = 6
SUMS = 4 * KINDS
NARROW, BROAD = 16, 32
COST = 1 << 34


def band_matrix(band, size):
    out = np.zeros((size, size), np.float32)
    for offset, value in enumerate(band):
        for row in range(size - offset):
            out[row, row + offset] = value
            out[row + offset, row] = value
    return out


def dot(left, right):
    return jnp.dot(left, right, precision=EXACT, preferred_element_type=jnp.float32)


def right_matrix(mass_band, stiff_band):
    mass, stiff = band_matrix(mass_band, LANES), band_matrix(stiff_band, LANES)
    return np.block([[mass, stiff], [np.zeros_like(mass), mass]])


def constants():
    high = right_matrix(MASS_HIGH, STIFF_HIGH).astype(jnp.bfloat16)
    low = right_matrix(MASS_LOW, STIFF_LOW).astype(jnp.bfloat16)
    return high, low


def banded(distance, band, inside=None):
    out = jnp.zeros(distance.shape, jnp.float32)
    for offset, value in enumerate(band):
        hit = distance == offset
        out = jnp.where(hit if inside is None else hit & inside, value, out)
    return out


class Body:
    def __init__(self, sizes, refs, copies=1):
        self.depth, self.patches, self.slabs = sizes
        self.copies = copies
        self.tables, refs = refs[:3], refs[3:]
        self.near, self.strip, self.turned, self.stood = refs[-4:]
        if len(refs) > 4:
            self.high, self.low = refs[:2]
        self.me = lax.axis_index("patch")
        self.lane = lax.broadcasted_iota(jnp.int32, (self.depth, LANES), 1)
        self.first, self.last = self.lane == 0, self.lane == LANES - 1
        self.wide = lax.broadcasted_iota(jnp.int32, (LANES, LANES), 1)
        self.edge = (self.wide == 0) | (self.wide == LANES - 1)
        row = lax.broadcasted_iota(jnp.int32, (LANES, LANES), 0)
        self.reverse = jnp.where(row + self.wide == LANES - 1, 1.0, 0.0)
        distance = jnp.abs(row - self.wide)
        self.plain = jnp.concatenate(
            [banded(distance, MASS_BAND), banded(distance, STIFF_BAND)], axis=1
        )
        n = 4 * self.depth
        row = lax.broadcasted_iota(jnp.int32, (n, 2 * n), 0)
        column = lax.broadcasted_iota(jnp.int32, (n, 2 * n), 1)
        left = column < n
        column = jnp.where(left, column, column - n)
        inside = row < 0
        for low in range(0, n, self.depth):
            top = low + self.depth
            inside = inside | ((row >= low) & (row < top) & (column >= low) & (column < top))
        distance = jnp.abs(row - column)
        self.third = banded(distance, MASS_BAND, inside & left) + banded(
            distance, STIFF_BAND, inside & ~left
        )

    def partner(self, patch, face):
        return self.tables[0][face, patch]

    def face_id(self, patch, face):
        return self.tables[1][face, patch]

    def flip(self, patch, face):
        return self.tables[2][face, patch]

    def split(self, value):
        pieces = []
        for last in (False, False, True):
            piece = value.astype(jnp.bfloat16)
            pieces.append(piece)
            if not last:
                value = value - piece.astype(jnp.float32)
        return pieces

    def stiff0(self, layer, finish):
        depth = self.depth
        zeros = jnp.zeros((PAD, LANES), jnp.float32)
        for i in range(4):
            self.near[i, :PAD] = zeros
            self.near[i, PAD + LANES :] = zeros
        for z in range(depth):
            middle = layer(z)
            massed = (MASS_BAND[0] / SCALE) * middle
            stiffed = (STIFF_BAND[0] / SCALE) * middle
            for offset in (1, 2, 3):
                near = [layer(k) for k in (z - offset, z + offset) if 0 <= k < depth]
                if near:
                    both = near[0] if len(near) == 1 else near[0] + near[1]
                    massed = massed + (MASS_BAND[offset] / SCALE) * both
                    stiffed = stiffed + (STIFF_BAND[offset] / SCALE) * both
            pieces = self.split(jnp.concatenate([massed, stiffed], axis=1))
            mixed = None
            for matrix, parts in ((self.high, pieces), (self.low, pieces[:2])):
                for piece in parts:
                    term = jnp.dot(piece, matrix[...], preferred_element_type=jnp.float32)
                    mixed = term if mixed is None else mixed + term
            a, b = 2 * (z % 2), 2 * (z % 2) + 1
            self.near[a, PAD : PAD + LANES] = mixed[:, :LANES]
            self.near[b, PAD : PAD + LANES] = mixed[:, LANES:]
            stiff = STIFF_BAND[0] * mixed[:, :LANES] + MASS_BAND[0] * mixed[:, LANES:]
            mass = MASS_BAND[0] * mixed[:, :LANES]
            for o in (1, 2, 3):
                low, high = slice(PAD - o, PAD - o + LANES), slice(PAD + o, PAD + o + LANES)
                both = self.near[a, low] + self.near[a, high]
                stiff = stiff + STIFF_BAND[o] * both
                stiff = stiff + MASS_BAND[o] * (self.near[b, low] + self.near[b, high])
                mass = mass + MASS_BAND[o] * both
            finish(z, stiff, mass)

    def strips(self, field, count=4):
        depth = field.shape[0]
        group = min(depth, 8)
        rows0 = [field[:, d, :] for d in range(count)]
        rows1 = [field[:, LANES - 1 - d, :] for d in range(count)]
        wanted = list(range(4 - count, 4 + count))
        pieces = {i: [] for i in wanted}
        for start in range(0, depth, group):
            stacked = jnp.zeros((LANES, LANES), jnp.float32)
            for j in range(group):
                rolled = pltpu.roll(field[start + j], (8 * j + 4) % LANES, 1)
                stacked = jnp.where((self.wide >> 3) == j, rolled, stacked)
            self.strip[...] = jnp.transpose(stacked)
            for i in wanted:
                pieces[i].append(self.strip[pl.ds(i, group, stride=8), :])
        columns = {i: jnp.concatenate(p, axis=0) if len(p) > 1 else p[0] for i, p in pieces.items()}
        return [
            rows0,
            rows1,
            [columns[4 + d] for d in range(count)],
            [columns[3 - d] for d in range(count)],
        ]

    def traces(self, field):
        return [strip[0] for strip in self.strips(field, 1)]

    def jumps(self, mine, other):
        return [PENALTY * (a - b) for a, b in zip(mine, other)]

    def stand(self, jump):
        for start in range(0, self.depth, 8):
            self.turned[pl.ds(0, 8, stride=2), :] = jump[3][start : start + 8]
            self.turned[pl.ds(1, 8, stride=2), :] = jump[2][start : start + 8]
            self.stood[start // 8] = jnp.transpose(self.turned[...])

    def column(self, z):
        rolled = pltpu.roll(self.stood[z // 8], (LANES - 2 * (z % 8) - 1) % LANES, 1)
        return jnp.where(self.edge, rolled, 0.0)

    def add_rows(self, field, jump, factor):
        field[:, 0, :] = field[:, 0, :] + factor * jump[0]
        field[:, LANES - 1, :] = field[:, LANES - 1, :] + factor * jump[1]

    def stiff_trace(self, inner, jump):
        out = []
        for f in range(4):
            side = f & 1
            low, high = (2, 3) if f < 2 else (0, 1)
            at = side * (LANES - 1)
            ends = []
            for face, end in ((low, 0), (high, LANES - 1)):
                shift = (end - at) % LANES
                ends.append(pltpu.roll(jump[face], shift, 1) if shift else jump[face])
            out.append(inner[f] + jump[f] + self.ends(*ends))
        return out

    def slab(self, stiffs, masses, plain=None):
        n = 4 * self.depth
        rows = [stack(masses), stack(stiffs)] + ([] if plain is None else [stack(plain)])
        both = dot(stack(rows), self.plain)
        lower = both[n : 2 * n, :LANES] + both[:n, LANES:]
        if plain is not None:
            lower = lower + both[2 * n :, :LANES]
        out = dot(self.third, stack([lower, both[:n, :LANES]]))
        return unstack(out, self.depth)

    def depth_sum(self, strip, band):
        out = band[0] * strip[0]
        for d in (1, 2, 3):
            out = out + band[d] * strip[d]
        return out

    def corner_table(self, trace, inner=None):
        table = jnp.zeros((self.depth, LANES), jnp.float32)
        ends = (0, LANES - 1)
        kinds = 1 if inner is None else KINDS
        if inner is not None:
            arms = dot(stack(trace), self.plain)
        for rs in range(2):
            for cs in range(2):
                slot = kinds * (2 * rs + cs)
                values = [(trace[rs], ends[cs])]
                if inner is not None:
                    values.append((inner[rs], ends[cs]))
                    for face, end in ((rs, ends[cs]), (2 + cs, ends[rs])):
                        part = arms[face * self.depth : (face + 1) * self.depth]
                        values.append((part[:, :LANES], end))
                        values.append((part[:, LANES:], end))
                for kind, (value, end) in enumerate(values):
                    shift = (slot + kind - end) % LANES
                    rolled = pltpu.roll(value, shift, 1) if shift else value
                    table = jnp.where(self.lane == slot + kind, rolled, table)
        return table

    def pack(self, table, width):
        count = width // NARROW
        rows = []
        for start in range(0, self.depth, 8):
            for low in range(count):
                total = None
                for i in range(low, 8, count):
                    layer = table[start + i : start + i + 1]
                    part = pltpu.roll(layer, LANES - NARROW * i, 1) if i else layer
                    total = part if total is None else total + part
                rows.append(total)
        return stack(rows) if len(rows) > 1 else rows[0]

    def send(self, payload, groups, packed):
        copies = self.copies
        rows = payload.shape[0] // (self.patches * copies)
        for f in range(4):
            to, at = self.partner(self.me, f) * copies, 0
            for group in groups:
                high = group[f].shape[0]
                for s in range(copies):
                    payload[pl.ds((to + s) * rows + at, high), :] = group[f]
                at += high
        for to in range(self.patches * copies):
            payload[to * rows + at : (to + 1) * rows, :] = packed

    def take(self, recv, patch, lo, count):
        rows = recv.shape[0] // (self.patches * self.copies)
        out = None
        for s in range(self.copies):
            part = recv[pl.ds((patch * self.copies + s) * rows + lo, count), :]
            out = part if out is None else out + part
        return out

    def received(self, recv, count, at=0):
        rows = count * self.depth
        return self.oriented(
            [self.take(recv, self.partner(self.me, f), at, rows) for f in range(4)], count
        )

    def oriented(self, raw, count):
        depth = self.depth
        rows = count * depth
        turned = dot(stack(raw), self.reverse)
        out = []
        for f in range(4):
            flipped = self.flip(self.me, f) == 1
            out.append(jnp.where(flipped, turned[f * rows : (f + 1) * rows], raw[f]))
        return [[out[f][i * depth : (i + 1) * depth] for f in range(4)] for i in range(count)]

    def corner(self, face, side):
        q, f1 = self.partner(self.me, face), self.face_id(self.me, face)
        eq = side ^ self.flip(self.me, face)
        s1 = f1 & 1
        upright = f1 < 2
        f2 = jnp.where(upright, 2 + eq, eq)
        kq = jnp.where(upright, 2 * s1 + eq, 2 * eq + s1)
        tq = jnp.where(upright, 4, 2)
        r, g = self.partner(q, f2), self.face_id(q, f2)
        s2 = s1 ^ self.flip(q, f2)
        flat = g < 2
        k = jnp.where(flat, 2 * (g & 1) + s2, 2 * s2 + (g & 1))
        t = jnp.where(flat, 2, 4)
        g2 = jnp.where(flat, 2 + s2, s2)
        r2, h = self.partner(r, g2), self.face_id(r, g2)
        s4 = (g & 1) ^ self.flip(r, g2)
        k2 = jnp.where(h < 2, 2 * (h & 1) + s4, 2 * s4 + (h & 1))
        return (q, kq, tq), (r, k, t), (r2, k2)

    def corners(self):
        return [[self.corner(f, s) for s in range(2)] for f in range(4)]

    def look(self, recv, at, patch, lane, side, width):
        count = width // NARROW
        shift = (side * (LANES - 1) + LANES - lane) & (LANES - 1)
        packed = self.take(recv, patch, at, self.depth // 8 * count)
        odd = (lax.broadcasted_iota(jnp.int32, (8, LANES), 0) & 1) == 1
        out = []
        for k in range(0, self.depth // 8 * count, count):
            spread = jnp.broadcast_to(packed[k : k + 1], (8, LANES))
            if count == 2:
                spread = jnp.where(odd, packed[k + 1 : k + 2], spread)
            out.append(pltpu.roll(spread, 0, 1, stride=NARROW, stride_axis=0))
        return pltpu.roll(stack(out) if len(out) > 1 else out[0], shift, 1)

    def ends(self, low, high):
        return jnp.where(self.first, low, jnp.where(self.last, high, 0.0))

    def other_stiff(self, recv, at, mine, theirs, inner, corners, kinds, width):
        out = []
        edge = self.first | self.last
        for f in range(4):
            across = []
            for s in range(2):
                r, k, t = corners[f][s][1]
                across.append(self.look(recv, at, r, kinds * k, s, width))
            value = inner[f] + PENALTY * (theirs[f] - mine[f])
            far = PENALTY * (theirs[f] - self.ends(*across))
            out.append(value + jnp.where(edge, far, 0.0))
        return out


def stack(values):
    return jnp.concatenate(values, 0)


def unstack(value, depth):
    return [value[f * depth : (f + 1) * depth] for f in range(4)]


def cubic(x, s):
    return x * x * x - x + GRADIENT_ENERGY * s


def start_kernel(sizes, own, payload, *refs):
    body = Body(sizes, refs, sizes[2])
    rows = own.shape[0]
    layer = lax.broadcasted_iota(jnp.int32, (body.depth, LANES), 0)
    low = lax.axis_index("sec") * rows
    here = (layer >= low) & (layer < low + rows)

    def place(value):
        return jnp.where(here, stack([value] * body.slabs), 0.0)

    strips = body.strips(own)
    trace = [s[0] for s in strips]
    inner = body.slab(
        [place(body.depth_sum(s, STIFF_BAND)) for s in strips],
        [place(body.depth_sum(s, MASS_BAND)) for s in strips],
    )
    table = body.corner_table([place(a) for a in trace])
    body.send(payload, [trace, inner], body.pack(table, NARROW))


def flux_tail(body, current, mine, other, r0, v1, m1, tr, tv, payload, potential):
    jump = body.jumps(mine, other)
    body.stand(jump)

    def residual(z, stiff, mass):
        r0[z] = -TIME_STEP * (stiff + body.column(z))

    body.stiff0(lambda z: potential[z], residual)
    body.add_rows(r0, jump, -TIME_STEP)

    def image(z, stiff, mass):
        v1[z] = stiff
        m1[z] = mass

    body.stiff0(lambda z: r0[z], image)
    trace, inner = body.traces(r0), body.traces(v1)
    tr[...], tv[...] = stack(trace), stack(inner)
    body.copies = 1
    body.send(payload, [trace, inner], body.pack(body.corner_table(trace), NARROW))


def middle_kernel(sizes, *refs):
    slabs, refs = refs[: sizes[2]], refs[sizes[2] :]
    c, v0, tc, tv = refs[:4]
    body = Body(sizes, refs[4:])
    count = body.slabs
    rows = body.depth // count
    for k, slab in enumerate(slabs):
        c[pl.ds(lax.rem(lax.axis_index("sec") + k, count) * rows, rows)] = slab[...]

    def image(z, stiff, mass):
        v0[z] = stiff

    body.stiff0(lambda z: c[z], image)
    tc[...], tv[...] = stack(body.traces(c)), stack(body.traces(v0))


def first_kernel(sizes, c, v0, tc, tv0, recv, sc, r0, v1, m1, ts, tr, tv, sides, payload,
                 potential, *refs):
    body = Body(sizes, refs, sizes[2])
    depth, count = body.depth, body.slabs
    rows = depth // count
    high = recv.shape[0] // (body.patches * count)
    raw = []
    for f in range(4):
        q = body.partner(body.me, f)
        parts = [recv[pl.ds((q * count + s) * high, rows), :] for s in range(count)]
        raw.append(stack(parts + [body.take(recv, q, rows, depth)]))
    other, inner = body.oriented(raw, 2)
    mine = unstack(tc, depth)
    jump = body.jumps(mine, other)
    body.stand(jump)
    for z in range(depth):
        sc[z] = v0[z] + body.column(z)
    body.add_rows(sc, jump, 1.0)
    for z in range(depth):
        potential[z] = cubic(c[z], sc[z])
    mine_s = body.stiff_trace(unstack(tv0, depth), jump)
    other_s = body.other_stiff(recv, rows + depth, mine, other, inner, body.corners(), 1, NARROW)
    ts[...] = stack(mine_s)
    sides[0], sides[1] = stack(other), stack(other_s)
    mine_p = [cubic(x, s) for x, s in zip(mine, mine_s)]
    other_p = [cubic(x, s) for x, s in zip(other, other_s)]
    flux_tail(body, c, mine_p, other_p, r0, v1, m1, tr, tv, payload, potential)


def second_kernel(sizes, r0, v1, m1, tr, tv, recv, u1, y, v2, m2, ty, tv2, tu, sides, payload,
                  *refs):
    body = Body(sizes, refs)
    depth = body.depth
    other, inner = body.received(recv, 2)
    mine = unstack(tr, depth)
    jump = body.jumps(mine, other)
    body.stand(jump)
    for z in range(depth):
        u1[z] = v1[z] + body.column(z)
    body.add_rows(u1, jump, 1.0)
    mine_s = body.stiff_trace(unstack(tv, depth), jump)
    other_s = body.other_stiff(
        recv, 2 * depth, mine, other, inner, body.corners(), 1, NARROW
    )
    tu[...] = stack(mine_s)
    sides[0], sides[1] = stack(other), stack(other_s)
    jump = body.jumps(mine_s, other_s)
    body.stand(jump)

    def image(z, stiff, mass):
        y[z] = m1[z] + TWICE * u1[z] + HALF * (stiff + body.column(z))

    body.stiff0(lambda z: u1[z], image)
    body.add_rows(y, jump, HALF)
    sums = [[], [], []]

    def again(z, stiff, mass):
        v2[z] = stiff
        m2[z] = mass
        a, b = r0[z], y[z]
        for i, product in enumerate((a * a, a * b, b * b)):
            sums[i].append(jnp.sum(product, axis=0, keepdims=True))

    body.stiff0(lambda z: y[z], again)
    strips_y, strips = body.strips(y), body.strips(v2)
    trace, inner = [s[0] for s in strips_y], [s[0] for s in strips]
    ty[...], tv2[...] = stack(trace), stack(inner)
    mixed = body.slab(
        [HALF * body.depth_sum(s, STIFF_BAND) for s in strips],
        [HALF * body.depth_sum(s, MASS_BAND) for s in strips],
        [body.depth_sum(s, MASS_BAND) for s in strips_y],
    )
    outer = [TWICE * a + b for a, b in zip(inner, mixed)]
    table = body.corner_table(trace, inner)
    for i in range(3):
        total = jnp.sum(stack(sums[i]), axis=1, keepdims=True)
        table = jnp.where(body.lane == SUMS + i, total, table)
    body.send(payload, [trace, inner, outer], body.pack(table, BROAD))


def third_kernel(sizes, last, r0, y, v2, m2, ty, tv2, recv, *refs):
    if last:
        t, base, payload, u2, zf, mt = refs[:6]
        body = Body(sizes, refs[6:])
    else:
        t, base, u2, zf, tt, tu2, tz, sides, payload, mt = refs[:10]
        body = Body(sizes, refs[10:])
    depth, patches = body.depth, body.patches
    at = 3 * depth
    packed = depth * BROAD // LANES
    known = recv[at : at + packed, :]
    for p in range(1, patches):
        known = known + recv[p * (at + packed) + at : (p + 1) * (at + packed), :]
    odd = lax.broadcasted_iota(jnp.int32, (packed, LANES), 0) & 1
    slot = lax.broadcasted_iota(jnp.int32, (packed, LANES), 1) + NARROW * odd
    slot = slot & (BROAD - 1)
    m0, m1, m2s = [
        jnp.sum(jnp.where(slot == SUMS + i, known, 0.0), keepdims=True) for i in range(3)
    ]
    a0 = m0 / m1
    other, inner, outer = body.received(recv, 3)
    corners = body.corners()
    mine = unstack(ty, depth)
    jump = body.jumps(mine, other)
    body.stand(jump)
    for z in range(depth):
        u2[z] = v2[z] + body.column(z)
    body.add_rows(u2, jump, 1.0)
    mine_s = body.stiff_trace(unstack(tv2, depth), jump)
    other_s = body.other_stiff(recv, at, mine, other, inner, corners, KINDS, BROAD)
    masses, stiffs, far = [], [], []
    for f in range(4):
        arm_m, arm_k, across = [], [], []
        for s in range(2):
            (q, kq, tq), (r, k, kind), (r2, k2) = corners[f][s]
            look = functools.partial(body.look, recv, at, side=s, width=BROAD)
            arm_m.append(look(q, KINDS * kq + tq) - look(r, KINDS * k + kind))
            arm_k.append(look(q, KINDS * kq + tq + 1) - look(r, KINDS * k + kind + 1))
            value = look(r, KINDS * k)
            across.append(
                look(r, KINDS * k + 1)
                + PENALTY * (value - other[f])
                + PENALTY * (value - look(r2, KINDS * k2))
            )
        theirs = PENALTY * (other[f] - mine[f])
        masses.append(MASS_BAND[0] * theirs + PENALTY * body.ends(*arm_m))
        stiffs.append(STIFF_BAND[0] * theirs + PENALTY * body.ends(*arm_k))
        far.append(body.ends(*across))
    pushed = body.slab(stiffs, masses)
    edge = body.first | body.last
    other_t = []
    for f in range(4):
        again = pushed[f] + PENALTY * (other_s[f] - mine_s[f])
        again = again + jnp.where(edge, PENALTY * (other_s[f] - far[f]), 0.0)
        image = outer[f] + TWICE * (other_s[f] - inner[f]) + HALF * again
        other_t.append(other[f] - a0 * image)
    jump = body.jumps(mine_s, other_s)
    body.stand(jump)

    def turn(z, stiff, mass):
        t[z] = y[z] - a0 * (m2[z] + TWICE * u2[z] + HALF * (stiff + body.column(z)))

    body.stiff0(lambda z: u2[z], turn)
    body.add_rows(t, jump, -HALF * a0)
    mine_t = body.traces(t)
    jump = body.jumps(mine_t, other_t)
    body.stand(jump)

    def image(z, stiff, mass):
        zf[z] = stiff + body.column(z)
        mt[z] = mass

    body.stiff0(lambda z: t[z], image)
    body.add_rows(zf, jump, 1.0)
    sums = [jnp.zeros((8, LANES), jnp.float32)] * 6
    for z in range(depth):
        b, x, s = y[z], t[z], zf[z]
        a = r0[z] - a0 * b
        energy = x * (mt[z] + TWICE * s) + HALF * (s * s)
        for i, product in enumerate((a * a, a * x, a * b, x * x, x * b, energy)):
            sums[i] = sums[i] + jnp.sum(product.reshape(LANES // 8, 8, LANES), axis=0)
    moments = jnp.zeros((1, LANES), jnp.float32)
    lane = lax.broadcasted_iota(jnp.int32, (1, LANES), 1)
    for i, value in enumerate(sums):
        value = jnp.sum(jnp.sum(value, axis=0, keepdims=True), axis=1, keepdims=True)
        moments = jnp.where(lane == i, value, moments)
    for i, value in enumerate((a0, m0, m1, m2s)):
        base[i : i + 1, :] = jnp.broadcast_to(value, (1, LANES))
    rows = payload.shape[0] // patches
    for to in range(patches):
        payload[to * rows : to * rows + 1, :] = moments
    if not last:
        trace = body.traces(zf)
        tt[...], tu2[...], tz[...] = stack(mine_t), stack(mine_s), stack(trace)
        sides[0], sides[1], sides[2] = stack(other), stack(other_s), stack(other_t)
        for f in range(4):
            payload[pl.ds(body.partner(body.me, f) * rows + 1, depth), :] = trace[f]


def weights(patches, base, recv):
    rows = recv.shape[0] // patches
    total = recv[:1, :]
    for p in range(1, patches):
        total = total + recv[p * rows : p * rows + 1, :]
    a0, m0, m1, m2 = [base[i : i + 1, :1] for i in range(4)]
    rr1, g1, g2, tt, ty, tat = [total[:, i : i + 1] for i in range(6)]
    b0 = rr1 / m0
    a1 = rr1 / (g1 + 2.0 * b0 * g2 + b0 * b0 * m1)
    rr2 = rr1 - 2.0 * a1 * (g1 + b0 * g2) + a1 * a1 * (tt + 2.0 * b0 * ty + b0 * b0 * m2)
    b1 = rr2 / rr1
    shift = a1 * b0 / a0
    c1, c0, c2 = 1.0 + b1 + shift, b1 * b0 - shift, -a1
    a2 = rr2 / (
        c1 * c1 * g1
        + c0 * c0 * m1
        + c2 * c2 * tat
        + 2.0 * (c1 * c0 * g2 + c1 * c2 * tt + c0 * c2 * ty)
    )
    return a0 + a1 * (1.0 + b0) + a2 * (c1 + c0), -a0 * (a1 + a2 * c1), a2 * c2


def next_kernel(sizes, c, r0, y, t, sc, u1, u2, zf, tc, ts, tr, tu, ty, tu2, tt, tz,
                side_c, side_r, side_y, base, recv,
                cn, rn, v1, m1, trn, tvn, payload, potential, *refs):
    body = Body(sizes, refs)
    depth = body.depth
    x = weights(body.patches, base, recv)

    def mix(*values):
        return values[0] + x[0] * values[1] + x[1] * values[2] + x[2] * values[3]

    for z in range(depth):
        cn[z] = mix(c[z], r0[z], y[z], t[z])
        potential[z] = cubic(cn[z], mix(sc[z], u1[z], u2[z], zf[z]))
    (side_z,) = body.received(recv, 1, 1)
    mine = cubic(
        mix(tc[...], tr[...], ty[...], tt[...]), mix(ts[...], tu[...], tu2[...], tz[...])
    )
    other = cubic(
        mix(side_c[0], side_r[0], side_y[0], side_y[2]),
        mix(side_c[1], side_r[1], side_y[1], stack(side_z)),
    )
    flux_tail(body, cn, unstack(mine, depth), unstack(other, depth),
              rn, v1, m1, trn, tvn, payload, potential)


def last_kernel(patches, c, r0, y, t, base, recv, out):
    x0, x1, x2 = weights(patches, base, recv)
    rows = out.shape[0]
    low = lax.axis_index("sec") * rows
    for z in range(rows):
        k = low + z
        out[z] = c[k] + x0 * r0[k] + x1 * y[k] + x2 * t[k]


def shards(patches, slabs, concentration, partner, face_id, flip):
    own = concentration[0]
    rows = own.shape[0]
    depth = rows * slabs
    halves = [own]
    for k in range(1, slabs):
        halves.append(lax.ppermute(own, "sec", [((i + k) % slabs, i) for i in range(slabs)]))
    matrices = [jnp.asarray(x) for x in constants()]
    tables = [partner.T, face_id.T, flip.T]
    vmem, smem = pl.BlockSpec(memory_space=pltpu.VMEM), pl.BlockSpec(memory_space=pltpu.SMEM)
    params = pltpu.CompilerParams(vmem_limit_bytes=(4 + depth) << 20)

    def shape(*dims):
        return jax.ShapeDtypeStruct(dims, jnp.float32)

    field, trace, base = shape(depth, LANES, LANES), shape(4 * depth, LANES), shape(8, LANES)

    def sides(count):
        return shape(count, 4 * depth, LANES)

    def load(count):
        return shape(patches * count, LANES)

    def call(kernel, outs, *args, fields=0, consts=matrices, cost=None):
        count, head = len(args), 3 + len(consts)
        inside = [pltpu.VMEM((depth, LANES, LANES), jnp.float32)] * fields
        shared = [
            pltpu.VMEM((4, LANES + 2 * PAD, LANES), jnp.float32),
            pltpu.VMEM((LANES, LANES), jnp.float32),
            pltpu.VMEM((LANES, LANES), jnp.float32),
            pltpu.VMEM((-(-depth // 8), LANES, LANES), jnp.float32),
        ]

        def run(*refs):
            common, rest = refs[:head], refs[head:]
            cut = len(rest) - len(shared)
            kernel((depth, patches, slabs), *rest[:cut], *common, *rest[cut:])

        return pl.pallas_call(
            run,
            out_shape=outs,
            in_specs=[smem] * 3 + [vmem] * (len(consts) + count),
            out_specs=[vmem] * len(outs),
            scratch_shapes=inside + shared,
            compiler_params=params,
            cost_estimate=cost,
            name=kernel.__name__ if hasattr(kernel, "__name__") else "third_kernel",
        )(*tables, *consts, *args)

    def swap(payload, axes="patch", parts=patches):
        rows = payload.shape[0] // parts
        moved = lax.all_to_all(payload.reshape(parts, 1, rows * LANES), axes, 0, 0)
        return moved.reshape(parts * rows, LANES)

    narrow, broad = depth * NARROW // LANES, depth * BROAD // LANES
    (payload,) = call(
        start_kernel,
        [load(slabs * (rows + depth + narrow))],
        own,
        consts=[],
        cost=pl.CostEstimate(flops=COST, bytes_accessed=4 * own.size, transcendentals=0),
    )
    c, v0, tc, tv0 = call(
        middle_kernel,
        [field, field, trace, trace],
        *halves,
        cost=pl.CostEstimate(flops=COST, bytes_accessed=4 * own.size, transcendentals=0),
    )
    sc, r0, v1, m1, ts, tr, tv, side_c, payload = call(
        first_kernel,
        [field] * 4 + [trace] * 3 + [sides(2), load(2 * depth + narrow)],
        c, v0, tc, tv0, swap(payload, ("patch", "sec"), patches * slabs),
        fields=1,
    )
    for step in range(STEPS):
        u1, y, v2, m2, ty, tv2, tu, side_r, payload = call(
            second_kernel,
            [field] * 4 + [trace] * 3 + [sides(2), load(3 * depth + broad)],
            r0, v1, m1, tr, tv, swap(payload),
        )
        last = step + 1 == STEPS
        outs = [field, base]
        if last:
            outs += [load(1)]
        else:
            outs += [field] * 2 + [trace] * 3 + [sides(3), load(1 + depth)]
        t, base_now, *rest = call(
            lambda sizes, *refs, last=last: third_kernel(sizes, last, *refs),
            outs,
            r0, y, v2, m2, ty, tv2, swap(payload),
            fields=3 if last else 1,
        )
        if last:
            (payload,) = rest
            break
        u2, zf, tt, tu2, tz, side_y, payload = rest
        c, r0, v1, m1, tr, tv, payload = call(
            next_kernel,
            [field] * 4 + [trace] * 2 + [load(2 * depth + narrow)],
            c, r0, y, t, sc, u1, u2, zf, tc, ts, tr, tu, ty, tu2, tt, tz,
            side_c, side_r, side_y, base_now, swap(payload),
            fields=1,
        )
    out = pl.pallas_call(
        functools.partial(last_kernel, patches),
        out_shape=shape(rows, LANES, LANES),
        in_specs=[vmem] * 6,
        out_specs=vmem,
        compiler_params=params,
    )(c, r0, y, t, base_now, swap(payload))
    return out[None]


def solution(mesh):
    placed = (P("patch", "sec", None, None), P(), P(), P())
    return jax.shard_map(
        functools.partial(shards, mesh.shape["patch"], mesh.shape["sec"]),
        mesh=mesh,
        in_specs=placed,
        out_specs=P("patch", "sec", None, None),
        check_vma=False,
    )
```

```python
import functools

import jax
import jax.numpy as jnp
import numpy as np
from jax import lax
from jax.experimental import pallas as pl
from jax.experimental.pallas import tpu as pltpu
from jax.sharding import PartitionSpec as P

STEPS = 2
MASS_BAND = (2416.0 / 5040.0, 1191.0 / 5040.0, 120.0 / 5040.0, 1.0 / 5040.0)
STIFF_BAND = (2.0 / 3.0, -0.125, -0.2, -1.0 / 120.0)
SCALE = 5040.0
MASS_HIGH, MASS_LOW = (2416.0, 1192.0, 120.0, 1.0), (0.0, -1.0, 0.0, 0.0)
STIFF_HIGH, STIFF_LOW = (3360.0, -632.0, -1008.0, -42.0), (0.0, 2.0, 0.0, 0.0)
PENALTY = 2.0
TIME_STEP = 1.0
STABILIZER = 2.0
GRADIENT_ENERGY = 0.5
HALF = TIME_STEP * GRADIENT_ENERGY
TWICE = TIME_STEP * STABILIZER
EXACT = lax.Precision.HIGHEST
LANES = 128
PAD = 8
KINDS = 6
SUMS = 4 * KINDS
NARROW, BROAD = 16, 32
COST = 1 << 34


def band_matrix(band, size):
    out = np.zeros((size, size), np.float32)
    for offset, value in enumerate(band):
        for row in range(size - offset):
            out[row, row + offset] = value
            out[row + offset, row] = value
    return out


def dot(left, right):
    return jnp.dot(left, right, precision=EXACT, preferred_element_type=jnp.float32)


def right_matrix(mass_band, stiff_band):
    mass, stiff = band_matrix(mass_band, LANES), band_matrix(stiff_band, LANES)
    return np.block([[mass, stiff], [np.zeros_like(mass), mass]])


def constants():
    high = right_matrix(MASS_HIGH, STIFF_HIGH).astype(jnp.bfloat16)
    low = right_matrix(MASS_LOW, STIFF_LOW).astype(jnp.bfloat16)
    return high, low


def banded(distance, band, inside=None):
    out = jnp.zeros(distance.shape, jnp.float32)
    for offset, value in enumerate(band):
        hit = distance == offset
        out = jnp.where(hit if inside is None else hit & inside, value, out)
    return out


def face_weights():
    mass, stiff = band_matrix(MASS_BAND, 16), band_matrix(STIFF_BAND, 16)
    mass, stiff = mass.astype(np.float64), stiff.astype(np.float64)
    pairs = ((stiff, stiff), (stiff, mass), (mass, stiff), (mass, mass))
    return [[float(x) for x in (a @ b)[0, :7]] for a, b in pairs]


class Body:
    def __init__(self, sizes, refs, copies=1):
        self.depth, self.patches, self.slabs = sizes
        self.copies = copies
        self.tables, refs = refs[:3], refs[3:]
        self.near, self.strip, self.turned, self.stood = refs[-4:]
        if len(refs) > 4:
            self.high, self.low = refs[:2]
        self.me = lax.axis_index("patch")
        self.lane = lax.broadcasted_iota(jnp.int32, (self.depth, LANES), 1)
        self.first, self.last = self.lane == 0, self.lane == LANES - 1
        self.wide = lax.broadcasted_iota(jnp.int32, (LANES, LANES), 1)
        self.edge = (self.wide == 0) | (self.wide == LANES - 1)
        row = lax.broadcasted_iota(jnp.int32, (LANES, LANES), 0)
        self.reverse = jnp.where(row + self.wide == LANES - 1, 1.0, 0.0)
        distance = jnp.abs(row - self.wide)
        self.plain = jnp.concatenate(
            [banded(distance, MASS_BAND), banded(distance, STIFF_BAND)], axis=1
        )
        n = 4 * self.depth
        row = lax.broadcasted_iota(jnp.int32, (n, 2 * n), 0)
        column = lax.broadcasted_iota(jnp.int32, (n, 2 * n), 1)
        left = column < n
        column = jnp.where(left, column, column - n)
        inside = row < 0
        for low in range(0, n, self.depth):
            top = low + self.depth
            inside = inside | ((row >= low) & (row < top) & (column >= low) & (column < top))
        distance = jnp.abs(row - column)
        self.third = banded(distance, MASS_BAND, inside & left) + banded(
            distance, STIFF_BAND, inside & ~left
        )

    def partner(self, patch, face):
        return self.tables[0][face, patch]

    def face_id(self, patch, face):
        return self.tables[1][face, patch]

    def flip(self, patch, face):
        return self.tables[2][face, patch]

    def split(self, value):
        pieces = []
        for last in (False, False, True):
            piece = value.astype(jnp.bfloat16)
            pieces.append(piece)
            if not last:
                value = value - piece.astype(jnp.float32)
        return pieces

    def stiff0(self, layer, finish):
        depth = self.depth
        zeros = jnp.zeros((PAD, LANES), jnp.float32)
        for i in range(4):
            self.near[i, :PAD] = zeros
            self.near[i, PAD + LANES :] = zeros
        for z in range(depth):
            middle = layer(z)
            massed = (MASS_BAND[0] / SCALE) * middle
            stiffed = (STIFF_BAND[0] / SCALE) * middle
            for offset in (1, 2, 3):
                near = [layer(k) for k in (z - offset, z + offset) if 0 <= k < depth]
                if near:
                    both = near[0] if len(near) == 1 else near[0] + near[1]
                    massed = massed + (MASS_BAND[offset] / SCALE) * both
                    stiffed = stiffed + (STIFF_BAND[offset] / SCALE) * both
            pieces = self.split(jnp.concatenate([massed, stiffed], axis=1))
            mixed = None
            for matrix, parts in ((self.high, pieces), (self.low, pieces[:2])):
                for piece in parts:
                    term = jnp.dot(piece, matrix[...], preferred_element_type=jnp.float32)
                    mixed = term if mixed is None else mixed + term
            a, b = 2 * (z % 2), 2 * (z % 2) + 1
            self.near[a, PAD : PAD + LANES] = mixed[:, :LANES]
            self.near[b, PAD : PAD + LANES] = mixed[:, LANES:]
            stiff = STIFF_BAND[0] * mixed[:, :LANES] + MASS_BAND[0] * mixed[:, LANES:]
            mass = MASS_BAND[0] * mixed[:, :LANES]
            for o in (1, 2, 3):
                low, high = slice(PAD - o, PAD - o + LANES), slice(PAD + o, PAD + o + LANES)
                both = self.near[a, low] + self.near[a, high]
                stiff = stiff + STIFF_BAND[o] * both
                stiff = stiff + MASS_BAND[o] * (self.near[b, low] + self.near[b, high])
                mass = mass + MASS_BAND[o] * both
            finish(z, stiff, mass)

    def strips(self, field, count=4):
        depth = field.shape[0]
        group = min(depth, 8)
        half = 8 if count > 4 else 4
        width, bits = 2 * half, (half * 2).bit_length() - 1
        rows0 = [field[:, d, :] for d in range(count)]
        rows1 = [field[:, LANES - 1 - d, :] for d in range(count)]
        wanted = list(range(half - count, half + count))
        pieces = {i: [] for i in wanted}
        for start in range(0, depth, group):
            stacked = jnp.zeros((LANES, LANES), jnp.float32)
            for j in range(group):
                rolled = pltpu.roll(field[start + j], (width * j + half) % LANES, 1)
                stacked = jnp.where((self.wide >> bits) == j, rolled, stacked)
            self.strip[...] = jnp.transpose(stacked)
            for i in wanted:
                pieces[i].append(self.strip[pl.ds(i, group, stride=width), :])
        columns = {i: jnp.concatenate(p, axis=0) if len(p) > 1 else p[0] for i, p in pieces.items()}
        return [
            rows0,
            rows1,
            [columns[half + d] for d in range(count)],
            [columns[half - 1 - d] for d in range(count)],
        ]

    def traces(self, field):
        return [strip[0] for strip in self.strips(field, 1)]

    def jumps(self, mine, other):
        return [PENALTY * (a - b) for a, b in zip(mine, other)]

    def stand(self, jump):
        for start in range(0, self.depth, 8):
            self.turned[pl.ds(0, 8, stride=2), :] = jump[3][start : start + 8]
            self.turned[pl.ds(1, 8, stride=2), :] = jump[2][start : start + 8]
            self.stood[start // 8] = jnp.transpose(self.turned[...])

    def column(self, z):
        rolled = pltpu.roll(self.stood[z // 8], (LANES - 2 * (z % 8) - 1) % LANES, 1)
        return jnp.where(self.edge, rolled, 0.0)

    def add_rows(self, field, jump, factor):
        field[:, 0, :] = field[:, 0, :] + factor * jump[0]
        field[:, LANES - 1, :] = field[:, LANES - 1, :] + factor * jump[1]

    def stiff_trace(self, inner, jump):
        out = []
        for f in range(4):
            side = f & 1
            low, high = (2, 3) if f < 2 else (0, 1)
            at = side * (LANES - 1)
            ends = []
            for face, end in ((low, 0), (high, LANES - 1)):
                shift = (end - at) % LANES
                ends.append(pltpu.roll(jump[face], shift, 1) if shift else jump[face])
            out.append(inner[f] + jump[f] + self.ends(*ends))
        return out

    def slabs_of(self, sets):
        n = 4 * self.depth
        rows = [stack(values) for values in sum(sets, ())]
        both = dot(stack(rows), self.plain)
        at, uppers, lowers = 0, [], []
        for values in sets:
            masses, stiffs = both[at + n : at + 2 * n], both[at : at + n, :LANES]
            lower = stiffs + masses[:, LANES:]
            if len(values) == 3:
                lower = lower + both[at + 2 * n : at + 3 * n, :LANES]
            uppers.append(lower)
            lowers.append(masses[:, :LANES])
            at += n * len(values)
        if len(sets) > 1:
            uppers, lowers = [jnp.concatenate(x, axis=1) for x in (uppers, lowers)]
        else:
            uppers, lowers = uppers[0], lowers[0]
        out = dot(self.third, stack([uppers, lowers]))
        return [unstack(out[:, k * LANES : (k + 1) * LANES], self.depth) for k in range(len(sets))]

    def slab(self, *lists):
        return self.slabs_of([lists])[0]

    def depth_sum(self, strip, band):
        out = band[0] * strip[0]
        for d in range(1, len(band)):
            out = out + band[d] * strip[d]
        return out

    def depth_sums(self, strips, band):
        return [self.depth_sum(strip, band) for strip in strips]

    def corner_table(self, trace, inner=None):
        table = jnp.zeros((self.depth, LANES), jnp.float32)
        ends = (0, LANES - 1)
        kinds = 1 if inner is None else KINDS
        if inner is not None:
            arms = dot(stack(trace), self.plain)
        for rs in range(2):
            for cs in range(2):
                slot = kinds * (2 * rs + cs)
                values = [(trace[rs], ends[cs])]
                if inner is not None:
                    values.append((inner[rs], ends[cs]))
                    for face, end in ((rs, ends[cs]), (2 + cs, ends[rs])):
                        part = arms[face * self.depth : (face + 1) * self.depth]
                        values.append((part[:, :LANES], end))
                        values.append((part[:, LANES:], end))
                for kind, (value, end) in enumerate(values):
                    shift = (slot + kind - end) % LANES
                    rolled = pltpu.roll(value, shift, 1) if shift else value
                    table = jnp.where(self.lane == slot + kind, rolled, table)
        return table

    def pack(self, table, width):
        count = width // NARROW
        rows = []
        for start in range(0, self.depth, 8):
            for low in range(count):
                total = None
                for i in range(low, 8, count):
                    layer = table[start + i : start + i + 1]
                    part = pltpu.roll(layer, LANES - NARROW * i, 1) if i else layer
                    total = part if total is None else total + part
                rows.append(total)
        return stack(rows) if len(rows) > 1 else rows[0]

    def send(self, payload, groups, packed):
        copies = self.copies
        rows = payload.shape[0] // (self.patches * copies)
        for f in range(4):
            to, at = self.partner(self.me, f) * copies, 0
            for group in groups:
                high = group[f].shape[0]
                for s in range(copies):
                    payload[pl.ds((to + s) * rows + at, high), :] = group[f]
                at += high
        for to in range(self.patches * copies):
            payload[to * rows + at : (to + 1) * rows, :] = packed

    def take(self, recv, patch, lo, count):
        rows = recv.shape[0] // (self.patches * self.copies)
        out = None
        for s in range(self.copies):
            part = recv[pl.ds((patch * self.copies + s) * rows + lo, count), :]
            out = part if out is None else out + part
        return out

    def received(self, recv, count, at=0):
        rows = count * self.depth
        return self.oriented(
            [self.take(recv, self.partner(self.me, f), at, rows) for f in range(4)], count
        )

    def oriented(self, raw, count):
        depth = self.depth
        rows = count * depth
        turned = dot(stack(raw), self.reverse)
        out = []
        for f in range(4):
            flipped = self.flip(self.me, f) == 1
            out.append(jnp.where(flipped, turned[f * rows : (f + 1) * rows], raw[f]))
        return [[out[f][i * depth : (i + 1) * depth] for f in range(4)] for i in range(count)]

    def corner(self, face, side):
        q, f1 = self.partner(self.me, face), self.face_id(self.me, face)
        eq = side ^ self.flip(self.me, face)
        s1 = f1 & 1
        upright = f1 < 2
        f2 = jnp.where(upright, 2 + eq, eq)
        kq = jnp.where(upright, 2 * s1 + eq, 2 * eq + s1)
        tq = jnp.where(upright, 4, 2)
        r, g = self.partner(q, f2), self.face_id(q, f2)
        s2 = s1 ^ self.flip(q, f2)
        flat = g < 2
        k = jnp.where(flat, 2 * (g & 1) + s2, 2 * s2 + (g & 1))
        t = jnp.where(flat, 2, 4)
        g2 = jnp.where(flat, 2 + s2, s2)
        r2, h = self.partner(r, g2), self.face_id(r, g2)
        s4 = (g & 1) ^ self.flip(r, g2)
        k2 = jnp.where(h < 2, 2 * (h & 1) + s4, 2 * s4 + (h & 1))
        return (q, kq, tq), (r, k, t), (r2, k2)

    def corners(self):
        return [[self.corner(f, s) for s in range(2)] for f in range(4)]

    def look(self, recv, at, patch, lane, side, width):
        count = width // NARROW
        shift = (side * (LANES - 1) + LANES - lane) & (LANES - 1)
        packed = self.take(recv, patch, at, self.depth // 8 * count)
        odd = (lax.broadcasted_iota(jnp.int32, (8, LANES), 0) & 1) == 1
        out = []
        for k in range(0, self.depth // 8 * count, count):
            spread = jnp.broadcast_to(packed[k : k + 1], (8, LANES))
            if count == 2:
                spread = jnp.where(odd, packed[k + 1 : k + 2], spread)
            out.append(pltpu.roll(spread, 0, 1, stride=NARROW, stride_axis=0))
        return pltpu.roll(stack(out) if len(out) > 1 else out[0], shift, 1)

    def ends(self, low, high):
        return jnp.where(self.first, low, jnp.where(self.last, high, 0.0))

    def other_stiff(self, recv, at, mine, theirs, inner, corners, kinds, width):
        out = []
        edge = self.first | self.last
        for f in range(4):
            across = []
            for s in range(2):
                r, k, t = corners[f][s][1]
                across.append(self.look(recv, at, r, kinds * k, s, width))
            value = inner[f] + PENALTY * (theirs[f] - mine[f])
            far = PENALTY * (theirs[f] - self.ends(*across))
            out.append(value + jnp.where(edge, far, 0.0))
        return out


def stack(values):
    return jnp.concatenate(values, 0)


def unstack(value, depth):
    return [value[f * depth : (f + 1) * depth] for f in range(4)]


def cubic(x, s):
    return x * x * x - x + GRADIENT_ENERGY * s


def start_kernel(sizes, own, payload, *refs):
    body = Body(sizes, refs, sizes[2])
    rows = own.shape[0]
    layer = lax.broadcasted_iota(jnp.int32, (body.depth, LANES), 0)
    low = lax.axis_index("sec") * rows
    here = (layer >= low) & (layer < low + rows)

    def place(value):
        return jnp.where(here, stack([value] * body.slabs), 0.0)

    strips = body.strips(own)
    trace = [s[0] for s in strips]
    inner = body.slab(
        [place(body.depth_sum(s, STIFF_BAND)) for s in strips],
        [place(body.depth_sum(s, MASS_BAND)) for s in strips],
    )
    table = body.corner_table([place(a) for a in trace])
    body.send(payload, [trace, inner], body.pack(table, NARROW))


def flux_tail(body, mine, other, r0, tr, tv, payload, potential):
    jump = body.jumps(mine, other)
    body.stand(jump)

    def residual(z, stiff, mass):
        r0[z] = -TIME_STEP * (stiff + body.column(z))

    body.stiff0(lambda z: potential[z], residual)
    body.add_rows(r0, jump, -TIME_STEP)
    strips = body.strips(r0)
    trace = [s[0] for s in strips]
    inner = body.slab(body.depth_sums(strips, STIFF_BAND), body.depth_sums(strips, MASS_BAND))
    tr[...], tv[...] = stack(trace), stack(inner)
    body.copies = 1
    body.send(payload, [trace, inner], body.pack(body.corner_table(trace), NARROW))


def image_kernel(sizes, field, v, m, *refs):
    body = Body(sizes, refs)

    def image(z, stiff, mass):
        v[z] = stiff
        m[z] = mass

    body.stiff0(lambda z: field[z], image)


def middle_kernel(sizes, *refs):
    slabs, refs = refs[: sizes[2]], refs[sizes[2] :]
    c, v0, tc, tv = refs[:4]
    body = Body(sizes, refs[4:])
    count = body.slabs
    rows = body.depth // count
    for k, slab in enumerate(slabs):
        c[pl.ds(lax.rem(lax.axis_index("sec") + k, count) * rows, rows)] = slab[...]

    def image(z, stiff, mass):
        v0[z] = stiff

    body.stiff0(lambda z: c[z], image)
    tc[...], tv[...] = stack(body.traces(c)), stack(body.traces(v0))


def first_kernel(sizes, c, v0, tc, tv0, recv, sc, r0, ts, tr, tv, sides, payload,
                 potential, *refs):
    body = Body(sizes, refs, sizes[2])
    depth, count = body.depth, body.slabs
    rows = depth // count
    high = recv.shape[0] // (body.patches * count)
    raw = []
    for f in range(4):
        q = body.partner(body.me, f)
        parts = [recv[pl.ds((q * count + s) * high, rows), :] for s in range(count)]
        raw.append(stack(parts + [body.take(recv, q, rows, depth)]))
    other, inner = body.oriented(raw, 2)
    mine = unstack(tc, depth)
    jump = body.jumps(mine, other)
    body.stand(jump)
    for z in range(depth):
        sc[z] = v0[z] + body.column(z)
    body.add_rows(sc, jump, 1.0)
    for z in range(depth):
        potential[z] = cubic(c[z], sc[z])
    mine_s = body.stiff_trace(unstack(tv0, depth), jump)
    other_s = body.other_stiff(recv, rows + depth, mine, other, inner, body.corners(), 1, NARROW)
    ts[...] = stack(mine_s)
    sides[0], sides[1] = stack(other), stack(other_s)
    mine_p = [cubic(x, s) for x, s in zip(mine, mine_s)]
    other_p = [cubic(x, s) for x, s in zip(other, other_s)]
    flux_tail(body, mine_p, other_p, r0, tr, tv, payload, potential)


def second_kernel(sizes, r0, v1, m1, tr, tv, recv, u1, y, ty, tv2, tu, sides, payload,
                  *refs):
    body = Body(sizes, refs)
    depth = body.depth
    other, inner = body.received(recv, 2)
    mine = unstack(tr, depth)
    jump = body.jumps(mine, other)
    body.stand(jump)
    for z in range(depth):
        u1[z] = v1[z] + body.column(z)
    body.add_rows(u1, jump, 1.0)
    mine_s = body.stiff_trace(unstack(tv, depth), jump)
    other_s = body.other_stiff(
        recv, 2 * depth, mine, other, inner, body.corners(), 1, NARROW
    )
    tu[...] = stack(mine_s)
    sides[0], sides[1] = stack(other), stack(other_s)
    jump = body.jumps(mine_s, other_s)
    body.stand(jump)

    def image(z, stiff, mass):
        y[z] = m1[z] + TWICE * u1[z] + HALF * (stiff + body.column(z))

    body.stiff0(lambda z: u1[z], image)
    body.add_rows(y, jump, HALF)
    sums = [[], [], []]
    for z in range(depth):
        a, b = r0[z], y[z]
        for i, product in enumerate((a * a, a * b, b * b)):
            sums[i].append(jnp.sum(product, axis=0, keepdims=True))
    strips = body.strips(y, 7)
    trace = [s[0] for s in strips]
    masses = body.depth_sums(strips, MASS_BAND)
    kk, km, mk, mm = [body.depth_sums(strips, band) for band in face_weights()]
    inner, ahead, across = body.slabs_of(
        [(body.depth_sums(strips, STIFF_BAND), masses), (kk, km), (mk, mm)]
    )
    ty[...], tv2[...] = stack(trace), stack(inner)
    mixed = body.slab([HALF * a for a in ahead], [HALF * a for a in across], masses)
    outer = [TWICE * a + b for a, b in zip(inner, mixed)]
    table = body.corner_table(trace, inner)
    for i in range(3):
        total = jnp.sum(stack(sums[i]), axis=1, keepdims=True)
        table = jnp.where(body.lane == SUMS + i, total, table)
    body.send(payload, [trace, inner, outer], body.pack(table, BROAD))


def third_kernel(sizes, last, r0, y, v2, m2, ty, tv2, recv, *refs):
    if last:
        t, base, payload, u2, zf, mt = refs[:6]
        body = Body(sizes, refs[6:])
    else:
        t, base, u2, zf, tt, tu2, tz, sides, payload, mt = refs[:10]
        body = Body(sizes, refs[10:])
    depth, patches = body.depth, body.patches
    at = 3 * depth
    packed = depth * BROAD // LANES
    known = recv[at : at + packed, :]
    for p in range(1, patches):
        known = known + recv[p * (at + packed) + at : (p + 1) * (at + packed), :]
    odd = lax.broadcasted_iota(jnp.int32, (packed, LANES), 0) & 1
    slot = lax.broadcasted_iota(jnp.int32, (packed, LANES), 1) + NARROW * odd
    slot = slot & (BROAD - 1)
    m0, m1, m2s = [
        jnp.sum(jnp.where(slot == SUMS + i, known, 0.0), keepdims=True) for i in range(3)
    ]
    a0 = m0 / m1
    other, inner, outer = body.received(recv, 3)
    corners = body.corners()
    mine = unstack(ty, depth)
    jump = body.jumps(mine, other)
    body.stand(jump)
    for z in range(depth):
        u2[z] = v2[z] + body.column(z)
    body.add_rows(u2, jump, 1.0)
    mine_s = body.stiff_trace(unstack(tv2, depth), jump)
    other_s = body.other_stiff(recv, at, mine, other, inner, corners, KINDS, BROAD)
    masses, stiffs, far = [], [], []
    for f in range(4):
        arm_m, arm_k, across = [], [], []
        for s in range(2):
            (q, kq, tq), (r, k, kind), (r2, k2) = corners[f][s]
            look = functools.partial(body.look, recv, at, side=s, width=BROAD)
            arm_m.append(look(q, KINDS * kq + tq) - look(r, KINDS * k + kind))
            arm_k.append(look(q, KINDS * kq + tq + 1) - look(r, KINDS * k + kind + 1))
            value = look(r, KINDS * k)
            across.append(
                look(r, KINDS * k + 1)
                + PENALTY * (value - other[f])
                + PENALTY * (value - look(r2, KINDS * k2))
            )
        theirs = PENALTY * (other[f] - mine[f])
        masses.append(MASS_BAND[0] * theirs + PENALTY * body.ends(*arm_m))
        stiffs.append(STIFF_BAND[0] * theirs + PENALTY * body.ends(*arm_k))
        far.append(body.ends(*across))
    pushed = body.slab(stiffs, masses)
    edge = body.first | body.last
    other_t = []
    for f in range(4):
        again = pushed[f] + PENALTY * (other_s[f] - mine_s[f])
        again = again + jnp.where(edge, PENALTY * (other_s[f] - far[f]), 0.0)
        image = outer[f] + TWICE * (other_s[f] - inner[f]) + HALF * again
        other_t.append(other[f] - a0 * image)
    jump = body.jumps(mine_s, other_s)
    body.stand(jump)

    def turn(z, stiff, mass):
        t[z] = y[z] - a0 * (m2[z] + TWICE * u2[z] + HALF * (stiff + body.column(z)))

    body.stiff0(lambda z: u2[z], turn)
    body.add_rows(t, jump, -HALF * a0)
    mine_t = body.traces(t)
    jump = body.jumps(mine_t, other_t)
    body.stand(jump)

    def image(z, stiff, mass):
        zf[z] = stiff + body.column(z)
        mt[z] = mass

    body.stiff0(lambda z: t[z], image)
    body.add_rows(zf, jump, 1.0)
    sums = [jnp.zeros((8, LANES), jnp.float32)] * 6
    for z in range(depth):
        b, x, s = y[z], t[z], zf[z]
        a = r0[z] - a0 * b
        energy = x * (mt[z] + TWICE * s) + HALF * (s * s)
        for i, product in enumerate((a * a, a * x, a * b, x * x, x * b, energy)):
            sums[i] = sums[i] + jnp.sum(product.reshape(LANES // 8, 8, LANES), axis=0)
    moments = jnp.zeros((1, LANES), jnp.float32)
    lane = lax.broadcasted_iota(jnp.int32, (1, LANES), 1)
    for i, value in enumerate(sums):
        value = jnp.sum(jnp.sum(value, axis=0, keepdims=True), axis=1, keepdims=True)
        moments = jnp.where(lane == i, value, moments)
    for i, value in enumerate((a0, m0, m1, m2s)):
        base[i : i + 1, :] = jnp.broadcast_to(value, (1, LANES))
    rows = payload.shape[0] // patches
    for to in range(patches):
        payload[to * rows : to * rows + 1, :] = moments
    if not last:
        trace = body.traces(zf)
        tt[...], tu2[...], tz[...] = stack(mine_t), stack(mine_s), stack(trace)
        sides[0], sides[1], sides[2] = stack(other), stack(other_s), stack(other_t)
        for f in range(4):
            payload[pl.ds(body.partner(body.me, f) * rows + 1, depth), :] = trace[f]


def weights(patches, base, recv):
    rows = recv.shape[0] // patches
    total = recv[:1, :]
    for p in range(1, patches):
        total = total + recv[p * rows : p * rows + 1, :]
    a0, m0, m1, m2 = [base[i : i + 1, :1] for i in range(4)]
    rr1, g1, g2, tt, ty, tat = [total[:, i : i + 1] for i in range(6)]
    b0 = rr1 / m0
    a1 = rr1 / (g1 + 2.0 * b0 * g2 + b0 * b0 * m1)
    rr2 = rr1 - 2.0 * a1 * (g1 + b0 * g2) + a1 * a1 * (tt + 2.0 * b0 * ty + b0 * b0 * m2)
    b1 = rr2 / rr1
    shift = a1 * b0 / a0
    c1, c0, c2 = 1.0 + b1 + shift, b1 * b0 - shift, -a1
    a2 = rr2 / (
        c1 * c1 * g1
        + c0 * c0 * m1
        + c2 * c2 * tat
        + 2.0 * (c1 * c0 * g2 + c1 * c2 * tt + c0 * c2 * ty)
    )
    return a0 + a1 * (1.0 + b0) + a2 * (c1 + c0), -a0 * (a1 + a2 * c1), a2 * c2


def next_kernel(sizes, c, r0, y, t, sc, u1, u2, zf, tc, ts, tr, tu, ty, tu2, tt, tz,
                side_c, side_r, side_y, base, recv,
                cn, rn, trn, tvn, payload, potential, *refs):
    body = Body(sizes, refs)
    depth = body.depth
    x = weights(body.patches, base, recv)

    def mix(*values):
        return values[0] + x[0] * values[1] + x[1] * values[2] + x[2] * values[3]

    for z in range(depth):
        cn[z] = mix(c[z], r0[z], y[z], t[z])
        potential[z] = cubic(cn[z], mix(sc[z], u1[z], u2[z], zf[z]))
    (side_z,) = body.received(recv, 1, 1)
    mine = cubic(
        mix(tc[...], tr[...], ty[...], tt[...]), mix(ts[...], tu[...], tu2[...], tz[...])
    )
    other = cubic(
        mix(side_c[0], side_r[0], side_y[0], side_y[2]),
        mix(side_c[1], side_r[1], side_y[1], stack(side_z)),
    )
    flux_tail(body, unstack(mine, depth), unstack(other, depth), rn, trn, tvn, payload, potential)


def last_kernel(patches, c, r0, y, t, base, recv, out):
    x0, x1, x2 = weights(patches, base, recv)
    rows = out.shape[0]
    low = lax.axis_index("sec") * rows
    for z in range(rows):
        k = low + z
        out[z] = c[k] + x0 * r0[k] + x1 * y[k] + x2 * t[k]


def shards(patches, slabs, concentration, partner, face_id, flip):
    own = concentration[0]
    rows = own.shape[0]
    depth = rows * slabs
    halves = [own]
    for k in range(1, slabs):
        halves.append(lax.ppermute(own, "sec", [((i + k) % slabs, i) for i in range(slabs)]))
    matrices = [jnp.asarray(x) for x in constants()]
    tables = [partner.T, face_id.T, flip.T]
    vmem, smem = pl.BlockSpec(memory_space=pltpu.VMEM), pl.BlockSpec(memory_space=pltpu.SMEM)
    params = pltpu.CompilerParams(vmem_limit_bytes=(4 + depth) << 20)

    def shape(*dims):
        return jax.ShapeDtypeStruct(dims, jnp.float32)

    field, trace, base = shape(depth, LANES, LANES), shape(4 * depth, LANES), shape(8, LANES)

    def sides(count):
        return shape(count, 4 * depth, LANES)

    def load(count):
        return shape(patches * count, LANES)

    def call(kernel, outs, *args, fields=0, consts=matrices, cost=None):
        count, head = len(args), 3 + len(consts)
        inside = [pltpu.VMEM((depth, LANES, LANES), jnp.float32)] * fields
        shared = [
            pltpu.VMEM((4, LANES + 2 * PAD, LANES), jnp.float32),
            pltpu.VMEM((LANES, LANES), jnp.float32),
            pltpu.VMEM((LANES, LANES), jnp.float32),
            pltpu.VMEM((-(-depth // 8), LANES, LANES), jnp.float32),
        ]

        def run(*refs):
            common, rest = refs[:head], refs[head:]
            cut = len(rest) - len(shared)
            kernel((depth, patches, slabs), *rest[:cut], *common, *rest[cut:])

        return pl.pallas_call(
            run,
            out_shape=outs,
            in_specs=[smem] * 3 + [vmem] * (len(consts) + count),
            out_specs=[vmem] * len(outs),
            scratch_shapes=inside + shared,
            compiler_params=params,
            cost_estimate=cost,
            name=kernel.__name__ if hasattr(kernel, "__name__") else "third_kernel",
        )(*tables, *consts, *args)

    def swap(payload, axes="patch", parts=patches):
        rows = payload.shape[0] // parts
        moved = lax.all_to_all(payload.reshape(parts, 1, rows * LANES), axes, 0, 0)
        return moved.reshape(parts * rows, LANES)

    cost = pl.CostEstimate(flops=COST, bytes_accessed=4 * own.size, transcendentals=0)
    narrow, broad = depth * NARROW // LANES, depth * BROAD // LANES
    (payload,) = call(
        start_kernel,
        [load(slabs * (rows + depth + narrow))],
        own,
        consts=[],
        cost=cost,
    )
    c, v0, tc, tv0 = call(
        middle_kernel,
        [field, field, trace, trace],
        *halves,
        cost=cost,
    )
    sc, r0, ts, tr, tv, side_c, payload = call(
        first_kernel,
        [field] * 2 + [trace] * 3 + [sides(2), load(2 * depth + narrow)],
        c, v0, tc, tv0, swap(payload, ("patch", "sec"), patches * slabs),
        fields=1,
    )
    for step in range(STEPS):
        v1, m1 = call(image_kernel, [field] * 2, r0, cost=cost)
        u1, y, ty, tv2, tu, side_r, payload = call(
            second_kernel,
            [field] * 2 + [trace] * 3 + [sides(2), load(3 * depth + broad)],
            r0, v1, m1, tr, tv, swap(payload),
        )
        v2, m2 = call(image_kernel, [field] * 2, y, cost=cost)
        last = step + 1 == STEPS
        outs = [field, base]
        if last:
            outs += [load(1)]
        else:
            outs += [field] * 2 + [trace] * 3 + [sides(3), load(1 + depth)]
        t, base_now, *rest = call(
            lambda sizes, *refs, last=last: third_kernel(sizes, last, *refs),
            outs,
            r0, y, v2, m2, ty, tv2, swap(payload),
            fields=3 if last else 1,
        )
        if last:
            (payload,) = rest
            break
        u2, zf, tt, tu2, tz, side_y, payload = rest
        c, r0, tr, tv, payload = call(
            next_kernel,
            [field] * 2 + [trace] * 2 + [load(2 * depth + narrow)],
            c, r0, y, t, sc, u1, u2, zf, tc, ts, tr, tu, ty, tu2, tt, tz,
            side_c, side_r, side_y, base_now, swap(payload),
            fields=1,
        )
    out = pl.pallas_call(
        functools.partial(last_kernel, patches),
        out_shape=shape(rows, LANES, LANES),
        in_specs=[vmem] * 6,
        out_specs=vmem,
        compiler_params=params,
    )(c, r0, y, t, base_now, swap(payload))
    return out[None]


def solution(mesh):
    placed = (P("patch", "sec", None, None), P(), P(), P())
    return jax.shard_map(
        functools.partial(shards, mesh.shape["patch"], mesh.shape["sec"]),
        mesh=mesh,
        in_specs=placed,
        out_specs=P("patch", "sec", None, None),
        check_vma=False,
    )
```

```python
import functools

import jax
import jax.numpy as jnp
import numpy as np
from jax import lax
from jax.experimental import pallas as pl
from jax.experimental.pallas import tpu as pltpu
from jax.sharding import PartitionSpec as P

STEPS = 2
MASS_BAND = (2416.0 / 5040.0, 1191.0 / 5040.0, 120.0 / 5040.0, 1.0 / 5040.0)
STIFF_BAND = (2.0 / 3.0, -0.125, -0.2, -1.0 / 120.0)
SCALE = 5040.0
MASS_HIGH, MASS_LOW = (2416.0, 1192.0, 120.0, 1.0), (0.0, -1.0, 0.0, 0.0)
STIFF_HIGH, STIFF_LOW = (3360.0, -632.0, -1008.0, -42.0), (0.0, 2.0, 0.0, 0.0)
PENALTY = 2.0
TIME_STEP = 1.0
STABILIZER = 2.0
GRADIENT_ENERGY = 0.5
HALF = TIME_STEP * GRADIENT_ENERGY
TWICE = TIME_STEP * STABILIZER
EXACT = lax.Precision.HIGHEST
LANES = 128
PAD = 8
KINDS = 6
SUMS = 4 * KINDS
NARROW, BROAD = 16, 32
COST = 1 << 34


def band_matrix(band, size):
    out = np.zeros((size, size), np.float32)
    for offset, value in enumerate(band):
        for row in range(size - offset):
            out[row, row + offset] = value
            out[row + offset, row] = value
    return out


def dot(left, right):
    return jnp.dot(left, right, precision=EXACT, preferred_element_type=jnp.float32)


def right_matrix(mass_band, stiff_band):
    mass, stiff = band_matrix(mass_band, LANES), band_matrix(stiff_band, LANES)
    return np.block([[mass, stiff], [np.zeros_like(mass), mass]])


def constants():
    high = right_matrix(MASS_HIGH, STIFF_HIGH).astype(jnp.bfloat16)
    low = right_matrix(MASS_LOW, STIFF_LOW).astype(jnp.bfloat16)
    return (np.concatenate([high, high, high, low, low]),)


def banded(distance, band, inside=None):
    out = jnp.zeros(distance.shape, jnp.float32)
    for offset, value in enumerate(band):
        hit = distance == offset
        out = jnp.where(hit if inside is None else hit & inside, value, out)
    return out


class Body:
    def __init__(self, sizes, refs, copies=1):
        self.depth, self.patches, self.slabs = sizes
        self.copies = copies
        self.tables, refs = refs[:3], refs[3:]
        self.near, self.strip, self.turned, self.stood = refs[-4:]
        if len(refs) > 4:
            self.pieces = refs[0]
        self.me = lax.axis_index("patch")
        self.lane = lax.broadcasted_iota(jnp.int32, (self.depth, LANES), 1)
        self.first, self.last = self.lane == 0, self.lane == LANES - 1
        self.wide = lax.broadcasted_iota(jnp.int32, (LANES, LANES), 1)
        self.edge = (self.wide == 0) | (self.wide == LANES - 1)
        row = lax.broadcasted_iota(jnp.int32, (LANES, LANES), 0)
        self.reverse = jnp.where(row + self.wide == LANES - 1, 1.0, 0.0)
        distance = jnp.abs(row - self.wide)
        self.plain = jnp.concatenate(
            [banded(distance, MASS_BAND), banded(distance, STIFF_BAND)], axis=1
        )

    def partner(self, patch, face):
        return self.tables[0][face, patch]

    def face_id(self, patch, face):
        return self.tables[1][face, patch]

    def flip(self, patch, face):
        return self.tables[2][face, patch]

    def split(self, value):
        pieces = []
        for last in (False, False, True):
            piece = value.astype(jnp.bfloat16)
            pieces.append(piece)
            if not last:
                value = value - piece.astype(jnp.float32)
        return pieces

    def stiff0(self, layer, finish):
        depth = self.depth
        zeros = jnp.zeros((PAD, LANES), jnp.float32)
        for i in range(4):
            self.near[i, :PAD] = zeros
            self.near[i, PAD + LANES :] = zeros
        for z in range(depth):
            middle = layer(z)
            massed = (MASS_BAND[0] / SCALE) * middle
            stiffed = (STIFF_BAND[0] / SCALE) * middle
            for offset in (1, 2, 3):
                near = [layer(k) for k in (z - offset, z + offset) if 0 <= k < depth]
                if near:
                    both = near[0] if len(near) == 1 else near[0] + near[1]
                    massed = massed + (MASS_BAND[offset] / SCALE) * both
                    stiffed = stiffed + (STIFF_BAND[offset] / SCALE) * both
            pieces = self.split(jnp.concatenate([massed, stiffed], axis=1))
            pieces = jnp.concatenate(pieces + pieces[:2], axis=1)
            mixed = jnp.dot(pieces, self.pieces[...], preferred_element_type=jnp.float32)
            a, b = 2 * (z % 2), 2 * (z % 2) + 1
            self.near[a, PAD : PAD + LANES] = mixed[:, :LANES]
            self.near[b, PAD : PAD + LANES] = mixed[:, LANES:]
            stiff = STIFF_BAND[0] * mixed[:, :LANES] + MASS_BAND[0] * mixed[:, LANES:]
            mass = MASS_BAND[0] * mixed[:, :LANES]
            for o in (1, 2, 3):
                low, high = slice(PAD - o, PAD - o + LANES), slice(PAD + o, PAD + o + LANES)
                both = self.near[a, low] + self.near[a, high]
                stiff = stiff + STIFF_BAND[o] * both
                stiff = stiff + MASS_BAND[o] * (self.near[b, low] + self.near[b, high])
                mass = mass + MASS_BAND[o] * both
            finish(z, stiff, mass)

    def strips(self, field, slot=None, count=4):
        depth = field.shape[0]
        group = min(depth, 8)
        if slot is None:
            slot = 0
            for z in range(depth):
                rolled = pltpu.roll(field[z], (8 * (z % 8) + 4) % LANES, 1)
                pltpu.store(self.strip.at[slot, z // 8], rolled, mask=(self.wide >> 3) == z % 8)
        rows0 = [field[:, d, :] for d in range(count)]
        rows1 = [field[:, LANES - 1 - d, :] for d in range(count)]
        wanted = list(range(4 - count, 4 + count))
        pieces = {i: [] for i in wanted}
        for start in range(0, depth, group):
            self.turned[...] = jnp.transpose(self.strip[slot, start // 8])
            for i in wanted:
                pieces[i].append(self.turned[pl.ds(i, group, stride=8), :])
        columns = {i: jnp.concatenate(p, axis=0) if len(p) > 1 else p[0] for i, p in pieces.items()}
        return [
            rows0,
            rows1,
            [columns[4 + d] for d in range(count)],
            [columns[3 - d] for d in range(count)],
        ]

    def traces(self, field, slot=None):
        return [strip[0] for strip in self.strips(field, slot, 1)]

    def jumps(self, mine, other):
        return [PENALTY * (a - b) for a, b in zip(mine, other)]

    def stand(self, jump, slot=0):
        for start in range(0, self.depth, 8):
            self.turned[pl.ds(0, 8, stride=2), :] = jump[3][start : start + 8]
            self.turned[pl.ds(1, 8, stride=2), :] = jump[2][start : start + 8]
            self.stood[slot, start // 8] = jnp.transpose(self.turned[...])

    def column(self, z, slot=0):
        rolled = pltpu.roll(self.stood[slot, z // 8], (LANES - 2 * (z % 8) - 1) % LANES, 1)
        return jnp.where(self.edge, rolled, 0.0)

    def emit(self, field, z, value, jump=None, factor=1.0, slot=None):
        field[z] = value
        if jump is not None:
            field[z, :1, :] = field[z, :1, :] + factor * jump[0][z : z + 1]
            at = LANES - 1
            field[z, at:, :] = field[z, at:, :] + factor * jump[1][z : z + 1]
        if slot is not None:
            rolled = pltpu.roll(field[z], (8 * (z % 8) + 4) % LANES, 1)
            mask = (self.wide >> 3) == z % 8
            pltpu.store(self.strip.at[slot, z // 8], rolled, mask=mask)

    def lazy(self, field, make):
        made = set()

        def layer(z):
            if z not in made:
                made.add(z)
                make(z)
            return field[z]

        return layer

    def stiff_trace(self, inner, jump):
        out = []
        for f in range(4):
            side = f & 1
            low, high = (2, 3) if f < 2 else (0, 1)
            at = side * (LANES - 1)
            ends = []
            for face, end in ((low, 0), (high, LANES - 1)):
                shift = (end - at) % LANES
                ends.append(pltpu.roll(jump[face], shift, 1) if shift else jump[face])
            out.append(inner[f] + jump[f] + self.ends(*ends))
        return out

    def third_axis(self, value, band):
        layer = lax.broadcasted_iota(jnp.int32, value.shape, 0)
        out = band[0] * value
        for o in (1, 2, 3):
            low = jnp.where(layer >= o, pltpu.roll(value, o, 0), 0.0)
            high = jnp.where(layer < self.depth - o, pltpu.roll(value, self.depth - o, 0), 0.0)
            out = out + band[o] * (low + high)
        return out

    def slab(self, stiffs, masses, plain=None, arms=None):
        n = 4 * self.depth
        rows = [stack(x) for x in (masses, stiffs, plain, arms) if x is not None]
        both = dot(stack(rows), self.plain)
        lower = both[n : 2 * n, :LANES] + both[:n, LANES:]
        if plain is not None:
            lower = lower + both[2 * n : 3 * n, :LANES]
        out = [
            self.third_axis(a, MASS_BAND) + self.third_axis(b, STIFF_BAND)
            for a, b in zip(unstack(lower, self.depth), unstack(both[:n, :LANES], self.depth))
        ]
        return out if arms is None else (out, both[3 * n :])

    def depth_sum(self, strip, band):
        out = band[0] * strip[0]
        for d in (1, 2, 3):
            out = out + band[d] * strip[d]
        return out

    def corner_table(self, trace, inner=None, arms=None):
        table = jnp.zeros((self.depth, LANES), jnp.float32)
        ends = (0, LANES - 1)
        kinds = 1 if inner is None else KINDS
        for rs in range(2):
            for cs in range(2):
                slot = kinds * (2 * rs + cs)
                values = [(trace[rs], ends[cs])]
                if inner is not None:
                    values.append((inner[rs], ends[cs]))
                    for face, end in ((rs, ends[cs]), (2 + cs, ends[rs])):
                        part = arms[face * self.depth : (face + 1) * self.depth]
                        values.append((part[:, :LANES], end))
                        values.append((part[:, LANES:], end))
                for kind, (value, end) in enumerate(values):
                    shift = (slot + kind - end) % LANES
                    rolled = pltpu.roll(value, shift, 1) if shift else value
                    table = jnp.where(self.lane == slot + kind, rolled, table)
        return table

    def pack(self, table, width):
        count = width // NARROW
        rows = []
        for start in range(0, self.depth, 8):
            for low in range(count):
                total = None
                for i in range(low, 8, count):
                    layer = table[start + i : start + i + 1]
                    part = pltpu.roll(layer, LANES - NARROW * i, 1) if i else layer
                    total = part if total is None else total + part
                rows.append(total)
        return stack(rows) if len(rows) > 1 else rows[0]

    def send(self, payload, groups, packed):
        copies = self.copies
        rows = payload.shape[0] // (self.patches * copies)
        for f in range(4):
            to, at = self.partner(self.me, f) * copies, 0
            for group in groups:
                high = group[f].shape[0]
                for s in range(copies):
                    payload[pl.ds((to + s) * rows + at, high), :] = group[f]
                at += high
        for to in range(self.patches * copies):
            payload[to * rows + at : (to + 1) * rows, :] = packed

    def take(self, recv, patch, lo, count):
        rows = recv.shape[0] // (self.patches * self.copies)
        out = None
        for s in range(self.copies):
            part = recv[pl.ds((patch * self.copies + s) * rows + lo, count), :]
            out = part if out is None else out + part
        return out

    def received(self, recv, count, at=0):
        rows = count * self.depth
        return self.oriented(
            [self.take(recv, self.partner(self.me, f), at, rows) for f in range(4)], count
        )

    def oriented(self, raw, count):
        depth = self.depth
        rows = count * depth
        turned = dot(stack(raw), self.reverse)
        out = []
        for f in range(4):
            flipped = self.flip(self.me, f) == 1
            out.append(jnp.where(flipped, turned[f * rows : (f + 1) * rows], raw[f]))
        return [[out[f][i * depth : (i + 1) * depth] for f in range(4)] for i in range(count)]

    def corner(self, face, side):
        q, f1 = self.partner(self.me, face), self.face_id(self.me, face)
        eq = side ^ self.flip(self.me, face)
        s1 = f1 & 1
        upright = f1 < 2
        f2 = jnp.where(upright, 2 + eq, eq)
        kq = jnp.where(upright, 2 * s1 + eq, 2 * eq + s1)
        tq = jnp.where(upright, 4, 2)
        r, g = self.partner(q, f2), self.face_id(q, f2)
        s2 = s1 ^ self.flip(q, f2)
        flat = g < 2
        k = jnp.where(flat, 2 * (g & 1) + s2, 2 * s2 + (g & 1))
        t = jnp.where(flat, 2, 4)
        g2 = jnp.where(flat, 2 + s2, s2)
        r2, h = self.partner(r, g2), self.face_id(r, g2)
        s4 = (g & 1) ^ self.flip(r, g2)
        k2 = jnp.where(h < 2, 2 * (h & 1) + s4, 2 * s4 + (h & 1))
        return (q, kq, tq), (r, k, t), (r2, k2)

    def corners(self):
        return [[self.corner(f, s) for s in range(2)] for f in range(4)]

    def look(self, recv, at, patch, lane, side, width):
        count = width // NARROW
        shift = (side * (LANES - 1) + LANES - lane) & (LANES - 1)
        packed = self.take(recv, patch, at, self.depth // 8 * count)
        odd = (lax.broadcasted_iota(jnp.int32, (8, LANES), 0) & 1) == 1
        out = []
        for k in range(0, self.depth // 8 * count, count):
            spread = jnp.broadcast_to(packed[k : k + 1], (8, LANES))
            if count == 2:
                spread = jnp.where(odd, packed[k + 1 : k + 2], spread)
            out.append(pltpu.roll(spread, 0, 1, stride=NARROW, stride_axis=0))
        return pltpu.roll(stack(out) if len(out) > 1 else out[0], shift, 1)

    def ends(self, low, high):
        return jnp.where(self.first, low, jnp.where(self.last, high, 0.0))

    def other_stiff(self, recv, at, mine, theirs, inner, corners, kinds, width):
        out = []
        edge = self.first | self.last
        for f in range(4):
            across = []
            for s in range(2):
                r, k, t = corners[f][s][1]
                across.append(self.look(recv, at, r, kinds * k, s, width))
            value = inner[f] + PENALTY * (theirs[f] - mine[f])
            far = PENALTY * (theirs[f] - self.ends(*across))
            out.append(value + jnp.where(edge, far, 0.0))
        return out


def stack(values):
    return jnp.concatenate(values, 0)


def unstack(value, depth):
    return [value[f * depth : (f + 1) * depth] for f in range(4)]


def cubic(x, s):
    return x * x * x - x + GRADIENT_ENERGY * s


def start_kernel(sizes, own, payload, *refs):
    body = Body(sizes, refs, sizes[2])
    rows = own.shape[0]
    layer = lax.broadcasted_iota(jnp.int32, (body.depth, LANES), 0)
    low = lax.axis_index("sec") * rows
    here = (layer >= low) & (layer < low + rows)

    def place(value):
        return jnp.where(here, stack([value] * body.slabs), 0.0)

    strips = body.strips(own)
    trace = [s[0] for s in strips]
    inner = body.slab(
        [place(body.depth_sum(s, STIFF_BAND)) for s in strips],
        [place(body.depth_sum(s, MASS_BAND)) for s in strips],
    )
    table = body.corner_table([place(a) for a in trace])
    body.send(payload, [trace, inner], body.pack(table, NARROW))


def flux_tail(body, layer, mine, other, r0, v1, m1, tr, tv, payload):
    jump = body.jumps(mine, other)
    body.stand(jump, 1)

    def residual(z, stiff, mass):
        body.emit(r0, z, -TIME_STEP * (stiff + body.column(z, 1)), jump, -TIME_STEP, 0)

    body.stiff0(layer, residual)

    def image(z, stiff, mass):
        body.emit(v1, z, stiff, slot=1)
        m1[z] = mass

    body.stiff0(lambda z: r0[z], image)
    trace, inner = body.traces(r0, 0), body.traces(v1, 1)
    tr[...], tv[...] = stack(trace), stack(inner)
    body.copies = 1
    body.send(payload, [trace, inner], body.pack(body.corner_table(trace), NARROW))


def middle_kernel(sizes, *refs):
    slabs, refs = refs[: sizes[2]], refs[sizes[2] :]
    c, v0, tc, tv = refs[:4]
    body = Body(sizes, refs[4:])
    count = body.slabs
    rows = body.depth // count
    for k, slab in enumerate(slabs):
        c[pl.ds(lax.rem(lax.axis_index("sec") + k, count) * rows, rows)] = slab[...]

    def image(z, stiff, mass):
        v0[z] = stiff

    body.stiff0(lambda z: c[z], image)
    tc[...], tv[...] = stack(body.traces(c)), stack(body.traces(v0))


def first_kernel(sizes, c, v0, tc, tv0, recv, sc, r0, v1, m1, ts, tr, tv, sides, payload,
                 potential, *refs):
    body = Body(sizes, refs, sizes[2])
    depth, count = body.depth, body.slabs
    rows = depth // count
    high = recv.shape[0] // (body.patches * count)
    raw = []
    for f in range(4):
        q = body.partner(body.me, f)
        parts = [recv[pl.ds((q * count + s) * high, rows), :] for s in range(count)]
        raw.append(stack(parts + [body.take(recv, q, rows, depth)]))
    other, inner = body.oriented(raw, 2)
    mine = unstack(tc, depth)
    jump = body.jumps(mine, other)
    body.stand(jump)

    def make(z):
        body.emit(sc, z, v0[z] + body.column(z), jump)
        potential[z] = cubic(c[z], sc[z])

    mine_s = body.stiff_trace(unstack(tv0, depth), jump)
    other_s = body.other_stiff(recv, rows + depth, mine, other, inner, body.corners(), 1, NARROW)
    ts[...] = stack(mine_s)
    sides[0], sides[1] = stack(other), stack(other_s)
    mine_p = [cubic(x, s) for x, s in zip(mine, mine_s)]
    other_p = [cubic(x, s) for x, s in zip(other, other_s)]
    layer = body.lazy(potential, make)
    flux_tail(body, layer, mine_p, other_p, r0, v1, m1, tr, tv, payload)


def second_kernel(sizes, r0, v1, m1, tr, tv, recv, u1, y, v2, m2, ty, tv2, tu, sides, payload,
                  *refs):
    body = Body(sizes, refs)
    depth = body.depth
    other, inner = body.received(recv, 2)
    mine = unstack(tr, depth)
    jump = body.jumps(mine, other)
    body.stand(jump)

    def make(z, jump=jump):
        body.emit(u1, z, v1[z] + body.column(z), jump)

    mine_s = body.stiff_trace(unstack(tv, depth), jump)
    other_s = body.other_stiff(
        recv, 2 * depth, mine, other, inner, body.corners(), 1, NARROW
    )
    tu[...] = stack(mine_s)
    sides[0], sides[1] = stack(other), stack(other_s)
    jump = body.jumps(mine_s, other_s)
    body.stand(jump, 1)

    def image(z, stiff, mass):
        value = m1[z] + TWICE * u1[z] + HALF * (stiff + body.column(z, 1))
        body.emit(y, z, value, jump, HALF, 0)

    body.stiff0(body.lazy(u1, make), image)
    sums = [[], [], []]

    def again(z, stiff, mass):
        body.emit(v2, z, stiff, slot=1)
        m2[z] = mass
        a, b = r0[z], y[z]
        for i, product in enumerate((a * a, a * b, b * b)):
            sums[i].append(jnp.sum(product, axis=0, keepdims=True))

    body.stiff0(lambda z: y[z], again)
    strips_y, strips = body.strips(y, 0), body.strips(v2, 1)
    trace, inner = [s[0] for s in strips_y], [s[0] for s in strips]
    ty[...], tv2[...] = stack(trace), stack(inner)
    mixed, arms = body.slab(
        [HALF * body.depth_sum(s, STIFF_BAND) for s in strips],
        [HALF * body.depth_sum(s, MASS_BAND) for s in strips],
        [body.depth_sum(s, MASS_BAND) for s in strips_y],
        trace,
    )
    outer = [TWICE * a + b for a, b in zip(inner, mixed)]
    table = body.corner_table(trace, inner, arms)
    for i in range(3):
        total = jnp.sum(stack(sums[i]), axis=1, keepdims=True)
        table = jnp.where(body.lane == SUMS + i, total, table)
    body.send(payload, [trace, inner, outer], body.pack(table, BROAD))


def third_kernel(sizes, last, r0, y, v2, m2, ty, tv2, recv, *refs):
    if last:
        t, base, payload, u2, zf = refs[:5]
        body = Body(sizes, refs[5:])
    else:
        t, base, u2, zf, tt, tu2, tz, sides, payload = refs[:9]
        body = Body(sizes, refs[9:])
    depth, patches = body.depth, body.patches
    at = 3 * depth
    packed = depth * BROAD // LANES
    known = recv[at : at + packed, :]
    for p in range(1, patches):
        known = known + recv[p * (at + packed) + at : (p + 1) * (at + packed), :]
    odd = lax.broadcasted_iota(jnp.int32, (packed, LANES), 0) & 1
    slot = lax.broadcasted_iota(jnp.int32, (packed, LANES), 1) + NARROW * odd
    slot = slot & (BROAD - 1)
    m0, m1, m2s = [
        jnp.sum(jnp.where(slot == SUMS + i, known, 0.0), keepdims=True) for i in range(3)
    ]
    a0 = m0 / m1
    other, inner, outer = body.received(recv, 3)
    corners = body.corners()
    mine = unstack(ty, depth)
    jump = body.jumps(mine, other)
    body.stand(jump)

    def make(z, jump=jump):
        body.emit(u2, z, v2[z] + body.column(z), jump)

    mine_s = body.stiff_trace(unstack(tv2, depth), jump)
    other_s = body.other_stiff(recv, at, mine, other, inner, corners, KINDS, BROAD)
    masses, stiffs, far = [], [], []
    for f in range(4):
        arm_m, arm_k, across = [], [], []
        for s in range(2):
            (q, kq, tq), (r, k, kind), (r2, k2) = corners[f][s]
            look = functools.partial(body.look, recv, at, side=s, width=BROAD)
            arm_m.append(look(q, KINDS * kq + tq) - look(r, KINDS * k + kind))
            arm_k.append(look(q, KINDS * kq + tq + 1) - look(r, KINDS * k + kind + 1))
            value = look(r, KINDS * k)
            across.append(
                look(r, KINDS * k + 1)
                + PENALTY * (value - other[f])
                + PENALTY * (value - look(r2, KINDS * k2))
            )
        theirs = PENALTY * (other[f] - mine[f])
        masses.append(MASS_BAND[0] * theirs + PENALTY * body.ends(*arm_m))
        stiffs.append(STIFF_BAND[0] * theirs + PENALTY * body.ends(*arm_k))
        far.append(body.ends(*across))
    pushed = body.slab(stiffs, masses)
    edge = body.first | body.last
    other_t = []
    for f in range(4):
        again = pushed[f] + PENALTY * (other_s[f] - mine_s[f])
        again = again + jnp.where(edge, PENALTY * (other_s[f] - far[f]), 0.0)
        image = outer[f] + TWICE * (other_s[f] - inner[f]) + HALF * again
        other_t.append(other[f] - a0 * image)
    jump_s = body.jumps(mine_s, other_s)
    body.stand(jump_s, 1)

    def turn(z, stiff, mass):
        image = m2[z] + TWICE * u2[z] + HALF * (stiff + body.column(z, 1))
        body.emit(t, z, y[z] - a0 * image, jump_s, -HALF * a0, 0)

    body.stiff0(body.lazy(u2, make), turn)
    mine_t = body.traces(t, 0)
    jump_t = body.jumps(mine_t, other_t)
    body.stand(jump_t)
    sums = [jnp.zeros((8, LANES), jnp.float32)] * 6

    def image(z, stiff, mass):
        body.emit(zf, z, stiff + body.column(z), jump_t, slot=None if last else 1)
        b, x, s = y[z], t[z], zf[z]
        a = r0[z] - a0 * b
        energy = x * (mass + TWICE * s) + HALF * (s * s)
        for i, product in enumerate((a * a, a * x, a * b, x * x, x * b, energy)):
            sums[i] = sums[i] + jnp.sum(product.reshape(LANES // 8, 8, LANES), axis=0)

    body.stiff0(lambda z: t[z], image)
    moments = jnp.zeros((1, LANES), jnp.float32)
    lane = lax.broadcasted_iota(jnp.int32, (1, LANES), 1)
    for i, value in enumerate(sums):
        value = jnp.sum(jnp.sum(value, axis=0, keepdims=True), axis=1, keepdims=True)
        moments = jnp.where(lane == i, value, moments)
    for i, value in enumerate((a0, m0, m1, m2s)):
        base[i : i + 1, :] = jnp.broadcast_to(value, (1, LANES))
    rows = payload.shape[0] // patches
    for to in range(patches):
        payload[to * rows : to * rows + 1, :] = moments
    if not last:
        trace = body.traces(zf, 1)
        tt[...], tu2[...], tz[...] = stack(mine_t), stack(mine_s), stack(trace)
        sides[0], sides[1], sides[2] = stack(other), stack(other_s), stack(other_t)
        for f in range(4):
            payload[pl.ds(body.partner(body.me, f) * rows + 1, depth), :] = trace[f]


def weights(patches, base, recv):
    rows = recv.shape[0] // patches
    total = recv[:1, :]
    for p in range(1, patches):
        total = total + recv[p * rows : p * rows + 1, :]
    a0, m0, m1, m2 = [base[i : i + 1, :1] for i in range(4)]
    rr1, g1, g2, tt, ty, tat = [total[:, i : i + 1] for i in range(6)]
    b0 = rr1 / m0
    a1 = rr1 / (g1 + 2.0 * b0 * g2 + b0 * b0 * m1)
    rr2 = rr1 - 2.0 * a1 * (g1 + b0 * g2) + a1 * a1 * (tt + 2.0 * b0 * ty + b0 * b0 * m2)
    b1 = rr2 / rr1
    shift = a1 * b0 / a0
    c1, c0, c2 = 1.0 + b1 + shift, b1 * b0 - shift, -a1
    a2 = rr2 / (
        c1 * c1 * g1
        + c0 * c0 * m1
        + c2 * c2 * tat
        + 2.0 * (c1 * c0 * g2 + c1 * c2 * tt + c0 * c2 * ty)
    )
    return a0 + a1 * (1.0 + b0) + a2 * (c1 + c0), -a0 * (a1 + a2 * c1), a2 * c2


def next_kernel(sizes, c, r0, y, t, sc, u1, u2, zf, tc, ts, tr, tu, ty, tu2, tt, tz,
                side_c, side_r, side_y, base, recv,
                cn, rn, v1, m1, trn, tvn, payload, potential, *refs):
    body = Body(sizes, refs)
    depth = body.depth
    x = weights(body.patches, base, recv)

    def mix(*values):
        return values[0] + x[0] * values[1] + x[1] * values[2] + x[2] * values[3]

    def make(z):
        cn[z] = mix(c[z], r0[z], y[z], t[z])
        potential[z] = cubic(cn[z], mix(sc[z], u1[z], u2[z], zf[z]))

    (side_z,) = body.received(recv, 1, 1)
    mine = cubic(
        mix(tc[...], tr[...], ty[...], tt[...]), mix(ts[...], tu[...], tu2[...], tz[...])
    )
    other = cubic(
        mix(side_c[0], side_r[0], side_y[0], side_y[2]),
        mix(side_c[1], side_r[1], side_y[1], stack(side_z)),
    )
    layer = body.lazy(potential, make)
    mine, other = unstack(mine, depth), unstack(other, depth)
    flux_tail(body, layer, mine, other, rn, v1, m1, trn, tvn, payload)


def last_kernel(patches, c, r0, y, t, base, recv, out):
    x0, x1, x2 = weights(patches, base, recv)
    rows = out.shape[0]
    low = lax.axis_index("sec") * rows
    for z in range(rows):
        k = low + z
        out[z] = c[k] + x0 * r0[k] + x1 * y[k] + x2 * t[k]


def shards(patches, slabs, concentration, partner, face_id, flip):
    own = concentration[0]
    rows = own.shape[0]
    depth = rows * slabs
    halves = [own]
    for k in range(1, slabs):
        halves.append(lax.ppermute(own, "sec", [((i + k) % slabs, i) for i in range(slabs)]))
    matrices = [jnp.asarray(x) for x in constants()]
    tables = [partner.T, face_id.T, flip.T]
    vmem, smem = pl.BlockSpec(memory_space=pltpu.VMEM), pl.BlockSpec(memory_space=pltpu.SMEM)
    params = pltpu.CompilerParams(vmem_limit_bytes=(4 + depth) << 20)

    def shape(*dims):
        return jax.ShapeDtypeStruct(dims, jnp.float32)

    field, trace, base = shape(depth, LANES, LANES), shape(4 * depth, LANES), shape(8, LANES)

    def sides(count):
        return shape(count, 4 * depth, LANES)

    def load(count):
        return shape(patches * count, LANES)

    def call(kernel, outs, *args, fields=0, consts=matrices, cost=None):
        count, head = len(args), 3 + len(consts)
        inside = [pltpu.VMEM((depth, LANES, LANES), jnp.float32)] * fields
        shared = [
            pltpu.VMEM((4, LANES + 2 * PAD, LANES), jnp.float32),
            pltpu.VMEM((2, -(-depth // 8), LANES, LANES), jnp.float32),
            pltpu.VMEM((LANES, LANES), jnp.float32),
            pltpu.VMEM((2, -(-depth // 8), LANES, LANES), jnp.float32),
        ]

        def run(*refs):
            common, rest = refs[:head], refs[head:]
            cut = len(rest) - len(shared)
            kernel((depth, patches, slabs), *rest[:cut], *common, *rest[cut:])

        return pl.pallas_call(
            run,
            out_shape=outs,
            in_specs=[smem] * 3 + [vmem] * (len(consts) + count),
            out_specs=[vmem] * len(outs),
            scratch_shapes=inside + shared,
            compiler_params=params,
            cost_estimate=cost,
            name=kernel.__name__ if hasattr(kernel, "__name__") else "third_kernel",
        )(*tables, *consts, *args)

    def swap(payload, axes="patch", parts=patches):
        rows = payload.shape[0] // parts
        moved = lax.all_to_all(payload.reshape(parts, 1, rows * LANES), axes, 0, 0)
        return moved.reshape(parts * rows, LANES)

    narrow, broad = depth * NARROW // LANES, depth * BROAD // LANES
    (payload,) = call(
        start_kernel,
        [load(slabs * (rows + depth + narrow))],
        own,
        consts=[],
        cost=pl.CostEstimate(flops=COST, bytes_accessed=4 * own.size, transcendentals=0),
    )
    c, v0, tc, tv0 = call(
        middle_kernel,
        [field, field, trace, trace],
        *halves,
        cost=pl.CostEstimate(flops=COST, bytes_accessed=4 * own.size, transcendentals=0),
    )
    sc, r0, v1, m1, ts, tr, tv, side_c, payload = call(
        first_kernel,
        [field] * 4 + [trace] * 3 + [sides(2), load(2 * depth + narrow)],
        c, v0, tc, tv0, swap(payload, ("patch", "sec"), patches * slabs),
        fields=1,
    )
    for step in range(STEPS):
        u1, y, v2, m2, ty, tv2, tu, side_r, payload = call(
            second_kernel,
            [field] * 4 + [trace] * 3 + [sides(2), load(3 * depth + broad)],
            r0, v1, m1, tr, tv, swap(payload),
        )
        last = step + 1 == STEPS
        outs = [field, base]
        if last:
            outs += [load(1)]
        else:
            outs += [field] * 2 + [trace] * 3 + [sides(3), load(1 + depth)]
        t, base_now, *rest = call(
            lambda sizes, *refs, last=last: third_kernel(sizes, last, *refs),
            outs,
            r0, y, v2, m2, ty, tv2, swap(payload),
            fields=2 if last else 0,
        )
        if last:
            (payload,) = rest
            break
        u2, zf, tt, tu2, tz, side_y, payload = rest
        c, r0, v1, m1, tr, tv, payload = call(
            next_kernel,
            [field] * 4 + [trace] * 2 + [load(2 * depth + narrow)],
            c, r0, y, t, sc, u1, u2, zf, tc, ts, tr, tu, ty, tu2, tt, tz,
            side_c, side_r, side_y, base_now, swap(payload),
            fields=1,
        )
    out = pl.pallas_call(
        functools.partial(last_kernel, patches),
        out_shape=shape(rows, LANES, LANES),
        in_specs=[vmem] * 6,
        out_specs=vmem,
        compiler_params=params,
    )(c, r0, y, t, base_now, swap(payload))
    return out[None]


def solution(mesh):
    placed = (P("patch", "sec", None, None), P(), P(), P())
    return jax.shard_map(
        functools.partial(shards, mesh.shape["patch"], mesh.shape["sec"]),
        mesh=mesh,
        in_specs=placed,
        out_specs=P("patch", "sec", None, None),
        check_vma=False,
    )
```

```python
import functools

import jax
import jax.numpy as jnp
import numpy as np
from jax import lax
from jax.experimental import pallas as pl
from jax.experimental.pallas import tpu as pltpu
from jax.sharding import PartitionSpec as P

STEPS = 2
MASS_BAND = (2416.0 / 5040.0, 1191.0 / 5040.0, 120.0 / 5040.0, 1.0 / 5040.0)
STIFF_BAND = (2.0 / 3.0, -0.125, -0.2, -1.0 / 120.0)
SCALE = 5040.0
MASS_HIGH, MASS_LOW = (2416.0, 1192.0, 120.0, 1.0), (0.0, -1.0, 0.0, 0.0)
STIFF_HIGH, STIFF_LOW = (3360.0, -632.0, -1008.0, -42.0), (0.0, 2.0, 0.0, 0.0)
PENALTY = 2.0
TIME_STEP = 1.0
STABILIZER = 2.0
GRADIENT_ENERGY = 0.5
HALF = TIME_STEP * GRADIENT_ENERGY
TWICE = TIME_STEP * STABILIZER
EXACT = lax.Precision.HIGHEST
LANES = 128
PAD = 8
KINDS = 6
SUMS = 4 * KINDS
NARROW, BROAD = 16, 32
COST = 1 << 34


def band_matrix(band, size):
    out = np.zeros((size, size), np.float32)
    for offset, value in enumerate(band):
        for row in range(size - offset):
            out[row, row + offset] = value
            out[row + offset, row] = value
    return out


def dot(left, right):
    return jnp.dot(left, right, precision=EXACT, preferred_element_type=jnp.float32)


def right_matrix(mass_band, stiff_band):
    mass, stiff = band_matrix(mass_band, LANES), band_matrix(stiff_band, LANES)
    return np.block([[mass, stiff], [np.zeros_like(mass), mass]])


def constants():
    high = right_matrix(MASS_HIGH, STIFF_HIGH).astype(jnp.bfloat16)
    low = right_matrix(MASS_LOW, STIFF_LOW).astype(jnp.bfloat16)
    return (np.concatenate([high, high, high, low]),)


def banded(distance, band, inside=None):
    out = jnp.zeros(distance.shape, jnp.float32)
    for offset, value in enumerate(band):
        hit = distance == offset
        out = jnp.where(hit if inside is None else hit & inside, value, out)
    return out


class Body:
    def __init__(self, sizes, refs, copies=1):
        self.depth, self.patches, self.slabs = sizes
        self.copies = copies
        self.tables, refs = refs[:3], refs[3:]
        self.near, self.strip, self.turned, self.stood = refs[-4:]
        if len(refs) > 4:
            self.pieces = refs[0]
        self.me = lax.axis_index("patch")
        self.lane = lax.broadcasted_iota(jnp.int32, (self.depth, LANES), 1)
        self.first, self.last = self.lane == 0, self.lane == LANES - 1
        self.wide = lax.broadcasted_iota(jnp.int32, (LANES, LANES), 1)
        self.edge = (self.wide == 0) | (self.wide == LANES - 1)
        row = lax.broadcasted_iota(jnp.int32, (LANES, LANES), 0)
        self.reverse = jnp.where(row + self.wide == LANES - 1, 1.0, 0.0)
        distance = jnp.abs(row - self.wide)
        self.plain = jnp.concatenate(
            [banded(distance, MASS_BAND), banded(distance, STIFF_BAND)], axis=1
        )

    def partner(self, patch, face):
        return self.tables[0][face, patch]

    def face_id(self, patch, face):
        return self.tables[1][face, patch]

    def flip(self, patch, face):
        return self.tables[2][face, patch]

    def split(self, value):
        pieces = []
        for last in (False, False, True):
            piece = value.astype(jnp.bfloat16)
            pieces.append(piece)
            if not last:
                value = value - piece.astype(jnp.float32)
        return pieces

    def stiff0(self, layer, finish, with_mass=False):
        depth = self.depth
        zeros = jnp.zeros((PAD, LANES), jnp.float32)
        for i in range(8):
            self.near[i, :PAD] = zeros
            self.near[i, PAD + LANES :] = zeros
        for z in range(depth):
            middle = layer(z)
            massed = (MASS_BAND[0] / SCALE) * middle
            stiffed = (STIFF_BAND[0] / SCALE) * middle
            for offset in (1, 2, 3):
                near = [layer(k) for k in (z - offset, z + offset) if 0 <= k < depth]
                if near:
                    both = near[0] if len(near) == 1 else near[0] + near[1]
                    massed = massed + (MASS_BAND[offset] / SCALE) * both
                    stiffed = stiffed + (STIFF_BAND[offset] / SCALE) * both
            pieces = self.split(jnp.concatenate([massed, stiffed], axis=1))
            pieces = jnp.concatenate(pieces + pieces[:1], axis=1)
            mixed = jnp.dot(pieces, self.pieces[...], preferred_element_type=jnp.float32)
            first, second = mixed[:, :LANES], mixed[:, LANES:]
            at, inside = 4 * (z % 2), slice(PAD, PAD + LANES)
            for o in (1, 2, 3):
                self.near[at + o, inside] = STIFF_BAND[o] * first + MASS_BAND[o] * second
            stiff = STIFF_BAND[0] * first + MASS_BAND[0] * second
            for o in (1, 2, 3):
                low, high = slice(PAD - o, PAD - o + LANES), slice(PAD + o, PAD + o + LANES)
                stiff = stiff + (self.near[at + o, low] + self.near[at + o, high])
            mass = None
            if with_mass:
                self.near[at, inside] = first
                mass = MASS_BAND[0] * first
                for o in (1, 2, 3):
                    low, high = slice(PAD - o, PAD - o + LANES), slice(PAD + o, PAD + o + LANES)
                    mass = mass + MASS_BAND[o] * (self.near[at, low] + self.near[at, high])
            finish(z, stiff, mass)

    def strips(self, field, slot=None, count=4):
        depth = field.shape[0]
        group = min(depth, 8)
        if slot is None:
            slot = 0
            for z in range(depth):
                rolled = pltpu.roll(field[z], (8 * (z % 8) + 4) % LANES, 1)
                pltpu.store(self.strip.at[slot, z // 8], rolled, mask=(self.wide >> 3) == z % 8)
        rows0 = [field[:, d, :] for d in range(count)]
        rows1 = [field[:, LANES - 1 - d, :] for d in range(count)]
        wanted = list(range(4 - count, 4 + count))
        pieces = {i: [] for i in wanted}
        for start in range(0, depth, group):
            self.turned[...] = jnp.transpose(self.strip[slot, start // 8])
            for i in wanted:
                pieces[i].append(self.turned[pl.ds(i, group, stride=8), :])
        columns = {i: jnp.concatenate(p, axis=0) if len(p) > 1 else p[0] for i, p in pieces.items()}
        return [
            rows0,
            rows1,
            [columns[4 + d] for d in range(count)],
            [columns[3 - d] for d in range(count)],
        ]

    def traces(self, field, slot=None):
        return [strip[0] for strip in self.strips(field, slot, 1)]

    def jumps(self, mine, other):
        return [PENALTY * (a - b) for a, b in zip(mine, other)]

    def stand(self, jump, slot=0):
        for start in range(0, self.depth, 8):
            self.turned[pl.ds(0, 8, stride=2), :] = jump[3][start : start + 8]
            self.turned[pl.ds(1, 8, stride=2), :] = jump[2][start : start + 8]
            self.stood[slot, start // 8] = jnp.transpose(self.turned[...])

    def column(self, z, slot=0):
        rolled = pltpu.roll(self.stood[slot, z // 8], (LANES - 2 * (z % 8) - 1) % LANES, 1)
        return jnp.where(self.edge, rolled, 0.0)

    def emit(self, field, z, value, jump=None, factor=1.0, slot=None):
        field[z] = value
        if jump is not None:
            field[z, :1, :] = field[z, :1, :] + factor * jump[0][z : z + 1]
            at = LANES - 1
            field[z, at:, :] = field[z, at:, :] + factor * jump[1][z : z + 1]
        if slot is not None:
            rolled = pltpu.roll(field[z], (8 * (z % 8) + 4) % LANES, 1)
            mask = (self.wide >> 3) == z % 8
            pltpu.store(self.strip.at[slot, z // 8], rolled, mask=mask)

    def lazy(self, field, make):
        made = set()

        def layer(z):
            if z not in made:
                made.add(z)
                make(z)
            return field[z]

        return layer

    def stiff_trace(self, inner, jump):
        out = []
        for f in range(4):
            side = f & 1
            low, high = (2, 3) if f < 2 else (0, 1)
            at = side * (LANES - 1)
            ends = []
            for face, end in ((low, 0), (high, LANES - 1)):
                shift = (end - at) % LANES
                ends.append(pltpu.roll(jump[face], shift, 1) if shift else jump[face])
            out.append(inner[f] + jump[f] + self.ends(*ends))
        return out

    def third_axis(self, value, band):
        layer = lax.broadcasted_iota(jnp.int32, value.shape, 0)
        out = band[0] * value
        for o in (1, 2, 3):
            low = jnp.where(layer >= o, pltpu.roll(value, o, 0), 0.0)
            high = jnp.where(layer < self.depth - o, pltpu.roll(value, self.depth - o, 0), 0.0)
            out = out + band[o] * (low + high)
        return out

    def slab(self, stiffs, masses, plain=None, arms=None):
        n = 4 * self.depth
        rows = [stack(x) for x in (masses, stiffs, plain, arms) if x is not None]
        both = dot(stack(rows), self.plain)
        lower = both[n : 2 * n, :LANES] + both[:n, LANES:]
        if plain is not None:
            lower = lower + both[2 * n : 3 * n, :LANES]
        out = [
            self.third_axis(a, MASS_BAND) + self.third_axis(b, STIFF_BAND)
            for a, b in zip(unstack(lower, self.depth), unstack(both[:n, :LANES], self.depth))
        ]
        return out if arms is None else (out, both[3 * n :])

    def depth_sum(self, strip, band):
        out = band[0] * strip[0]
        for d in (1, 2, 3):
            out = out + band[d] * strip[d]
        return out

    def corner_table(self, trace, inner=None, arms=None):
        table = jnp.zeros((self.depth, LANES), jnp.float32)
        ends = (0, LANES - 1)
        kinds = 1 if inner is None else KINDS
        for rs in range(2):
            for cs in range(2):
                slot = kinds * (2 * rs + cs)
                values = [(trace[rs], ends[cs])]
                if inner is not None:
                    values.append((inner[rs], ends[cs]))
                    for face, end in ((rs, ends[cs]), (2 + cs, ends[rs])):
                        part = arms[face * self.depth : (face + 1) * self.depth]
                        values.append((part[:, :LANES], end))
                        values.append((part[:, LANES:], end))
                for kind, (value, end) in enumerate(values):
                    shift = (slot + kind - end) % LANES
                    rolled = pltpu.roll(value, shift, 1) if shift else value
                    table = jnp.where(self.lane == slot + kind, rolled, table)
        return table

    def pack(self, table, width):
        count = width // NARROW
        rows = []
        for start in range(0, self.depth, 8):
            for low in range(count):
                total = None
                for i in range(low, 8, count):
                    layer = table[start + i : start + i + 1]
                    part = pltpu.roll(layer, LANES - NARROW * i, 1) if i else layer
                    total = part if total is None else total + part
                rows.append(total)
        return stack(rows) if len(rows) > 1 else rows[0]

    def send(self, payload, groups, packed):
        copies = self.copies
        rows = payload.shape[0] // (self.patches * copies)
        for f in range(4):
            to, at = self.partner(self.me, f) * copies, 0
            for group in groups:
                high = group[f].shape[0]
                for s in range(copies):
                    payload[pl.ds((to + s) * rows + at, high), :] = group[f]
                at += high
        for to in range(self.patches * copies):
            payload[to * rows + at : (to + 1) * rows, :] = packed

    def take(self, recv, patch, lo, count):
        rows = recv.shape[0] // (self.patches * self.copies)
        out = None
        for s in range(self.copies):
            part = recv[pl.ds((patch * self.copies + s) * rows + lo, count), :]
            out = part if out is None else out + part
        return out

    def received(self, recv, count, at=0):
        rows = count * self.depth
        return self.oriented(
            [self.take(recv, self.partner(self.me, f), at, rows) for f in range(4)], count
        )

    def oriented(self, raw, count):
        depth = self.depth
        rows = count * depth
        turned = dot(stack(raw), self.reverse)
        out = []
        for f in range(4):
            flipped = self.flip(self.me, f) == 1
            out.append(jnp.where(flipped, turned[f * rows : (f + 1) * rows], raw[f]))
        return [[out[f][i * depth : (i + 1) * depth] for f in range(4)] for i in range(count)]

    def corner(self, face, side):
        q, f1 = self.partner(self.me, face), self.face_id(self.me, face)
        eq = side ^ self.flip(self.me, face)
        s1 = f1 & 1
        upright = f1 < 2
        f2 = jnp.where(upright, 2 + eq, eq)
        kq = jnp.where(upright, 2 * s1 + eq, 2 * eq + s1)
        tq = jnp.where(upright, 4, 2)
        r, g = self.partner(q, f2), self.face_id(q, f2)
        s2 = s1 ^ self.flip(q, f2)
        flat = g < 2
        k = jnp.where(flat, 2 * (g & 1) + s2, 2 * s2 + (g & 1))
        t = jnp.where(flat, 2, 4)
        g2 = jnp.where(flat, 2 + s2, s2)
        r2, h = self.partner(r, g2), self.face_id(r, g2)
        s4 = (g & 1) ^ self.flip(r, g2)
        k2 = jnp.where(h < 2, 2 * (h & 1) + s4, 2 * s4 + (h & 1))
        return (q, kq, tq), (r, k, t), (r2, k2)

    def corners(self):
        return [[self.corner(f, s) for s in range(2)] for f in range(4)]

    def look(self, recv, at, patch, lane, side, width):
        count = width // NARROW
        shift = (side * (LANES - 1) + LANES - lane) & (LANES - 1)
        packed = self.take(recv, patch, at, self.depth // 8 * count)
        odd = (lax.broadcasted_iota(jnp.int32, (8, LANES), 0) & 1) == 1
        out = []
        for k in range(0, self.depth // 8 * count, count):
            spread = jnp.broadcast_to(packed[k : k + 1], (8, LANES))
            if count == 2:
                spread = jnp.where(odd, packed[k + 1 : k + 2], spread)
            out.append(pltpu.roll(spread, 0, 1, stride=NARROW, stride_axis=0))
        return pltpu.roll(stack(out) if len(out) > 1 else out[0], shift, 1)

    def ends(self, low, high):
        return jnp.where(self.first, low, jnp.where(self.last, high, 0.0))

    def other_stiff(self, recv, at, mine, theirs, inner, corners, kinds, width):
        out = []
        edge = self.first | self.last
        for f in range(4):
            across = []
            for s in range(2):
                r, k, t = corners[f][s][1]
                across.append(self.look(recv, at, r, kinds * k, s, width))
            value = inner[f] + PENALTY * (theirs[f] - mine[f])
            far = PENALTY * (theirs[f] - self.ends(*across))
            out.append(value + jnp.where(edge, far, 0.0))
        return out


def stack(values):
    return jnp.concatenate(values, 0)


def unstack(value, depth):
    return [value[f * depth : (f + 1) * depth] for f in range(4)]


def cubic(x, s):
    return x * x * x - x + GRADIENT_ENERGY * s


def start_kernel(sizes, own, payload, *refs):
    body = Body(sizes, refs, sizes[2])
    rows = own.shape[0]
    layer = lax.broadcasted_iota(jnp.int32, (body.depth, LANES), 0)
    low = lax.axis_index("sec") * rows
    here = (layer >= low) & (layer < low + rows)

    def place(value):
        return jnp.where(here, stack([value] * body.slabs), 0.0)

    strips = body.strips(own)
    trace = [s[0] for s in strips]
    inner = body.slab(
        [place(body.depth_sum(s, STIFF_BAND)) for s in strips],
        [place(body.depth_sum(s, MASS_BAND)) for s in strips],
    )
    table = body.corner_table([place(a) for a in trace])
    body.send(payload, [trace, inner], body.pack(table, NARROW))


def flux_tail(body, layer, mine, other, r0, v1, m1, tr, tv, payload):
    jump = body.jumps(mine, other)
    body.stand(jump, 1)

    def residual(z, stiff, mass):
        body.emit(r0, z, -TIME_STEP * (stiff + body.column(z, 1)), jump, -TIME_STEP, 0)

    body.stiff0(layer, residual)

    def image(z, stiff, mass):
        body.emit(v1, z, stiff, slot=1)
        m1[z] = mass

    body.stiff0(lambda z: r0[z], image, True)
    trace, inner = body.traces(r0, 0), body.traces(v1, 1)
    tr[...], tv[...] = stack(trace), stack(inner)
    body.copies = 1
    body.send(payload, [trace, inner], body.pack(body.corner_table(trace), NARROW))


def middle_kernel(sizes, *refs):
    slabs, refs = refs[: sizes[2]], refs[sizes[2] :]
    c, v0, tc, tv = refs[:4]
    body = Body(sizes, refs[4:])
    count = body.slabs
    rows = body.depth // count
    for k, slab in enumerate(slabs):
        c[pl.ds(lax.rem(lax.axis_index("sec") + k, count) * rows, rows)] = slab[...]

    def image(z, stiff, mass):
        v0[z] = stiff

    body.stiff0(lambda z: c[z], image)
    tc[...], tv[...] = stack(body.traces(c)), stack(body.traces(v0))


def first_kernel(sizes, c, v0, tc, tv0, recv, sc, r0, v1, m1, ts, tr, tv, sides, payload,
                 potential, *refs):
    body = Body(sizes, refs, sizes[2])
    depth, count = body.depth, body.slabs
    rows = depth // count
    high = recv.shape[0] // (body.patches * count)
    raw = []
    for f in range(4):
        q = body.partner(body.me, f)
        parts = [recv[pl.ds((q * count + s) * high, rows), :] for s in range(count)]
        raw.append(stack(parts + [body.take(recv, q, rows, depth)]))
    other, inner = body.oriented(raw, 2)
    mine = unstack(tc, depth)
    jump = body.jumps(mine, other)
    body.stand(jump)

    def make(z):
        body.emit(sc, z, v0[z] + body.column(z), jump)
        potential[z] = cubic(c[z], sc[z])

    mine_s = body.stiff_trace(unstack(tv0, depth), jump)
    other_s = body.other_stiff(recv, rows + depth, mine, other, inner, body.corners(), 1, NARROW)
    ts[...] = stack(mine_s)
    sides[0], sides[1] = stack(other), stack(other_s)
    mine_p = [cubic(x, s) for x, s in zip(mine, mine_s)]
    other_p = [cubic(x, s) for x, s in zip(other, other_s)]
    layer = body.lazy(potential, make)
    flux_tail(body, layer, mine_p, other_p, r0, v1, m1, tr, tv, payload)


def second_kernel(sizes, r0, v1, m1, tr, tv, recv, u1, y, v2, m2, ty, tv2, tu, sides, payload,
                  *refs):
    body = Body(sizes, refs)
    depth = body.depth
    other, inner = body.received(recv, 2)
    mine = unstack(tr, depth)
    jump = body.jumps(mine, other)
    body.stand(jump)

    def make(z, jump=jump):
        body.emit(u1, z, v1[z] + body.column(z), jump)

    mine_s = body.stiff_trace(unstack(tv, depth), jump)
    other_s = body.other_stiff(
        recv, 2 * depth, mine, other, inner, body.corners(), 1, NARROW
    )
    tu[...] = stack(mine_s)
    sides[0], sides[1] = stack(other), stack(other_s)
    jump = body.jumps(mine_s, other_s)
    body.stand(jump, 1)

    def image(z, stiff, mass):
        value = m1[z] + TWICE * u1[z] + HALF * (stiff + body.column(z, 1))
        body.emit(y, z, value, jump, HALF, 0)

    body.stiff0(body.lazy(u1, make), image)
    sums = [[], [], []]

    def again(z, stiff, mass):
        body.emit(v2, z, stiff, slot=1)
        m2[z] = mass
        a, b = r0[z], y[z]
        for i, product in enumerate((a * a, a * b, b * b)):
            sums[i].append(jnp.sum(product, axis=0, keepdims=True))

    body.stiff0(lambda z: y[z], again, True)
    strips_y, strips = body.strips(y, 0), body.strips(v2, 1)
    trace, inner = [s[0] for s in strips_y], [s[0] for s in strips]
    ty[...], tv2[...] = stack(trace), stack(inner)
    mixed, arms = body.slab(
        [HALF * body.depth_sum(s, STIFF_BAND) for s in strips],
        [HALF * body.depth_sum(s, MASS_BAND) for s in strips],
        [body.depth_sum(s, MASS_BAND) for s in strips_y],
        trace,
    )
    outer = [TWICE * a + b for a, b in zip(inner, mixed)]
    table = body.corner_table(trace, inner, arms)
    for i in range(3):
        total = jnp.sum(stack(sums[i]), axis=1, keepdims=True)
        table = jnp.where(body.lane == SUMS + i, total, table)
    body.send(payload, [trace, inner, outer], body.pack(table, BROAD))


def third_kernel(sizes, last, r0, y, v2, m2, ty, tv2, recv, *refs):
    if last:
        t, base, payload, u2, zf = refs[:5]
        body = Body(sizes, refs[5:])
    else:
        t, base, u2, zf, tt, tu2, tz, sides, payload = refs[:9]
        body = Body(sizes, refs[9:])
    depth, patches = body.depth, body.patches
    at = 3 * depth
    packed = depth * BROAD // LANES
    known = recv[at : at + packed, :]
    for p in range(1, patches):
        known = known + recv[p * (at + packed) + at : (p + 1) * (at + packed), :]
    odd = lax.broadcasted_iota(jnp.int32, (packed, LANES), 0) & 1
    slot = lax.broadcasted_iota(jnp.int32, (packed, LANES), 1) + NARROW * odd
    slot = slot & (BROAD - 1)
    m0, m1, m2s = [
        jnp.sum(jnp.where(slot == SUMS + i, known, 0.0), keepdims=True) for i in range(3)
    ]
    a0 = m0 / m1
    other, inner, outer = body.received(recv, 3)
    corners = body.corners()
    mine = unstack(ty, depth)
    jump = body.jumps(mine, other)
    body.stand(jump)

    def make(z, jump=jump):
        body.emit(u2, z, v2[z] + body.column(z), jump)

    mine_s = body.stiff_trace(unstack(tv2, depth), jump)
    other_s = body.other_stiff(recv, at, mine, other, inner, corners, KINDS, BROAD)
    masses, stiffs, far = [], [], []
    for f in range(4):
        arm_m, arm_k, across = [], [], []
        for s in range(2):
            (q, kq, tq), (r, k, kind), (r2, k2) = corners[f][s]
            look = functools.partial(body.look, recv, at, side=s, width=BROAD)
            arm_m.append(look(q, KINDS * kq + tq) - look(r, KINDS * k + kind))
            arm_k.append(look(q, KINDS * kq + tq + 1) - look(r, KINDS * k + kind + 1))
            value = look(r, KINDS * k)
            across.append(
                look(r, KINDS * k + 1)
                + PENALTY * (value - other[f])
                + PENALTY * (value - look(r2, KINDS * k2))
            )
        theirs = PENALTY * (other[f] - mine[f])
        masses.append(MASS_BAND[0] * theirs + PENALTY * body.ends(*arm_m))
        stiffs.append(STIFF_BAND[0] * theirs + PENALTY * body.ends(*arm_k))
        far.append(body.ends(*across))
    pushed = body.slab(stiffs, masses)
    edge = body.first | body.last
    other_t = []
    for f in range(4):
        again = pushed[f] + PENALTY * (other_s[f] - mine_s[f])
        again = again + jnp.where(edge, PENALTY * (other_s[f] - far[f]), 0.0)
        image = outer[f] + TWICE * (other_s[f] - inner[f]) + HALF * again
        other_t.append(other[f] - a0 * image)
    jump_s = body.jumps(mine_s, other_s)
    body.stand(jump_s, 1)

    def turn(z, stiff, mass):
        image = m2[z] + TWICE * u2[z] + HALF * (stiff + body.column(z, 1))
        body.emit(t, z, y[z] - a0 * image, jump_s, -HALF * a0, 0)

    body.stiff0(body.lazy(u2, make), turn)
    mine_t = body.traces(t, 0)
    jump_t = body.jumps(mine_t, other_t)
    body.stand(jump_t)
    sums = [jnp.zeros((8, LANES), jnp.float32)] * 6

    def image(z, stiff, mass):
        body.emit(zf, z, stiff + body.column(z), jump_t, slot=None if last else 1)
        b, x, s = y[z], t[z], zf[z]
        a = r0[z] - a0 * b
        energy = x * (mass + TWICE * s) + HALF * (s * s)
        for i, product in enumerate((a * a, a * x, a * b, x * x, x * b, energy)):
            sums[i] = sums[i] + jnp.sum(product.reshape(LANES // 8, 8, LANES), axis=0)

    body.stiff0(lambda z: t[z], image, True)
    moments = jnp.zeros((1, LANES), jnp.float32)
    lane = lax.broadcasted_iota(jnp.int32, (1, LANES), 1)
    for i, value in enumerate(sums):
        value = jnp.sum(jnp.sum(value, axis=0, keepdims=True), axis=1, keepdims=True)
        moments = jnp.where(lane == i, value, moments)
    for i, value in enumerate((a0, m0, m1, m2s)):
        base[i : i + 1, :] = jnp.broadcast_to(value, (1, LANES))
    rows = payload.shape[0] // patches
    for to in range(patches):
        payload[to * rows : to * rows + 1, :] = moments
    if not last:
        trace = body.traces(zf, 1)
        tt[...], tu2[...], tz[...] = stack(mine_t), stack(mine_s), stack(trace)
        sides[0], sides[1], sides[2] = stack(other), stack(other_s), stack(other_t)
        for f in range(4):
            payload[pl.ds(body.partner(body.me, f) * rows + 1, depth), :] = trace[f]


def weights(patches, base, recv):
    rows = recv.shape[0] // patches
    total = recv[:1, :]
    for p in range(1, patches):
        total = total + recv[p * rows : p * rows + 1, :]
    a0, m0, m1, m2 = [base[i : i + 1, :1] for i in range(4)]
    rr1, g1, g2, tt, ty, tat = [total[:, i : i + 1] for i in range(6)]
    b0 = rr1 / m0
    a1 = rr1 / (g1 + 2.0 * b0 * g2 + b0 * b0 * m1)
    rr2 = rr1 - 2.0 * a1 * (g1 + b0 * g2) + a1 * a1 * (tt + 2.0 * b0 * ty + b0 * b0 * m2)
    b1 = rr2 / rr1
    shift = a1 * b0 / a0
    c1, c0, c2 = 1.0 + b1 + shift, b1 * b0 - shift, -a1
    a2 = rr2 / (
        c1 * c1 * g1
        + c0 * c0 * m1
        + c2 * c2 * tat
        + 2.0 * (c1 * c0 * g2 + c1 * c2 * tt + c0 * c2 * ty)
    )
    return a0 + a1 * (1.0 + b0) + a2 * (c1 + c0), -a0 * (a1 + a2 * c1), a2 * c2


def next_kernel(sizes, c, r0, y, t, sc, u1, u2, zf, tc, ts, tr, tu, ty, tu2, tt, tz,
                side_c, side_r, side_y, base, recv,
                cn, rn, v1, m1, trn, tvn, payload, potential, *refs):
    body = Body(sizes, refs)
    depth = body.depth
    x = weights(body.patches, base, recv)

    def mix(*values):
        return values[0] + x[0] * values[1] + x[1] * values[2] + x[2] * values[3]

    def make(z):
        cn[z] = mix(c[z], r0[z], y[z], t[z])
        potential[z] = cubic(cn[z], mix(sc[z], u1[z], u2[z], zf[z]))

    (side_z,) = body.received(recv, 1, 1)
    mine = cubic(
        mix(tc[...], tr[...], ty[...], tt[...]), mix(ts[...], tu[...], tu2[...], tz[...])
    )
    other = cubic(
        mix(side_c[0], side_r[0], side_y[0], side_y[2]),
        mix(side_c[1], side_r[1], side_y[1], stack(side_z)),
    )
    layer = body.lazy(potential, make)
    mine, other = unstack(mine, depth), unstack(other, depth)
    flux_tail(body, layer, mine, other, rn, v1, m1, trn, tvn, payload)


def last_kernel(patches, c, r0, y, t, base, recv, out):
    x0, x1, x2 = weights(patches, base, recv)
    rows = out.shape[0]
    low = lax.axis_index("sec") * rows
    for z in range(rows):
        k = low + z
        out[z] = c[k] + x0 * r0[k] + x1 * y[k] + x2 * t[k]


def shards(patches, slabs, concentration, partner, face_id, flip):
    own = concentration[0]
    rows = own.shape[0]
    depth = rows * slabs
    halves = [own]
    for k in range(1, slabs):
        halves.append(lax.ppermute(own, "sec", [((i + k) % slabs, i) for i in range(slabs)]))
    matrices = [jnp.asarray(x) for x in constants()]
    tables = [partner.T, face_id.T, flip.T]
    vmem, smem = pl.BlockSpec(memory_space=pltpu.VMEM), pl.BlockSpec(memory_space=pltpu.SMEM)
    params = pltpu.CompilerParams(vmem_limit_bytes=(4 + depth) << 20)

    def shape(*dims):
        return jax.ShapeDtypeStruct(dims, jnp.float32)

    field, trace, base = shape(depth, LANES, LANES), shape(4 * depth, LANES), shape(8, LANES)

    def sides(count):
        return shape(count, 4 * depth, LANES)

    def load(count):
        return shape(patches * count, LANES)

    def call(kernel, outs, *args, fields=0, consts=matrices, cost=None):
        count, head = len(args), 3 + len(consts)
        inside = [pltpu.VMEM((depth, LANES, LANES), jnp.float32)] * fields
        shared = [
            pltpu.VMEM((8, LANES + 2 * PAD, LANES), jnp.float32),
            pltpu.VMEM((2, -(-depth // 8), LANES, LANES), jnp.float32),
            pltpu.VMEM((LANES, LANES), jnp.float32),
            pltpu.VMEM((2, -(-depth // 8), LANES, LANES), jnp.float32),
        ]

        def run(*refs):
            common, rest = refs[:head], refs[head:]
            cut = len(rest) - len(shared)
            kernel((depth, patches, slabs), *rest[:cut], *common, *rest[cut:])

        return pl.pallas_call(
            run,
            out_shape=outs,
            in_specs=[smem] * 3 + [vmem] * (len(consts) + count),
            out_specs=[vmem] * len(outs),
            scratch_shapes=inside + shared,
            compiler_params=params,
            cost_estimate=cost,
            name=kernel.__name__ if hasattr(kernel, "__name__") else "third_kernel",
        )(*tables, *consts, *args)

    def swap(payload, axes="patch", parts=patches):
        rows = payload.shape[0] // parts
        moved = lax.all_to_all(payload.reshape(parts, 1, rows * LANES), axes, 0, 0)
        return moved.reshape(parts * rows, LANES)

    narrow, broad = depth * NARROW // LANES, depth * BROAD // LANES
    (payload,) = call(
        start_kernel,
        [load(slabs * (rows + depth + narrow))],
        own,
        consts=[],
        cost=pl.CostEstimate(flops=COST, bytes_accessed=4 * own.size, transcendentals=0),
    )
    c, v0, tc, tv0 = call(
        middle_kernel,
        [field, field, trace, trace],
        *halves,
        cost=pl.CostEstimate(flops=COST, bytes_accessed=4 * own.size, transcendentals=0),
    )
    sc, r0, v1, m1, ts, tr, tv, side_c, payload = call(
        first_kernel,
        [field] * 4 + [trace] * 3 + [sides(2), load(2 * depth + narrow)],
        c, v0, tc, tv0, swap(payload, ("patch", "sec"), patches * slabs),
        fields=1,
    )
    for step in range(STEPS):
        u1, y, v2, m2, ty, tv2, tu, side_r, payload = call(
            second_kernel,
            [field] * 4 + [trace] * 3 + [sides(2), load(3 * depth + broad)],
            r0, v1, m1, tr, tv, swap(payload),
        )
        last = step + 1 == STEPS
        outs = [field, base]
        if last:
            outs += [load(1)]
        else:
            outs += [field] * 2 + [trace] * 3 + [sides(3), load(1 + depth)]
        t, base_now, *rest = call(
            lambda sizes, *refs, last=last: third_kernel(sizes, last, *refs),
            outs,
            r0, y, v2, m2, ty, tv2, swap(payload),
            fields=2 if last else 0,
        )
        if last:
            (payload,) = rest
            break
        u2, zf, tt, tu2, tz, side_y, payload = rest
        c, r0, v1, m1, tr, tv, payload = call(
            next_kernel,
            [field] * 4 + [trace] * 2 + [load(2 * depth + narrow)],
            c, r0, y, t, sc, u1, u2, zf, tc, ts, tr, tu, ty, tu2, tt, tz,
            side_c, side_r, side_y, base_now, swap(payload),
            fields=1,
        )
    out = pl.pallas_call(
        functools.partial(last_kernel, patches),
        out_shape=shape(rows, LANES, LANES),
        in_specs=[vmem] * 6,
        out_specs=vmem,
        compiler_params=params,
    )(c, r0, y, t, base_now, swap(payload))
    return out[None]


def solution(mesh):
    placed = (P("patch", "sec", None, None), P(), P(), P())
    return jax.shard_map(
        functools.partial(shards, mesh.shape["patch"], mesh.shape["sec"]),
        mesh=mesh,
        in_specs=placed,
        out_specs=P("patch", "sec", None, None),
        check_vma=False,
    )
```

```python
import functools

import jax
import jax.numpy as jnp
import numpy as np
from jax import lax
from jax.experimental import pallas as pl
from jax.experimental.pallas import tpu as pltpu
from jax.sharding import PartitionSpec as P

STEPS = 2
MASS_BAND = (2416.0 / 5040.0, 1191.0 / 5040.0, 120.0 / 5040.0, 1.0 / 5040.0)
STIFF_BAND = (2.0 / 3.0, -0.125, -0.2, -1.0 / 120.0)
SCALE = 5040.0
MASS_HIGH, MASS_LOW = (2416.0, 1192.0, 120.0, 1.0), (0.0, -1.0, 0.0, 0.0)
STIFF_HIGH, STIFF_LOW = (3360.0, -632.0, -1008.0, -42.0), (0.0, 2.0, 0.0, 0.0)
PENALTY = 2.0
TIME_STEP = 1.0
STABILIZER = 2.0
GRADIENT_ENERGY = 0.5
HALF = TIME_STEP * GRADIENT_ENERGY
TWICE = TIME_STEP * STABILIZER
EXACT = lax.Precision.HIGHEST
LANES = 128
PAD = 8
KINDS = 6
SUMS = 4 * KINDS
NARROW, BROAD = 16, 32
COST = 1 << 34


def band_matrix(band, size):
    out = np.zeros((size, size), np.float32)
    for offset, value in enumerate(band):
        for row in range(size - offset):
            out[row, row + offset] = value
            out[row + offset, row] = value
    return out


def dot(left, right):
    return jnp.dot(left, right, precision=EXACT, preferred_element_type=jnp.float32)


def right_matrix(mass_band, stiff_band):
    mass, stiff = band_matrix(mass_band, LANES), band_matrix(stiff_band, LANES)
    return np.block([[mass, stiff], [np.zeros_like(mass), mass]])


def constants():
    high = right_matrix(MASS_HIGH, STIFF_HIGH).astype(jnp.bfloat16)
    low = right_matrix(MASS_LOW, STIFF_LOW).astype(jnp.bfloat16)
    return (np.concatenate([high, high, high, low]),)


def banded(distance, band, inside=None):
    out = jnp.zeros(distance.shape, jnp.float32)
    for offset, value in enumerate(band):
        hit = distance == offset
        out = jnp.where(hit if inside is None else hit & inside, value, out)
    return out


class Body:
    def __init__(self, sizes, refs, copies=1):
        self.depth, self.patches, self.slabs = sizes
        self.copies = copies
        self.tables, refs = refs[:3], refs[3:]
        self.near, self.strip, self.turned, self.stood = refs[-4:]
        self.pieces = refs[0] if len(refs) > 4 else None
        self.me = lax.axis_index("patch")
        self.lane = lax.broadcasted_iota(jnp.int32, (self.depth, LANES), 1)
        self.first, self.last = self.lane == 0, self.lane == LANES - 1
        self.wide = lax.broadcasted_iota(jnp.int32, (LANES, LANES), 1)
        self.edge = (self.wide == 0) | (self.wide == LANES - 1)
        row = lax.broadcasted_iota(jnp.int32, (LANES, LANES), 0)
        reverse = jnp.where(row + self.wide == LANES - 1, 1.0, 0.0).astype(jnp.bfloat16)
        self.reverse = stack([reverse] * 3)
        distance = jnp.abs(row - self.wide)
        if self.pieces is None:
            self.plain = jnp.concatenate(
                [banded(distance, MASS_BAND), banded(distance, STIFF_BAND)], axis=1
            )
        else:
            high = self.pieces[:LANES]
            self.plain = stack([high, high, high, self.pieces[6 * LANES : 7 * LANES]])

    def partner(self, patch, face):
        return self.tables[0][face, patch]

    def face_id(self, patch, face):
        return self.tables[1][face, patch]

    def flip(self, patch, face):
        return self.tables[2][face, patch]

    def split(self, value):
        pieces = []
        for last in (False, False, True):
            piece = value.astype(jnp.bfloat16)
            pieces.append(piece)
            if not last:
                value = value - piece.astype(jnp.float32)
        return pieces

    def stiff0(self, layer, finish, with_mass=False):
        depth = self.depth
        zeros = jnp.zeros((PAD, LANES), jnp.float32)
        for i in range(8):
            self.near[i, :PAD] = zeros
            self.near[i, PAD + LANES :] = zeros
        for z in range(depth):
            middle = layer(z)
            massed = (MASS_BAND[0] / SCALE) * middle
            stiffed = (STIFF_BAND[0] / SCALE) * middle
            for offset in (1, 2, 3):
                near = [layer(k) for k in (z - offset, z + offset) if 0 <= k < depth]
                if near:
                    both = near[0] if len(near) == 1 else near[0] + near[1]
                    massed = massed + (MASS_BAND[offset] / SCALE) * both
                    stiffed = stiffed + (STIFF_BAND[offset] / SCALE) * both
            pieces = self.split(jnp.concatenate([massed, stiffed], axis=1))
            pieces = jnp.concatenate(pieces + pieces[:1], axis=1)
            mixed = jnp.dot(pieces, self.pieces[...], preferred_element_type=jnp.float32)
            first, second = mixed[:, :LANES], mixed[:, LANES:]
            at, inside = 4 * (z % 2), slice(PAD, PAD + LANES)
            for o in (1, 2, 3):
                self.near[at + o, inside] = STIFF_BAND[o] * first + MASS_BAND[o] * second
            stiff = STIFF_BAND[0] * first + MASS_BAND[0] * second
            for o in (1, 2, 3):
                low, high = slice(PAD - o, PAD - o + LANES), slice(PAD + o, PAD + o + LANES)
                stiff = stiff + (self.near[at + o, low] + self.near[at + o, high])
            mass = None
            if with_mass:
                self.near[at, inside] = first
                mass = MASS_BAND[0] * first
                for o in (1, 2, 3):
                    low, high = slice(PAD - o, PAD - o + LANES), slice(PAD + o, PAD + o + LANES)
                    mass = mass + MASS_BAND[o] * (self.near[at, low] + self.near[at, high])
            finish(z, stiff, mass)

    def strips(self, field, slot=None, count=4):
        depth = field.shape[0]
        group = min(depth, 8)
        if slot is None:
            slot = 0
            for z in range(depth):
                rolled = pltpu.roll(field[z], (8 * (z % 8) + 4) % LANES, 1)
                pltpu.store(self.strip.at[slot, z // 8], rolled, mask=(self.wide >> 3) == z % 8)
        rows0 = [field[:, d, :] for d in range(count)]
        rows1 = [field[:, LANES - 1 - d, :] for d in range(count)]
        wanted = list(range(4 - count, 4 + count))
        pieces = {i: [] for i in wanted}
        for start in range(0, depth, group):
            self.turned[...] = jnp.transpose(self.strip[slot, start // 8])
            for i in wanted:
                pieces[i].append(self.turned[pl.ds(i, group, stride=8), :])
        columns = {i: jnp.concatenate(p, axis=0) if len(p) > 1 else p[0] for i, p in pieces.items()}
        return [
            rows0,
            rows1,
            [columns[4 + d] for d in range(count)],
            [columns[3 - d] for d in range(count)],
        ]

    def traces(self, field, slot=None):
        return [strip[0] for strip in self.strips(field, slot, 1)]

    def jumps(self, mine, other):
        return [PENALTY * (a - b) for a, b in zip(mine, other)]

    def stand(self, jump, slot=0):
        for start in range(0, self.depth, 8):
            self.turned[pl.ds(0, 8, stride=2), :] = jump[3][start : start + 8]
            self.turned[pl.ds(1, 8, stride=2), :] = jump[2][start : start + 8]
            self.stood[slot, start // 8] = jnp.transpose(self.turned[...])

    def column(self, z, slot=0):
        rolled = pltpu.roll(self.stood[slot, z // 8], (LANES - 2 * (z % 8) - 1) % LANES, 1)
        return jnp.where(self.edge, rolled, 0.0)

    def emit(self, field, z, value, jump=None, factor=1.0, slot=None):
        field[z] = value
        if jump is not None:
            field[z, :1, :] = field[z, :1, :] + factor * jump[0][z : z + 1]
            at = LANES - 1
            field[z, at:, :] = field[z, at:, :] + factor * jump[1][z : z + 1]
        if slot is not None:
            rolled = pltpu.roll(field[z], (8 * (z % 8) + 4) % LANES, 1)
            mask = (self.wide >> 3) == z % 8
            pltpu.store(self.strip.at[slot, z // 8], rolled, mask=mask)

    def lazy(self, field, make):
        made = set()

        def layer(z):
            if z not in made:
                made.add(z)
                make(z)
            return field[z]

        return layer

    def stiff_trace(self, inner, jump):
        out = []
        for f in range(4):
            side = f & 1
            low, high = (2, 3) if f < 2 else (0, 1)
            at = side * (LANES - 1)
            ends = []
            for face, end in ((low, 0), (high, LANES - 1)):
                shift = (end - at) % LANES
                ends.append(pltpu.roll(jump[face], shift, 1) if shift else jump[face])
            out.append(inner[f] + jump[f] + self.ends(*ends))
        return out

    def lane_bands(self, value):
        if self.pieces is None:
            return dot(value, self.plain)
        pieces = self.split(value * (1.0 / SCALE))
        pieces = jnp.concatenate(pieces + pieces[:1], axis=1)
        return jnp.dot(pieces, self.plain, preferred_element_type=jnp.float32)

    def third_axis(self, value, band):
        layer = lax.broadcasted_iota(jnp.int32, value.shape, 0)
        out = band[0] * value
        for o in (1, 2, 3):
            low = jnp.where(layer >= o, pltpu.roll(value, o, 0), 0.0)
            high = jnp.where(layer < self.depth - o, pltpu.roll(value, self.depth - o, 0), 0.0)
            out = out + band[o] * (low + high)
        return out

    def slab(self, stiffs, masses, plain=None, arms=None):
        n = 4 * self.depth
        rows = [stack(x) for x in (masses, stiffs, plain, arms) if x is not None]
        both = self.lane_bands(stack(rows))
        lower = both[n : 2 * n, :LANES] + both[:n, LANES:]
        if plain is not None:
            lower = lower + both[2 * n : 3 * n, :LANES]
        out = [
            self.third_axis(a, MASS_BAND) + self.third_axis(b, STIFF_BAND)
            for a, b in zip(unstack(lower, self.depth), unstack(both[:n, :LANES], self.depth))
        ]
        return out if arms is None else (out, both[3 * n :])

    def depth_sum(self, strip, band):
        out = band[0] * strip[0]
        for d in (1, 2, 3):
            out = out + band[d] * strip[d]
        return out

    def corner_table(self, trace, inner=None, arms=None):
        table = jnp.zeros((self.depth, LANES), jnp.float32)
        ends = (0, LANES - 1)
        kinds = 1 if inner is None else KINDS
        for rs in range(2):
            for cs in range(2):
                slot = kinds * (2 * rs + cs)
                values = [(trace[rs], ends[cs])]
                if inner is not None:
                    values.append((inner[rs], ends[cs]))
                    for face, end in ((rs, ends[cs]), (2 + cs, ends[rs])):
                        part = arms[face * self.depth : (face + 1) * self.depth]
                        values.append((part[:, :LANES], end))
                        values.append((part[:, LANES:], end))
                for kind, (value, end) in enumerate(values):
                    shift = (slot + kind - end) % LANES
                    rolled = pltpu.roll(value, shift, 1) if shift else value
                    table = jnp.where(self.lane == slot + kind, rolled, table)
        return table

    def pack(self, table, width):
        count = width // NARROW
        rows = []
        for start in range(0, self.depth, 8):
            for low in range(count):
                total = None
                for i in range(low, 8, count):
                    layer = table[start + i : start + i + 1]
                    part = pltpu.roll(layer, LANES - NARROW * i, 1) if i else layer
                    total = part if total is None else total + part
                rows.append(total)
        return stack(rows) if len(rows) > 1 else rows[0]

    def send(self, payload, groups, packed):
        copies = self.copies
        rows = payload.shape[0] // (self.patches * copies)
        for f in range(4):
            to, at = self.partner(self.me, f) * copies, 0
            for group in groups:
                high = group[f].shape[0]
                for s in range(copies):
                    payload[pl.ds((to + s) * rows + at, high), :] = group[f]
                at += high
        for to in range(self.patches * copies):
            payload[to * rows + at : (to + 1) * rows, :] = packed

    def take(self, recv, patch, lo, count):
        rows = recv.shape[0] // (self.patches * self.copies)
        out = None
        for s in range(self.copies):
            part = recv[pl.ds((patch * self.copies + s) * rows + lo, count), :]
            out = part if out is None else out + part
        return out

    def received(self, recv, count, at=0):
        rows = count * self.depth
        return self.oriented(
            [self.take(recv, self.partner(self.me, f), at, rows) for f in range(4)], count
        )

    def oriented(self, raw, count):
        depth = self.depth
        rows = count * depth
        pieces = jnp.concatenate(self.split(stack(raw)), axis=1)
        turned = jnp.dot(pieces, self.reverse, preferred_element_type=jnp.float32)
        out = []
        for f in range(4):
            flipped = self.flip(self.me, f) == 1
            out.append(jnp.where(flipped, turned[f * rows : (f + 1) * rows], raw[f]))
        return [[out[f][i * depth : (i + 1) * depth] for f in range(4)] for i in range(count)]

    def corner(self, face, side):
        q, f1 = self.partner(self.me, face), self.face_id(self.me, face)
        eq = side ^ self.flip(self.me, face)
        s1 = f1 & 1
        upright = f1 < 2
        f2 = jnp.where(upright, 2 + eq, eq)
        kq = jnp.where(upright, 2 * s1 + eq, 2 * eq + s1)
        tq = jnp.where(upright, 4, 2)
        r, g = self.partner(q, f2), self.face_id(q, f2)
        s2 = s1 ^ self.flip(q, f2)
        flat = g < 2
        k = jnp.where(flat, 2 * (g & 1) + s2, 2 * s2 + (g & 1))
        t = jnp.where(flat, 2, 4)
        g2 = jnp.where(flat, 2 + s2, s2)
        r2, h = self.partner(r, g2), self.face_id(r, g2)
        s4 = (g & 1) ^ self.flip(r, g2)
        k2 = jnp.where(h < 2, 2 * (h & 1) + s4, 2 * s4 + (h & 1))
        return (q, kq, tq), (r, k, t), (r2, k2)

    def corners(self):
        return [[self.corner(f, s) for s in range(2)] for f in range(4)]

    def look(self, recv, at, patch, lane, side, width):
        count = width // NARROW
        shift = (side * (LANES - 1) + LANES - lane) & (LANES - 1)
        packed = self.take(recv, patch, at, self.depth // 8 * count)
        odd = (lax.broadcasted_iota(jnp.int32, (8, LANES), 0) & 1) == 1
        out = []
        for k in range(0, self.depth // 8 * count, count):
            spread = jnp.broadcast_to(packed[k : k + 1], (8, LANES))
            if count == 2:
                spread = jnp.where(odd, packed[k + 1 : k + 2], spread)
            out.append(pltpu.roll(spread, 0, 1, stride=NARROW, stride_axis=0))
        return pltpu.roll(stack(out) if len(out) > 1 else out[0], shift, 1)

    def ends(self, low, high):
        return jnp.where(self.first, low, jnp.where(self.last, high, 0.0))

    def other_stiff(self, recv, at, mine, theirs, inner, corners, kinds, width):
        out = []
        edge = self.first | self.last
        for f in range(4):
            across = []
            for s in range(2):
                r, k, t = corners[f][s][1]
                across.append(self.look(recv, at, r, kinds * k, s, width))
            value = inner[f] + PENALTY * (theirs[f] - mine[f])
            far = PENALTY * (theirs[f] - self.ends(*across))
            out.append(value + jnp.where(edge, far, 0.0))
        return out


def stack(values):
    return jnp.concatenate(values, 0)


def unstack(value, depth):
    return [value[f * depth : (f + 1) * depth] for f in range(4)]


def cubic(x, s):
    return x * x * x - x + GRADIENT_ENERGY * s


def start_kernel(sizes, own, payload, *refs):
    body = Body(sizes, refs, sizes[2])
    rows = own.shape[0]
    layer = lax.broadcasted_iota(jnp.int32, (body.depth, LANES), 0)
    low = lax.axis_index("sec") * rows
    here = (layer >= low) & (layer < low + rows)

    def place(value):
        return jnp.where(here, stack([value] * body.slabs), 0.0)

    strips = body.strips(own)
    trace = [s[0] for s in strips]
    inner = body.slab(
        [place(body.depth_sum(s, STIFF_BAND)) for s in strips],
        [place(body.depth_sum(s, MASS_BAND)) for s in strips],
    )
    table = body.corner_table([place(a) for a in trace])
    body.send(payload, [trace, inner], body.pack(table, NARROW))


def flux_tail(body, layer, mine, other, r0, v1, m1, tr, tv, payload):
    jump = body.jumps(mine, other)
    body.stand(jump, 1)

    def residual(z, stiff, mass):
        body.emit(r0, z, -TIME_STEP * (stiff + body.column(z, 1)), jump, -TIME_STEP, 0)

    body.stiff0(layer, residual)

    def image(z, stiff, mass):
        body.emit(v1, z, stiff, slot=1)
        m1[z] = mass

    body.stiff0(lambda z: r0[z], image, True)
    trace, inner = body.traces(r0, 0), body.traces(v1, 1)
    tr[...], tv[...] = stack(trace), stack(inner)
    body.copies = 1
    body.send(payload, [trace, inner], body.pack(body.corner_table(trace), NARROW))


def middle_kernel(sizes, *refs):
    slabs, refs = refs[: sizes[2]], refs[sizes[2] :]
    c, v0, tc, tv = refs[:4]
    body = Body(sizes, refs[4:])
    count = body.slabs
    rows = body.depth // count
    for k, slab in enumerate(slabs):
        c[pl.ds(lax.rem(lax.axis_index("sec") + k, count) * rows, rows)] = slab[...]

    def image(z, stiff, mass):
        v0[z] = stiff

    body.stiff0(lambda z: c[z], image)
    tc[...], tv[...] = stack(body.traces(c)), stack(body.traces(v0))


def first_kernel(sizes, c, v0, tc, tv0, recv, sc, r0, v1, m1, ts, tr, tv, sides, payload,
                 potential, *refs):
    body = Body(sizes, refs, sizes[2])
    depth, count = body.depth, body.slabs
    rows = depth // count
    high = recv.shape[0] // (body.patches * count)
    raw = []
    for f in range(4):
        q = body.partner(body.me, f)
        parts = [recv[pl.ds((q * count + s) * high, rows), :] for s in range(count)]
        raw.append(stack(parts + [body.take(recv, q, rows, depth)]))
    other, inner = body.oriented(raw, 2)
    mine = unstack(tc, depth)
    jump = body.jumps(mine, other)
    body.stand(jump)

    def make(z):
        body.emit(sc, z, v0[z] + body.column(z), jump)
        potential[z] = cubic(c[z], sc[z])

    mine_s = body.stiff_trace(unstack(tv0, depth), jump)
    other_s = body.other_stiff(recv, rows + depth, mine, other, inner, body.corners(), 1, NARROW)
    ts[...] = stack(mine_s)
    sides[0], sides[1] = stack(other), stack(other_s)
    mine_p = [cubic(x, s) for x, s in zip(mine, mine_s)]
    other_p = [cubic(x, s) for x, s in zip(other, other_s)]
    layer = body.lazy(potential, make)
    flux_tail(body, layer, mine_p, other_p, r0, v1, m1, tr, tv, payload)


def second_kernel(sizes, last, r0, v1, m1, tr, tv, recv, y, v2, m2, ty, tv2, payload, u1, *refs):
    if not last:
        tu, sides, *refs = refs
    body = Body(sizes, refs)
    depth = body.depth
    other, inner = body.received(recv, 2)
    mine = unstack(tr, depth)
    jump = body.jumps(mine, other)
    body.stand(jump)

    def make(z, jump=jump):
        body.emit(u1, z, v1[z] + body.column(z), jump)

    mine_s = body.stiff_trace(unstack(tv, depth), jump)
    other_s = body.other_stiff(
        recv, 2 * depth, mine, other, inner, body.corners(), 1, NARROW
    )
    if not last:
        tu[...] = stack(mine_s)
        sides[0], sides[1] = stack(other), stack(other_s)
    jump = body.jumps(mine_s, other_s)
    body.stand(jump, 1)

    def image(z, stiff, mass):
        value = m1[z] + TWICE * u1[z] + HALF * (stiff + body.column(z, 1))
        body.emit(y, z, value, jump, HALF, 0)

    body.stiff0(body.lazy(u1, make), image)
    sums = [[], [], []]

    def again(z, stiff, mass):
        body.emit(v2, z, stiff, slot=1)
        m2[z] = mass
        a, b = r0[z], y[z]
        for i, product in enumerate((a * a, a * b, b * b)):
            sums[i].append(jnp.sum(product, axis=0, keepdims=True))

    body.stiff0(lambda z: y[z], again, True)
    strips_y, strips = body.strips(y, 0), body.strips(v2, 1)
    trace, inner = [s[0] for s in strips_y], [s[0] for s in strips]
    ty[...], tv2[...] = stack(trace), stack(inner)
    mixed, arms = body.slab(
        [HALF * body.depth_sum(s, STIFF_BAND) for s in strips],
        [HALF * body.depth_sum(s, MASS_BAND) for s in strips],
        [body.depth_sum(s, MASS_BAND) for s in strips_y],
        trace,
    )
    outer = [TWICE * a + b for a, b in zip(inner, mixed)]
    table = body.corner_table(trace, inner, arms)
    for i in range(3):
        total = jnp.sum(stack(sums[i]), axis=1, keepdims=True)
        table = jnp.where(body.lane == SUMS + i, total, table)
    body.send(payload, [trace, inner, outer], body.pack(table, BROAD))


def third_kernel(sizes, last, r0, y, v2, m2, ty, tv2, recv, *refs):
    if last:
        t, base, payload, u2, zf = refs[:5]
        body = Body(sizes, refs[5:])
    else:
        t, base, u2, zf, tt, tu2, tz, sides, payload = refs[:9]
        body = Body(sizes, refs[9:])
    depth, patches = body.depth, body.patches
    at = 3 * depth
    packed = depth * BROAD // LANES
    known = recv[at : at + packed, :]
    for p in range(1, patches):
        known = known + recv[p * (at + packed) + at : (p + 1) * (at + packed), :]
    odd = lax.broadcasted_iota(jnp.int32, (packed, LANES), 0) & 1
    slot = lax.broadcasted_iota(jnp.int32, (packed, LANES), 1) + NARROW * odd
    slot = slot & (BROAD - 1)
    m0, m1, m2s = [
        jnp.sum(jnp.where(slot == SUMS + i, known, 0.0), keepdims=True) for i in range(3)
    ]
    a0 = m0 / m1
    other, inner, outer = body.received(recv, 3)
    corners = body.corners()
    mine = unstack(ty, depth)
    jump = body.jumps(mine, other)
    body.stand(jump)

    def make(z, jump=jump):
        body.emit(u2, z, v2[z] + body.column(z), jump)

    mine_s = body.stiff_trace(unstack(tv2, depth), jump)
    other_s = body.other_stiff(recv, at, mine, other, inner, corners, KINDS, BROAD)
    masses, stiffs, far = [], [], []
    for f in range(4):
        arm_m, arm_k, across = [], [], []
        for s in range(2):
            (q, kq, tq), (r, k, kind), (r2, k2) = corners[f][s]
            look = functools.partial(body.look, recv, at, side=s, width=BROAD)
            arm_m.append(look(q, KINDS * kq + tq) - look(r, KINDS * k + kind))
            arm_k.append(look(q, KINDS * kq + tq + 1) - look(r, KINDS * k + kind + 1))
            value = look(r, KINDS * k)
            across.append(
                look(r, KINDS * k + 1)
                + PENALTY * (value - other[f])
                + PENALTY * (value - look(r2, KINDS * k2))
            )
        theirs = PENALTY * (other[f] - mine[f])
        masses.append(MASS_BAND[0] * theirs + PENALTY * body.ends(*arm_m))
        stiffs.append(STIFF_BAND[0] * theirs + PENALTY * body.ends(*arm_k))
        far.append(body.ends(*across))
    pushed = body.slab(stiffs, masses)
    edge = body.first | body.last
    other_t = []
    for f in range(4):
        again = pushed[f] + PENALTY * (other_s[f] - mine_s[f])
        again = again + jnp.where(edge, PENALTY * (other_s[f] - far[f]), 0.0)
        image = outer[f] + TWICE * (other_s[f] - inner[f]) + HALF * again
        other_t.append(other[f] - a0 * image)
    jump_s = body.jumps(mine_s, other_s)
    body.stand(jump_s, 1)

    def turn(z, stiff, mass):
        image = m2[z] + TWICE * u2[z] + HALF * (stiff + body.column(z, 1))
        body.emit(t, z, y[z] - a0 * image, jump_s, -HALF * a0, 0)

    body.stiff0(body.lazy(u2, make), turn)
    mine_t = body.traces(t, 0)
    jump_t = body.jumps(mine_t, other_t)
    body.stand(jump_t)
    sums = [jnp.zeros((8, LANES), jnp.float32)] * 6

    def image(z, stiff, mass):
        body.emit(zf, z, stiff + body.column(z), jump_t, slot=None if last else 1)
        b, x, s = y[z], t[z], zf[z]
        a = r0[z] - a0 * b
        energy = x * (mass + TWICE * s) + HALF * (s * s)
        for i, product in enumerate((a * a, a * x, a * b, x * x, x * b, energy)):
            sums[i] = sums[i] + jnp.sum(product.reshape(LANES // 8, 8, LANES), axis=0)

    body.stiff0(lambda z: t[z], image, True)
    moments = jnp.zeros((1, LANES), jnp.float32)
    lane = lax.broadcasted_iota(jnp.int32, (1, LANES), 1)
    for i, value in enumerate(sums):
        value = jnp.sum(jnp.sum(value, axis=0, keepdims=True), axis=1, keepdims=True)
        moments = jnp.where(lane == i, value, moments)
    for i, value in enumerate((a0, m0, m1, m2s)):
        base[i : i + 1, :] = jnp.broadcast_to(value, (1, LANES))
    rows = payload.shape[0] // patches
    for to in range(patches):
        payload[to * rows : to * rows + 1, :] = moments
    if not last:
        trace = body.traces(zf, 1)
        tt[...], tu2[...], tz[...] = stack(mine_t), stack(mine_s), stack(trace)
        sides[0], sides[1], sides[2] = stack(other), stack(other_s), stack(other_t)
        for f in range(4):
            payload[pl.ds(body.partner(body.me, f) * rows + 1, depth), :] = trace[f]


def weights(patches, base, recv):
    rows = recv.shape[0] // patches
    total = recv[:1, :]
    for p in range(1, patches):
        total = total + recv[p * rows : p * rows + 1, :]
    a0, m0, m1, m2 = [base[i : i + 1, :1] for i in range(4)]
    rr1, g1, g2, tt, ty, tat = [total[:, i : i + 1] for i in range(6)]
    b0 = rr1 / m0
    a1 = rr1 / (g1 + 2.0 * b0 * g2 + b0 * b0 * m1)
    rr2 = rr1 - 2.0 * a1 * (g1 + b0 * g2) + a1 * a1 * (tt + 2.0 * b0 * ty + b0 * b0 * m2)
    b1 = rr2 / rr1
    shift = a1 * b0 / a0
    c1, c0, c2 = 1.0 + b1 + shift, b1 * b0 - shift, -a1
    a2 = rr2 / (
        c1 * c1 * g1
        + c0 * c0 * m1
        + c2 * c2 * tat
        + 2.0 * (c1 * c0 * g2 + c1 * c2 * tt + c0 * c2 * ty)
    )
    return a0 + a1 * (1.0 + b0) + a2 * (c1 + c0), -a0 * (a1 + a2 * c1), a2 * c2


def next_kernel(sizes, c, r0, y, t, sc, u1, u2, zf, tc, ts, tr, tu, ty, tu2, tt, tz,
                side_c, side_r, side_y, base, recv,
                cn, rn, v1, m1, trn, tvn, payload, potential, *refs):
    body = Body(sizes, refs)
    depth = body.depth
    x = weights(body.patches, base, recv)

    def mix(*values):
        return values[0] + x[0] * values[1] + x[1] * values[2] + x[2] * values[3]

    def make(z):
        cn[z] = mix(c[z], r0[z], y[z], t[z])
        potential[z] = cubic(cn[z], mix(sc[z], u1[z], u2[z], zf[z]))

    (side_z,) = body.received(recv, 1, 1)
    mine = cubic(
        mix(tc[...], tr[...], ty[...], tt[...]), mix(ts[...], tu[...], tu2[...], tz[...])
    )
    other = cubic(
        mix(side_c[0], side_r[0], side_y[0], side_y[2]),
        mix(side_c[1], side_r[1], side_y[1], stack(side_z)),
    )
    layer = body.lazy(potential, make)
    mine, other = unstack(mine, depth), unstack(other, depth)
    flux_tail(body, layer, mine, other, rn, v1, m1, trn, tvn, payload)


def last_kernel(patches, c, r0, y, t, base, recv, out):
    x0, x1, x2 = weights(patches, base, recv)
    rows = out.shape[0]
    low = lax.axis_index("sec") * rows
    for z in range(rows):
        k = low + z
        out[z] = c[k] + x0 * r0[k] + x1 * y[k] + x2 * t[k]


def shards(patches, slabs, concentration, partner, face_id, flip):
    own = concentration[0]
    rows = own.shape[0]
    depth = rows * slabs
    halves = [own]
    for k in range(1, slabs):
        halves.append(lax.ppermute(own, "sec", [((i + k) % slabs, i) for i in range(slabs)]))
    matrices = [jnp.asarray(x) for x in constants()]
    tables = [partner.T, face_id.T, flip.T]
    vmem, smem = pl.BlockSpec(memory_space=pltpu.VMEM), pl.BlockSpec(memory_space=pltpu.SMEM)
    params = pltpu.CompilerParams(vmem_limit_bytes=(4 + depth) << 20)

    def shape(*dims):
        return jax.ShapeDtypeStruct(dims, jnp.float32)

    field, trace, base = shape(depth, LANES, LANES), shape(4 * depth, LANES), shape(8, LANES)

    def sides(count):
        return shape(count, 4 * depth, LANES)

    def load(count):
        return shape(patches * count, LANES)

    def call(kernel, outs, *args, fields=0, consts=matrices, cost=None):
        count, head = len(args), 3 + len(consts)
        inside = [pltpu.VMEM((depth, LANES, LANES), jnp.float32)] * fields
        shared = [
            pltpu.VMEM((8, LANES + 2 * PAD, LANES), jnp.float32),
            pltpu.VMEM((2, -(-depth // 8), LANES, LANES), jnp.float32),
            pltpu.VMEM((LANES, LANES), jnp.float32),
            pltpu.VMEM((2, -(-depth // 8), LANES, LANES), jnp.float32),
        ]

        def run(*refs):
            common, rest = refs[:head], refs[head:]
            cut = len(rest) - len(shared)
            kernel((depth, patches, slabs), *rest[:cut], *common, *rest[cut:])

        return pl.pallas_call(
            run,
            out_shape=outs,
            in_specs=[smem] * 3 + [vmem] * (len(consts) + count),
            out_specs=[vmem] * len(outs),
            scratch_shapes=inside + shared,
            compiler_params=params,
            cost_estimate=cost,
            name=kernel.__name__.strip("<>"),
        )(*tables, *consts, *args)

    def swap(payload, axes="patch", parts=patches):
        rows = payload.shape[0] // parts
        moved = lax.all_to_all(payload.reshape(parts, 1, rows * LANES), axes, 0, 0)
        return moved.reshape(parts * rows, LANES)

    narrow, broad = depth * NARROW // LANES, depth * BROAD // LANES
    (payload,) = call(
        start_kernel,
        [load(slabs * (rows + depth + narrow))],
        own,
        consts=[],
        cost=pl.CostEstimate(flops=COST, bytes_accessed=4 * own.size, transcendentals=0),
    )
    c, v0, tc, tv0 = call(
        middle_kernel,
        [field, field, trace, trace],
        *halves,
        cost=pl.CostEstimate(flops=COST, bytes_accessed=4 * own.size, transcendentals=0),
    )
    sc, r0, v1, m1, ts, tr, tv, side_c, payload = call(
        first_kernel,
        [field] * 4 + [trace] * 3 + [sides(2), load(2 * depth + narrow)],
        c, v0, tc, tv0, swap(payload, ("patch", "sec"), patches * slabs),
        fields=1,
    )
    for step in range(STEPS):
        last = step + 1 == STEPS
        outs = [field] * 3 + [trace] * 2 + [load(3 * depth + broad)]
        y, v2, m2, ty, tv2, payload, *rest = call(
            lambda sizes, *refs, last=last: second_kernel(sizes, last, *refs),
            outs + ([] if last else [field, trace, sides(2)]),
            r0, v1, m1, tr, tv, swap(payload),
            fields=1 if last else 0,
        )
        if not last:
            u1, tu, side_r = rest
        outs = [field, base]
        if last:
            outs += [load(1)]
        else:
            outs += [field] * 2 + [trace] * 3 + [sides(3), load(1 + depth)]
        t, base_now, *rest = call(
            lambda sizes, *refs, last=last: third_kernel(sizes, last, *refs),
            outs,
            r0, y, v2, m2, ty, tv2, swap(payload),
            fields=2 if last else 0,
        )
        if last:
            (payload,) = rest
            break
        u2, zf, tt, tu2, tz, side_y, payload = rest
        c, r0, v1, m1, tr, tv, payload = call(
            next_kernel,
            [field] * 4 + [trace] * 2 + [load(2 * depth + narrow)],
            c, r0, y, t, sc, u1, u2, zf, tc, ts, tr, tu, ty, tu2, tt, tz,
            side_c, side_r, side_y, base_now, swap(payload),
            fields=1,
        )
    out = pl.pallas_call(
        functools.partial(last_kernel, patches),
        out_shape=shape(rows, LANES, LANES),
        in_specs=[vmem] * 6,
        out_specs=vmem,
        compiler_params=params,
    )(c, r0, y, t, base_now, swap(payload))
    return out[None]


def solution(mesh):
    placed = (P("patch", "sec", None, None), P(), P(), P())
    return jax.shard_map(
        functools.partial(shards, mesh.shape["patch"], mesh.shape["sec"]),
        mesh=mesh,
        in_specs=placed,
        out_specs=P("patch", "sec", None, None),
        check_vma=False,
    )
```

```python
import functools

import jax
import jax.numpy as jnp
import numpy as np
from jax import lax
from jax.experimental import pallas as pl
from jax.experimental.pallas import tpu as pltpu
from jax.sharding import PartitionSpec as P

STEPS = 2
MASS_BAND = (2416.0 / 5040.0, 1191.0 / 5040.0, 120.0 / 5040.0, 1.0 / 5040.0)
STIFF_BAND = (2.0 / 3.0, -0.125, -0.2, -1.0 / 120.0)
SCALE = 5040.0
MASS_HIGH, MASS_LOW = (2416.0, 1192.0, 120.0, 1.0), (0.0, -1.0, 0.0, 0.0)
STIFF_HIGH, STIFF_LOW = (3360.0, -632.0, -1008.0, -42.0), (0.0, 2.0, 0.0, 0.0)
PENALTY = 2.0
TIME_STEP = 1.0
STABILIZER = 2.0
GRADIENT_ENERGY = 0.5
HALF = TIME_STEP * GRADIENT_ENERGY
TWICE = TIME_STEP * STABILIZER
EXACT = lax.Precision.HIGHEST
LANES = 128
PAD = 8
KINDS = 6
SUMS = 4 * KINDS
NARROW, BROAD = 16, 32
COST = 1 << 34


def band_matrix(band, size):
    out = np.zeros((size, size), np.float32)
    for offset, value in enumerate(band):
        for row in range(size - offset):
            out[row, row + offset] = value
            out[row + offset, row] = value
    return out


def dot(left, right):
    return jnp.dot(left, right, precision=EXACT, preferred_element_type=jnp.float32)


def right_matrix(mass_band, stiff_band):
    mass, stiff = band_matrix(mass_band, LANES), band_matrix(stiff_band, LANES)
    return np.block([[mass, stiff], [np.zeros_like(mass), mass]])


def constants():
    high = right_matrix(MASS_HIGH, STIFF_HIGH).astype(jnp.bfloat16)
    low = right_matrix(MASS_LOW, STIFF_LOW).astype(jnp.bfloat16)
    return (np.concatenate([high, high, high, low]),)


def banded(distance, band, inside=None):
    out = jnp.zeros(distance.shape, jnp.float32)
    for offset, value in enumerate(band):
        hit = distance == offset
        out = jnp.where(hit if inside is None else hit & inside, value, out)
    return out


class Body:
    def __init__(self, sizes, refs, copies=1):
        self.depth, self.patches, self.slabs = sizes
        self.copies = copies
        self.tables, refs = refs[:3], refs[3:]
        self.near, self.strip, self.turned, self.stood = refs[-4:]
        self.pieces = refs[0] if len(refs) > 4 else None
        self.me = lax.axis_index("patch")
        self.lane = lax.broadcasted_iota(jnp.int32, (self.depth, LANES), 1)
        self.first, self.last = self.lane == 0, self.lane == LANES - 1
        self.wide = lax.broadcasted_iota(jnp.int32, (LANES, LANES), 1)
        self.edge = (self.wide == 0) | (self.wide == LANES - 1)
        row = lax.broadcasted_iota(jnp.int32, (LANES, LANES), 0)
        reverse = jnp.where(row + self.wide == LANES - 1, 1.0, 0.0).astype(jnp.bfloat16)
        self.reverse = stack([reverse] * 3)
        distance = jnp.abs(row - self.wide)
        if self.pieces is None:
            self.plain = jnp.concatenate(
                [banded(distance, MASS_BAND), banded(distance, STIFF_BAND)], axis=1
            )
        else:
            high = self.pieces[:LANES]
            self.plain = stack([high, high, high, self.pieces[6 * LANES : 7 * LANES]])

    def partner(self, patch, face):
        return self.tables[0][face, patch]

    def face_id(self, patch, face):
        return self.tables[1][face, patch]

    def flip(self, patch, face):
        return self.tables[2][face, patch]

    def split(self, value):
        pieces = []
        for last in (False, False, True):
            piece = value.astype(jnp.bfloat16)
            pieces.append(piece)
            if not last:
                value = value - piece.astype(jnp.float32)
        return pieces

    def stiff0(self, layer, finish, with_mass=False):
        depth = self.depth
        zeros = jnp.zeros((PAD, LANES), jnp.float32)
        for i in range(8):
            self.near[i, :PAD] = zeros
            self.near[i, PAD + LANES :] = zeros
        for z in range(depth):
            middle = layer(z)
            massed = (MASS_BAND[0] / SCALE) * middle
            stiffed = (STIFF_BAND[0] / SCALE) * middle
            for offset in (1, 2, 3):
                near = [layer(k) for k in (z - offset, z + offset) if 0 <= k < depth]
                if near:
                    both = near[0] if len(near) == 1 else near[0] + near[1]
                    massed = massed + (MASS_BAND[offset] / SCALE) * both
                    stiffed = stiffed + (STIFF_BAND[offset] / SCALE) * both
            pieces = self.split(jnp.concatenate([massed, stiffed], axis=1))
            pieces = jnp.concatenate(pieces + pieces[:1], axis=1)
            mixed = jnp.dot(pieces, self.pieces[...], preferred_element_type=jnp.float32)
            first, second = mixed[:, :LANES], mixed[:, LANES:]
            at, inside = 4 * (z % 2), slice(PAD, PAD + LANES)
            for o in (1, 2, 3):
                self.near[at + o, inside] = STIFF_BAND[o] * first + MASS_BAND[o] * second
            stiff = STIFF_BAND[0] * first + MASS_BAND[0] * second
            for o in (1, 2, 3):
                low, high = slice(PAD - o, PAD - o + LANES), slice(PAD + o, PAD + o + LANES)
                stiff = stiff + (self.near[at + o, low] + self.near[at + o, high])
            mass = None
            if with_mass:
                self.near[at, inside] = first
                mass = MASS_BAND[0] * first
                for o in (1, 2, 3):
                    low, high = slice(PAD - o, PAD - o + LANES), slice(PAD + o, PAD + o + LANES)
                    mass = mass + MASS_BAND[o] * (self.near[at, low] + self.near[at, high])
            finish(z, stiff, mass)

    def strips(self, field, slot=None, count=4):
        depth = field.shape[0]
        group = min(depth, 8)
        if slot is None:
            slot = 0
            for z in range(depth):
                rolled = pltpu.roll(field[z], (8 * (z % 8) + 4) % LANES, 1)
                pltpu.store(self.strip.at[slot, z // 8], rolled, mask=(self.wide >> 3) == z % 8)
        rows0 = [field[:, d, :] for d in range(count)]
        rows1 = [field[:, LANES - 1 - d, :] for d in range(count)]
        wanted = list(range(4 - count, 4 + count))
        pieces = {i: [] for i in wanted}
        for start in range(0, depth, group):
            self.turned[...] = jnp.transpose(self.strip[slot, start // 8])
            for i in wanted:
                pieces[i].append(self.turned[pl.ds(i, group, stride=8), :])
        columns = {i: jnp.concatenate(p, axis=0) if len(p) > 1 else p[0] for i, p in pieces.items()}
        return [
            rows0,
            rows1,
            [columns[4 + d] for d in range(count)],
            [columns[3 - d] for d in range(count)],
        ]

    def traces(self, field, slot=None):
        return [strip[0] for strip in self.strips(field, slot, 1)]

    def jumps(self, mine, other):
        return [PENALTY * (a - b) for a, b in zip(mine, other)]

    def stand(self, jump, slot=0):
        for start in range(0, self.depth, 8):
            self.turned[pl.ds(0, 8, stride=2), :] = jump[3][start : start + 8]
            self.turned[pl.ds(1, 8, stride=2), :] = jump[2][start : start + 8]
            self.stood[slot, start // 8] = jnp.transpose(self.turned[...])

    def column(self, z, slot=0):
        rolled = pltpu.roll(self.stood[slot, z // 8], (LANES - 2 * (z % 8) - 1) % LANES, 1)
        return jnp.where(self.edge, rolled, 0.0)

    def emit(self, field, z, value, jump=None, factor=1.0, slot=None):
        field[z] = value
        if jump is not None:
            field[z, :1, :] = field[z, :1, :] + factor * jump[0][z : z + 1]
            at = LANES - 1
            field[z, at:, :] = field[z, at:, :] + factor * jump[1][z : z + 1]
        if slot is not None:
            rolled = pltpu.roll(field[z], (8 * (z % 8) + 4) % LANES, 1)
            mask = (self.wide >> 3) == z % 8
            pltpu.store(self.strip.at[slot, z // 8], rolled, mask=mask)

    def lazy(self, field, make):
        made = set()

        def layer(z):
            if z not in made:
                made.add(z)
                make(z)
            return field[z]

        return layer

    def stiff_trace(self, inner, jump):
        out = []
        for f in range(4):
            side = f & 1
            low, high = (2, 3) if f < 2 else (0, 1)
            at = side * (LANES - 1)
            ends = []
            for face, end in ((low, 0), (high, LANES - 1)):
                shift = (end - at) % LANES
                ends.append(pltpu.roll(jump[face], shift, 1) if shift else jump[face])
            out.append(inner[f] + jump[f] + self.ends(*ends))
        return out

    def lane_bands(self, value):
        if self.pieces is None:
            return dot(value, self.plain)
        pieces = self.split(value * (1.0 / SCALE))
        pieces = jnp.concatenate(pieces + pieces[:1], axis=1)
        return jnp.dot(pieces, self.plain, preferred_element_type=jnp.float32)

    def third_axis(self, value, band):
        layer = lax.broadcasted_iota(jnp.int32, value.shape, 0)
        out = band[0] * value
        for o in (1, 2, 3):
            low = jnp.where(layer >= o, pltpu.roll(value, o, 0), 0.0)
            high = jnp.where(layer < self.depth - o, pltpu.roll(value, self.depth - o, 0), 0.0)
            out = out + band[o] * (low + high)
        return out

    def slab(self, stiffs, masses, plain=None, arms=None):
        n = 4 * self.depth
        rows = [stack(x) for x in (masses, stiffs, plain, arms) if x is not None]
        both = self.lane_bands(stack(rows))
        lower = both[n : 2 * n, :LANES] + both[:n, LANES:]
        if plain is not None:
            lower = lower + both[2 * n : 3 * n, :LANES]
        out = [
            self.third_axis(a, MASS_BAND) + self.third_axis(b, STIFF_BAND)
            for a, b in zip(unstack(lower, self.depth), unstack(both[:n, :LANES], self.depth))
        ]
        return out if arms is None else (out, both[3 * n :])

    def depth_sum(self, strip, band):
        out = band[0] * strip[0]
        for d in (1, 2, 3):
            out = out + band[d] * strip[d]
        return out

    def corner_table(self, trace, inner=None, arms=None):
        table = jnp.zeros((self.depth, LANES), jnp.float32)
        ends = (0, LANES - 1)
        kinds = 1 if inner is None else KINDS
        for rs in range(2):
            for cs in range(2):
                slot = kinds * (2 * rs + cs)
                values = [(trace[rs], ends[cs])]
                if inner is not None:
                    values.append((inner[rs], ends[cs]))
                    for face, end in ((rs, ends[cs]), (2 + cs, ends[rs])):
                        part = arms[face * self.depth : (face + 1) * self.depth]
                        values.append((part[:, :LANES], end))
                        values.append((part[:, LANES:], end))
                for kind, (value, end) in enumerate(values):
                    shift = (slot + kind - end) % LANES
                    rolled = pltpu.roll(value, shift, 1) if shift else value
                    table = jnp.where(self.lane == slot + kind, rolled, table)
        return table

    def pack(self, table, width):
        count = width // NARROW
        rows = []
        for start in range(0, self.depth, 8):
            for low in range(count):
                total = None
                for i in range(low, 8, count):
                    layer = table[start + i : start + i + 1]
                    part = pltpu.roll(layer, LANES - NARROW * i, 1) if i else layer
                    total = part if total is None else total + part
                rows.append(total)
        return stack(rows) if len(rows) > 1 else rows[0]

    def send(self, payload, groups, packed):
        copies = self.copies
        rows = payload.shape[0] // (self.patches * copies)
        for f in range(4):
            to, at = self.partner(self.me, f) * copies, 0
            for group in groups:
                high = group[f].shape[0]
                for s in range(copies):
                    payload[pl.ds((to + s) * rows + at, high), :] = group[f]
                at += high
        for to in range(self.patches * copies):
            payload[to * rows + at : (to + 1) * rows, :] = packed

    def take(self, recv, patch, lo, count):
        rows = recv.shape[0] // (self.patches * self.copies)
        out = None
        for s in range(self.copies):
            part = recv[pl.ds((patch * self.copies + s) * rows + lo, count), :]
            out = part if out is None else out + part
        return out

    def received(self, recv, count, at=0):
        rows = count * self.depth
        return self.oriented(
            [self.take(recv, self.partner(self.me, f), at, rows) for f in range(4)], count
        )

    def oriented(self, raw, count):
        depth = self.depth
        rows = count * depth
        pieces = jnp.concatenate(self.split(stack(raw)), axis=1)
        turned = jnp.dot(pieces, self.reverse, preferred_element_type=jnp.float32)
        out = []
        for f in range(4):
            flipped = self.flip(self.me, f) == 1
            out.append(jnp.where(flipped, turned[f * rows : (f + 1) * rows], raw[f]))
        return [[out[f][i * depth : (i + 1) * depth] for f in range(4)] for i in range(count)]

    def corner(self, face, side):
        q, f1 = self.partner(self.me, face), self.face_id(self.me, face)
        eq = side ^ self.flip(self.me, face)
        s1 = f1 & 1
        upright = f1 < 2
        f2 = jnp.where(upright, 2 + eq, eq)
        kq = jnp.where(upright, 2 * s1 + eq, 2 * eq + s1)
        tq = jnp.where(upright, 4, 2)
        r, g = self.partner(q, f2), self.face_id(q, f2)
        s2 = s1 ^ self.flip(q, f2)
        flat = g < 2
        k = jnp.where(flat, 2 * (g & 1) + s2, 2 * s2 + (g & 1))
        t = jnp.where(flat, 2, 4)
        g2 = jnp.where(flat, 2 + s2, s2)
        r2, h = self.partner(r, g2), self.face_id(r, g2)
        s4 = (g & 1) ^ self.flip(r, g2)
        k2 = jnp.where(h < 2, 2 * (h & 1) + s4, 2 * s4 + (h & 1))
        return (q, kq, tq), (r, k, t), (r2, k2)

    def corners(self):
        return [[self.corner(f, s) for s in range(2)] for f in range(4)]

    def look(self, recv, at, patch, lane, side, width):
        count = width // NARROW
        shift = (side * (LANES - 1) + LANES - lane) & (LANES - 1)
        packed = self.take(recv, patch, at, self.depth // 8 * count)
        odd = (lax.broadcasted_iota(jnp.int32, (8, LANES), 0) & 1) == 1
        out = []
        for k in range(0, self.depth // 8 * count, count):
            spread = jnp.broadcast_to(packed[k : k + 1], (8, LANES))
            if count == 2:
                spread = jnp.where(odd, packed[k + 1 : k + 2], spread)
            out.append(pltpu.roll(spread, 0, 1, stride=NARROW, stride_axis=0))
        return pltpu.roll(stack(out) if len(out) > 1 else out[0], shift, 1)

    def ends(self, low, high):
        return jnp.where(self.first, low, jnp.where(self.last, high, 0.0))

    def other_stiff(self, recv, at, mine, theirs, inner, corners, kinds, width):
        out = []
        edge = self.first | self.last
        for f in range(4):
            across = []
            for s in range(2):
                r, k, t = corners[f][s][1]
                across.append(self.look(recv, at, r, kinds * k, s, width))
            value = inner[f] + PENALTY * (theirs[f] - mine[f])
            far = PENALTY * (theirs[f] - self.ends(*across))
            out.append(value + jnp.where(edge, far, 0.0))
        return out


def stack(values):
    return jnp.concatenate(values, 0)


def unstack(value, depth):
    return [value[f * depth : (f + 1) * depth] for f in range(4)]


def cubic(x, s):
    return x * x * x - x + GRADIENT_ENERGY * s


def start_kernel(sizes, own, payload, *refs):
    body = Body(sizes, refs, sizes[2])
    rows = own.shape[0]
    layer = lax.broadcasted_iota(jnp.int32, (body.depth, LANES), 0)
    low = lax.axis_index("sec") * rows
    here = (layer >= low) & (layer < low + rows)

    def place(value):
        return jnp.where(here, stack([value] * body.slabs), 0.0)

    strips = body.strips(own)
    trace = [s[0] for s in strips]
    inner = body.slab(
        [place(body.depth_sum(s, STIFF_BAND)) for s in strips],
        [place(body.depth_sum(s, MASS_BAND)) for s in strips],
    )
    table = body.corner_table([place(a) for a in trace])
    body.send(payload, [trace, inner], body.pack(table, NARROW))


def fetch_kernel(sizes, partner, face_id, flip, own, payload, *refs):
    here, sems, refs = refs[:4], refs[4], refs[5:]
    sources = (partner, face_id, flip, own)
    copies = [
        pltpu.make_async_copy(source, target, sems.at[i])
        for i, (source, target) in enumerate(zip(sources, here))
    ]
    for copy in copies:
        copy.start()
    for copy in copies:
        copy.wait()
    start_kernel(sizes, here[3], payload, *here[:3], *refs)


def flux_tail(body, layer, mine, other, r0, v1, m1, tr, tv, payload):
    jump = body.jumps(mine, other)
    body.stand(jump, 1)

    def residual(z, stiff, mass):
        body.emit(r0, z, -TIME_STEP * (stiff + body.column(z, 1)), jump, -TIME_STEP, 0)

    body.stiff0(layer, residual)

    def image(z, stiff, mass):
        body.emit(v1, z, stiff, slot=1)
        m1[z] = mass

    body.stiff0(lambda z: r0[z], image, True)
    trace, inner = body.traces(r0, 0), body.traces(v1, 1)
    tr[...], tv[...] = stack(trace), stack(inner)
    body.copies = 1
    body.send(payload, [trace, inner], body.pack(body.corner_table(trace), NARROW))


def middle_kernel(sizes, *refs):
    slabs, refs = refs[: sizes[2]], refs[sizes[2] :]
    c, v0, tc, tv = refs[:4]
    body = Body(sizes, refs[4:])
    count = body.slabs
    rows = body.depth // count
    for k, slab in enumerate(slabs):
        c[pl.ds(lax.rem(lax.axis_index("sec") + k, count) * rows, rows)] = slab[...]

    def image(z, stiff, mass):
        v0[z] = stiff

    body.stiff0(lambda z: c[z], image)
    tc[...], tv[...] = stack(body.traces(c)), stack(body.traces(v0))


def first_kernel(sizes, c, v0, tc, tv0, recv, sc, r0, v1, m1, ts, tr, tv, sides, payload,
                 potential, *refs):
    body = Body(sizes, refs, sizes[2])
    depth, count = body.depth, body.slabs
    rows = depth // count
    high = recv.shape[0] // (body.patches * count)
    raw = []
    for f in range(4):
        q = body.partner(body.me, f)
        parts = [recv[pl.ds((q * count + s) * high, rows), :] for s in range(count)]
        raw.append(stack(parts + [body.take(recv, q, rows, depth)]))
    other, inner = body.oriented(raw, 2)
    mine = unstack(tc, depth)
    jump = body.jumps(mine, other)
    body.stand(jump)

    def make(z):
        body.emit(sc, z, v0[z] + body.column(z), jump)
        potential[z] = cubic(c[z], sc[z])

    mine_s = body.stiff_trace(unstack(tv0, depth), jump)
    other_s = body.other_stiff(recv, rows + depth, mine, other, inner, body.corners(), 1, NARROW)
    ts[...] = stack(mine_s)
    sides[0], sides[1] = stack(other), stack(other_s)
    mine_p = [cubic(x, s) for x, s in zip(mine, mine_s)]
    other_p = [cubic(x, s) for x, s in zip(other, other_s)]
    layer = body.lazy(potential, make)
    flux_tail(body, layer, mine_p, other_p, r0, v1, m1, tr, tv, payload)


def second_kernel(sizes, last, r0, v1, m1, tr, tv, recv, y, v2, m2, ty, tv2, payload, u1, *refs):
    if not last:
        tu, sides, *refs = refs
    body = Body(sizes, refs)
    depth = body.depth
    other, inner = body.received(recv, 2)
    mine = unstack(tr, depth)
    jump = body.jumps(mine, other)
    body.stand(jump)

    def make(z, jump=jump):
        body.emit(u1, z, v1[z] + body.column(z), jump)

    mine_s = body.stiff_trace(unstack(tv, depth), jump)
    other_s = body.other_stiff(
        recv, 2 * depth, mine, other, inner, body.corners(), 1, NARROW
    )
    if not last:
        tu[...] = stack(mine_s)
        sides[0], sides[1] = stack(other), stack(other_s)
    jump = body.jumps(mine_s, other_s)
    body.stand(jump, 1)

    def image(z, stiff, mass):
        value = m1[z] + TWICE * u1[z] + HALF * (stiff + body.column(z, 1))
        body.emit(y, z, value, jump, HALF, 0)

    body.stiff0(body.lazy(u1, make), image)
    sums = [[], [], []]

    def again(z, stiff, mass):
        body.emit(v2, z, stiff, slot=1)
        m2[z] = mass
        a, b = r0[z], y[z]
        for i, product in enumerate((a * a, a * b, b * b)):
            sums[i].append(jnp.sum(product, axis=0, keepdims=True))

    body.stiff0(lambda z: y[z], again, True)
    strips_y, strips = body.strips(y, 0), body.strips(v2, 1)
    trace, inner = [s[0] for s in strips_y], [s[0] for s in strips]
    ty[...], tv2[...] = stack(trace), stack(inner)
    mixed, arms = body.slab(
        [HALF * body.depth_sum(s, STIFF_BAND) for s in strips],
        [HALF * body.depth_sum(s, MASS_BAND) for s in strips],
        [body.depth_sum(s, MASS_BAND) for s in strips_y],
        trace,
    )
    outer = [TWICE * a + b for a, b in zip(inner, mixed)]
    table = body.corner_table(trace, inner, arms)
    for i in range(3):
        total = jnp.sum(stack(sums[i]), axis=1, keepdims=True)
        table = jnp.where(body.lane == SUMS + i, total, table)
    body.send(payload, [trace, inner, outer], body.pack(table, BROAD))


def third_kernel(sizes, last, r0, y, v2, m2, ty, tv2, recv, *refs):
    if last:
        t, base, payload, u2, zf = refs[:5]
        body = Body(sizes, refs[5:])
    else:
        t, base, u2, zf, tt, tu2, tz, sides, payload = refs[:9]
        body = Body(sizes, refs[9:])
    depth, patches = body.depth, body.patches
    at = 3 * depth
    packed = depth * BROAD // LANES
    known = recv[at : at + packed, :]
    for p in range(1, patches):
        known = known + recv[p * (at + packed) + at : (p + 1) * (at + packed), :]
    odd = lax.broadcasted_iota(jnp.int32, (packed, LANES), 0) & 1
    slot = lax.broadcasted_iota(jnp.int32, (packed, LANES), 1) + NARROW * odd
    slot = slot & (BROAD - 1)
    m0, m1, m2s = [
        jnp.sum(jnp.where(slot == SUMS + i, known, 0.0), keepdims=True) for i in range(3)
    ]
    a0 = m0 / m1
    other, inner, outer = body.received(recv, 3)
    corners = body.corners()
    mine = unstack(ty, depth)
    jump = body.jumps(mine, other)
    body.stand(jump)

    def make(z, jump=jump):
        body.emit(u2, z, v2[z] + body.column(z), jump)

    mine_s = body.stiff_trace(unstack(tv2, depth), jump)
    other_s = body.other_stiff(recv, at, mine, other, inner, corners, KINDS, BROAD)
    masses, stiffs, far = [], [], []
    for f in range(4):
        arm_m, arm_k, across = [], [], []
        for s in range(2):
            (q, kq, tq), (r, k, kind), (r2, k2) = corners[f][s]
            look = functools.partial(body.look, recv, at, side=s, width=BROAD)
            arm_m.append(look(q, KINDS * kq + tq) - look(r, KINDS * k + kind))
            arm_k.append(look(q, KINDS * kq + tq + 1) - look(r, KINDS * k + kind + 1))
            value = look(r, KINDS * k)
            across.append(
                look(r, KINDS * k + 1)
                + PENALTY * (value - other[f])
                + PENALTY * (value - look(r2, KINDS * k2))
            )
        theirs = PENALTY * (other[f] - mine[f])
        masses.append(MASS_BAND[0] * theirs + PENALTY * body.ends(*arm_m))
        stiffs.append(STIFF_BAND[0] * theirs + PENALTY * body.ends(*arm_k))
        far.append(body.ends(*across))
    pushed = body.slab(stiffs, masses)
    edge = body.first | body.last
    other_t = []
    for f in range(4):
        again = pushed[f] + PENALTY * (other_s[f] - mine_s[f])
        again = again + jnp.where(edge, PENALTY * (other_s[f] - far[f]), 0.0)
        image = outer[f] + TWICE * (other_s[f] - inner[f]) + HALF * again
        other_t.append(other[f] - a0 * image)
    jump_s = body.jumps(mine_s, other_s)
    body.stand(jump_s, 1)

    def turn(z, stiff, mass):
        image = m2[z] + TWICE * u2[z] + HALF * (stiff + body.column(z, 1))
        body.emit(t, z, y[z] - a0 * image, jump_s, -HALF * a0, 0)

    body.stiff0(body.lazy(u2, make), turn)
    mine_t = body.traces(t, 0)
    jump_t = body.jumps(mine_t, other_t)
    body.stand(jump_t)
    sums = [jnp.zeros((8, LANES), jnp.float32)] * 6

    def image(z, stiff, mass):
        body.emit(zf, z, stiff + body.column(z), jump_t, slot=None if last else 1)
        b, x, s = y[z], t[z], zf[z]
        a = r0[z] - a0 * b
        energy = x * (mass + TWICE * s) + HALF * (s * s)
        for i, product in enumerate((a * a, a * x, a * b, x * x, x * b, energy)):
            sums[i] = sums[i] + jnp.sum(product.reshape(LANES // 8, 8, LANES), axis=0)

    body.stiff0(lambda z: t[z], image, True)
    moments = jnp.zeros((1, LANES), jnp.float32)
    lane = lax.broadcasted_iota(jnp.int32, (1, LANES), 1)
    for i, value in enumerate(sums):
        value = jnp.sum(jnp.sum(value, axis=0, keepdims=True), axis=1, keepdims=True)
        moments = jnp.where(lane == i, value, moments)
    for i, value in enumerate((a0, m0, m1, m2s)):
        base[i : i + 1, :] = jnp.broadcast_to(value, (1, LANES))
    rows = payload.shape[0] // patches
    for to in range(patches):
        payload[to * rows : to * rows + 1, :] = moments
    if not last:
        trace = body.traces(zf, 1)
        tt[...], tu2[...], tz[...] = stack(mine_t), stack(mine_s), stack(trace)
        sides[0], sides[1], sides[2] = stack(other), stack(other_s), stack(other_t)
        for f in range(4):
            payload[pl.ds(body.partner(body.me, f) * rows + 1, depth), :] = trace[f]


def weights(patches, base, recv):
    rows = recv.shape[0] // patches
    total = recv[:1, :]
    for p in range(1, patches):
        total = total + recv[p * rows : p * rows + 1, :]
    a0, m0, m1, m2 = [base[i : i + 1, :1] for i in range(4)]
    rr1, g1, g2, tt, ty, tat = [total[:, i : i + 1] for i in range(6)]
    b0 = rr1 / m0
    a1 = rr1 / (g1 + 2.0 * b0 * g2 + b0 * b0 * m1)
    rr2 = rr1 - 2.0 * a1 * (g1 + b0 * g2) + a1 * a1 * (tt + 2.0 * b0 * ty + b0 * b0 * m2)
    b1 = rr2 / rr1
    shift = a1 * b0 / a0
    c1, c0, c2 = 1.0 + b1 + shift, b1 * b0 - shift, -a1
    a2 = rr2 / (
        c1 * c1 * g1
        + c0 * c0 * m1
        + c2 * c2 * tat
        + 2.0 * (c1 * c0 * g2 + c1 * c2 * tt + c0 * c2 * ty)
    )
    return a0 + a1 * (1.0 + b0) + a2 * (c1 + c0), -a0 * (a1 + a2 * c1), a2 * c2


def next_kernel(sizes, c, r0, y, t, sc, u1, u2, zf, tc, ts, tr, tu, ty, tu2, tt, tz,
                side_c, side_r, side_y, base, recv,
                cn, rn, v1, m1, trn, tvn, payload, potential, *refs):
    body = Body(sizes, refs)
    depth = body.depth
    x = weights(body.patches, base, recv)

    def mix(*values):
        return values[0] + x[0] * values[1] + x[1] * values[2] + x[2] * values[3]

    def make(z):
        cn[z] = mix(c[z], r0[z], y[z], t[z])
        potential[z] = cubic(cn[z], mix(sc[z], u1[z], u2[z], zf[z]))

    (side_z,) = body.received(recv, 1, 1)
    mine = cubic(
        mix(tc[...], tr[...], ty[...], tt[...]), mix(ts[...], tu[...], tu2[...], tz[...])
    )
    other = cubic(
        mix(side_c[0], side_r[0], side_y[0], side_y[2]),
        mix(side_c[1], side_r[1], side_y[1], stack(side_z)),
    )
    layer = body.lazy(potential, make)
    mine, other = unstack(mine, depth), unstack(other, depth)
    flux_tail(body, layer, mine, other, rn, v1, m1, trn, tvn, payload)


def last_kernel(patches, c, r0, y, t, base, recv, out):
    x0, x1, x2 = weights(patches, base, recv)
    rows = out.shape[0]
    low = lax.axis_index("sec") * rows
    for z in range(rows):
        k = low + z
        out[z] = c[k] + x0 * r0[k] + x1 * y[k] + x2 * t[k]


def shards(patches, slabs, concentration, partner, face_id, flip):
    own = concentration[0]
    rows = own.shape[0]
    depth = rows * slabs
    halves = [own]
    for k in range(1, slabs):
        halves.append(lax.ppermute(own, "sec", [((i + k) % slabs, i) for i in range(slabs)]))
    matrices = [jnp.asarray(x) for x in constants()]
    tables = [partner.T, face_id.T, flip.T]
    vmem, smem = pl.BlockSpec(memory_space=pltpu.VMEM), pl.BlockSpec(memory_space=pltpu.SMEM)
    params = pltpu.CompilerParams(vmem_limit_bytes=(4 + depth) << 20)

    def shape(*dims):
        return jax.ShapeDtypeStruct(dims, jnp.float32)

    field, trace, base = shape(depth, LANES, LANES), shape(4 * depth, LANES), shape(8, LANES)

    def sides(count):
        return shape(count, 4 * depth, LANES)

    def load(count):
        return shape(patches * count, LANES)

    shared = [
        pltpu.VMEM((8, LANES + 2 * PAD, LANES), jnp.float32),
        pltpu.VMEM((2, -(-depth // 8), LANES, LANES), jnp.float32),
        pltpu.VMEM((LANES, LANES), jnp.float32),
        pltpu.VMEM((2, -(-depth // 8), LANES, LANES), jnp.float32),
    ]

    def call(kernel, outs, *args, fields=0, consts=matrices, cost=None):
        count, head = len(args), 3 + len(consts)
        inside = [pltpu.VMEM((depth, LANES, LANES), jnp.float32)] * fields
        def run(*refs):
            common, rest = refs[:head], refs[head:]
            cut = len(rest) - len(shared)
            kernel((depth, patches, slabs), *rest[:cut], *common, *rest[cut:])

        return pl.pallas_call(
            run,
            out_shape=outs,
            in_specs=[smem] * 3 + [vmem] * (len(consts) + count),
            out_specs=[vmem] * len(outs),
            scratch_shapes=inside + shared,
            compiler_params=params,
            cost_estimate=cost,
            name=kernel.__name__.strip("<>"),
        )(*tables, *consts, *args)

    def swap(payload, axes="patch", parts=patches):
        rows = payload.shape[0] // parts
        moved = lax.all_to_all(payload.reshape(parts, 1, rows * LANES), axes, 0, 0)
        return moved.reshape(parts * rows, LANES)

    cost = pl.CostEstimate(flops=COST, bytes_accessed=4 * own.size, transcendentals=0)
    narrow, broad = depth * NARROW // LANES, depth * BROAD // LANES
    payload = pl.pallas_call(
        functools.partial(fetch_kernel, (depth, patches, slabs)),
        out_shape=load(slabs * (rows + depth + narrow)),
        in_specs=[pl.BlockSpec(memory_space=pltpu.HBM)] * 4,
        out_specs=vmem,
        scratch_shapes=[pltpu.SMEM((4, patches), jnp.int32)] * 3
        + [pltpu.VMEM(own.shape, jnp.float32), pltpu.SemaphoreType.DMA((4,))]
        + shared,
        compiler_params=params,
        cost_estimate=cost,
        name="start_kernel",
    )(*[pltpu.with_memory_space_constraint(x, pltpu.HBM) for x in (*tables, own)])
    c, v0, tc, tv0 = call(
        middle_kernel,
        [field, field, trace, trace],
        *halves,
        cost=pl.CostEstimate(flops=COST, bytes_accessed=4 * own.size, transcendentals=0),
    )
    sc, r0, v1, m1, ts, tr, tv, side_c, payload = call(
        first_kernel,
        [field] * 4 + [trace] * 3 + [sides(2), load(2 * depth + narrow)],
        c, v0, tc, tv0, swap(payload, ("patch", "sec"), patches * slabs),
        fields=1,
    )
    for step in range(STEPS):
        last = step + 1 == STEPS
        outs = [field] * 3 + [trace] * 2 + [load(3 * depth + broad)]
        y, v2, m2, ty, tv2, payload, *rest = call(
            lambda sizes, *refs, last=last: second_kernel(sizes, last, *refs),
            outs + ([] if last else [field, trace, sides(2)]),
            r0, v1, m1, tr, tv, swap(payload),
            fields=1 if last else 0,
        )
        if not last:
            u1, tu, side_r = rest
        outs = [field, base]
        if last:
            outs += [load(1)]
        else:
            outs += [field] * 2 + [trace] * 3 + [sides(3), load(1 + depth)]
        t, base_now, *rest = call(
            lambda sizes, *refs, last=last: third_kernel(sizes, last, *refs),
            outs,
            r0, y, v2, m2, ty, tv2, swap(payload),
            fields=2 if last else 0,
        )
        if last:
            (payload,) = rest
            break
        u2, zf, tt, tu2, tz, side_y, payload = rest
        c, r0, v1, m1, tr, tv, payload = call(
            next_kernel,
            [field] * 4 + [trace] * 2 + [load(2 * depth + narrow)],
            c, r0, y, t, sc, u1, u2, zf, tc, ts, tr, tu, ty, tu2, tt, tz,
            side_c, side_r, side_y, base_now, swap(payload),
            fields=1,
        )
    out = pl.pallas_call(
        functools.partial(last_kernel, patches),
        out_shape=shape(rows, LANES, LANES),
        in_specs=[vmem] * 6,
        out_specs=vmem,
        compiler_params=params,
    )(c, r0, y, t, base_now, swap(payload))
    return out[None]


def solution(mesh):
    placed = (P("patch", "sec", None, None), P(), P(), P())
    return jax.shard_map(
        functools.partial(shards, mesh.shape["patch"], mesh.shape["sec"]),
        mesh=mesh,
        in_specs=placed,
        out_specs=P("patch", "sec", None, None),
        check_vma=False,
    )
```

```python
import functools

import jax
import jax.numpy as jnp
import numpy as np
from jax import lax
from jax.experimental import pallas as pl
from jax.experimental.pallas import tpu as pltpu
from jax.sharding import PartitionSpec as P

STEPS = 2
MASS_BAND = (2416.0 / 5040.0, 1191.0 / 5040.0, 120.0 / 5040.0, 1.0 / 5040.0)
STIFF_BAND = (2.0 / 3.0, -0.125, -0.2, -1.0 / 120.0)
SCALE = 5040.0
MASS_HIGH, MASS_LOW = (2416.0, 1192.0, 120.0, 1.0), (0.0, -1.0, 0.0, 0.0)
STIFF_HIGH, STIFF_LOW = (3360.0, -632.0, -1008.0, -42.0), (0.0, 2.0, 0.0, 0.0)
PENALTY = 2.0
TIME_STEP = 1.0
STABILIZER = 2.0
GRADIENT_ENERGY = 0.5
HALF = TIME_STEP * GRADIENT_ENERGY
TWICE = TIME_STEP * STABILIZER
EXACT = lax.Precision.HIGHEST
LANES = 128
PAD = 8
KINDS = 6
SUMS = 4 * KINDS
NARROW, BROAD = 16, 32
COST = 1 << 34


def band_matrix(band, size):
    out = np.zeros((size, size), np.float32)
    for offset, value in enumerate(band):
        for row in range(size - offset):
            out[row, row + offset] = value
            out[row + offset, row] = value
    return out


def dot(left, right):
    return jnp.dot(left, right, precision=EXACT, preferred_element_type=jnp.float32)


def right_matrix(mass_band, stiff_band):
    mass, stiff = band_matrix(mass_band, LANES), band_matrix(stiff_band, LANES)
    return np.block([[mass, stiff], [np.zeros_like(mass), mass]])


def constants():
    high = right_matrix(MASS_HIGH, STIFF_HIGH).astype(jnp.bfloat16)
    low = right_matrix(MASS_LOW, STIFF_LOW).astype(jnp.bfloat16)
    return (np.concatenate([high, high, high, low]),)


def banded(distance, band, inside=None):
    out = jnp.zeros(distance.shape, jnp.float32)
    for offset, value in enumerate(band):
        hit = distance == offset
        out = jnp.where(hit if inside is None else hit & inside, value, out)
    return out


class Body:
    def __init__(self, sizes, refs, copies=1):
        self.depth, self.patches, self.slabs = sizes
        self.copies, self.spread = copies, {}
        self.tables, refs = refs[:3], refs[3:]
        self.near, self.strip, self.turned, self.stood = refs[-4:]
        self.pieces = refs[0] if len(refs) > 4 else None
        self.me = lax.axis_index("patch")
        self.lane = lax.broadcasted_iota(jnp.int32, (self.depth, LANES), 1)
        self.first, self.last = self.lane == 0, self.lane == LANES - 1
        self.wide = lax.broadcasted_iota(jnp.int32, (LANES, LANES), 1)
        self.edge = (self.wide == 0) | (self.wide == LANES - 1)
        row = lax.broadcasted_iota(jnp.int32, (LANES, LANES), 0)
        reverse = jnp.where(row + self.wide == LANES - 1, 1.0, 0.0).astype(jnp.bfloat16)
        self.reverse = stack([reverse] * 3)
        distance = jnp.abs(row - self.wide)
        if self.pieces is None:
            self.plain = jnp.concatenate(
                [banded(distance, MASS_BAND), banded(distance, STIFF_BAND)], axis=1
            )
        else:
            high = self.pieces[:LANES]
            self.plain = stack([high, high, high, self.pieces[6 * LANES : 7 * LANES]])

    def partner(self, patch, face):
        return self.tables[0][face, patch]

    def face_id(self, patch, face):
        return self.tables[1][face, patch]

    def flip(self, patch, face):
        return self.tables[2][face, patch]

    def split(self, value):
        pieces = []
        for last in (False, False, True):
            piece = value.astype(jnp.bfloat16)
            pieces.append(piece)
            if not last:
                value = value - piece.astype(jnp.float32)
        return pieces

    def stiff0(self, layer, finish, with_mass=False):
        depth = self.depth
        zeros = jnp.zeros((PAD, LANES), jnp.float32)
        for i in range(8):
            self.near[i, :PAD] = zeros
            self.near[i, PAD + LANES :] = zeros
        for z in range(depth):
            middle = layer(z)
            massed = (MASS_BAND[0] / SCALE) * middle
            stiffed = (STIFF_BAND[0] / SCALE) * middle
            for offset in (1, 2, 3):
                near = [layer(k) for k in (z - offset, z + offset) if 0 <= k < depth]
                if near:
                    both = near[0] if len(near) == 1 else near[0] + near[1]
                    massed = massed + (MASS_BAND[offset] / SCALE) * both
                    stiffed = stiffed + (STIFF_BAND[offset] / SCALE) * both
            pieces = self.split(jnp.concatenate([massed, stiffed], axis=1))
            pieces = jnp.concatenate(pieces + pieces[:1], axis=1)
            mixed = jnp.dot(pieces, self.pieces[...], preferred_element_type=jnp.float32)
            first, second = mixed[:, :LANES], mixed[:, LANES:]
            at, inside = 4 * (z % 2), slice(PAD, PAD + LANES)
            for o in (1, 2, 3):
                self.near[at + o, inside] = STIFF_BAND[o] * first + MASS_BAND[o] * second
            stiff = STIFF_BAND[0] * first + MASS_BAND[0] * second
            for o in (1, 2, 3):
                low, high = slice(PAD - o, PAD - o + LANES), slice(PAD + o, PAD + o + LANES)
                stiff = stiff + (self.near[at + o, low] + self.near[at + o, high])
            mass = None
            if with_mass:
                self.near[at, inside] = first
                mass = MASS_BAND[0] * first
                for o in (1, 2, 3):
                    low, high = slice(PAD - o, PAD - o + LANES), slice(PAD + o, PAD + o + LANES)
                    mass = mass + MASS_BAND[o] * (self.near[at, low] + self.near[at, high])
            finish(z, stiff, mass)

    def strips(self, field, slot=None, count=4):
        depth = field.shape[0]
        group = min(depth, 8)
        if slot is None:
            slot = 0
            for z in range(depth):
                rolled = pltpu.roll(field[z], (8 * (z % 8) + 4) % LANES, 1)
                pltpu.store(self.strip.at[slot, z // 8], rolled, mask=(self.wide >> 3) == z % 8)
        rows0 = [field[:, d, :] for d in range(count)]
        rows1 = [field[:, LANES - 1 - d, :] for d in range(count)]
        wanted = list(range(4 - count, 4 + count))
        pieces = {i: [] for i in wanted}
        for start in range(0, depth, group):
            self.turned[...] = jnp.transpose(self.strip[slot, start // 8])
            for i in wanted:
                pieces[i].append(self.turned[pl.ds(i, group, stride=8), :])
        columns = {i: jnp.concatenate(p, axis=0) if len(p) > 1 else p[0] for i, p in pieces.items()}
        return [
            rows0,
            rows1,
            [columns[4 + d] for d in range(count)],
            [columns[3 - d] for d in range(count)],
        ]

    def traces(self, field, slot=None):
        return [strip[0] for strip in self.strips(field, slot, 1)]

    def jumps(self, mine, other):
        return [PENALTY * (a - b) for a, b in zip(mine, other)]

    def stand(self, jump, slot=0):
        for start in range(0, self.depth, 8):
            self.turned[pl.ds(0, 8, stride=2), :] = jump[3][start : start + 8]
            self.turned[pl.ds(1, 8, stride=2), :] = jump[2][start : start + 8]
            self.stood[slot, start // 8] = jnp.transpose(self.turned[...])

    def column(self, z, slot=0):
        rolled = pltpu.roll(self.stood[slot, z // 8], (LANES - 2 * (z % 8) - 1) % LANES, 1)
        return jnp.where(self.edge, rolled, 0.0)

    def emit(self, field, z, value, jump=None, factor=1.0, slot=None):
        field[z] = value
        if jump is not None:
            field[z, :1, :] = field[z, :1, :] + factor * jump[0][z : z + 1]
            at = LANES - 1
            field[z, at:, :] = field[z, at:, :] + factor * jump[1][z : z + 1]
        if slot is not None:
            rolled = pltpu.roll(field[z], (8 * (z % 8) + 4) % LANES, 1)
            mask = (self.wide >> 3) == z % 8
            pltpu.store(self.strip.at[slot, z // 8], rolled, mask=mask)

    def lazy(self, field, make):
        made = set()

        def layer(z):
            if z not in made:
                made.add(z)
                make(z)
            return field[z]

        return layer

    def stiff_trace(self, inner, jump):
        out = []
        for f in range(4):
            side = f & 1
            low, high = (2, 3) if f < 2 else (0, 1)
            at = side * (LANES - 1)
            ends = []
            for face, end in ((low, 0), (high, LANES - 1)):
                shift = (end - at) % LANES
                ends.append(pltpu.roll(jump[face], shift, 1) if shift else jump[face])
            out.append(inner[f] + jump[f] + self.ends(*ends))
        return out

    def lane_bands(self, value):
        if self.pieces is None:
            return dot(value, self.plain)
        pieces = self.split(value * (1.0 / SCALE))
        pieces = jnp.concatenate(pieces + pieces[:1], axis=1)
        return jnp.dot(pieces, self.plain, preferred_element_type=jnp.float32)

    def third_axis(self, value, band):
        layer = lax.broadcasted_iota(jnp.int32, value.shape, 0)
        out = band[0] * value
        for o in (1, 2, 3):
            low = jnp.where(layer >= o, pltpu.roll(value, o, 0), 0.0)
            high = jnp.where(layer < self.depth - o, pltpu.roll(value, self.depth - o, 0), 0.0)
            out = out + band[o] * (low + high)
        return out

    def slab(self, stiffs, masses, plain=None, arms=None):
        n = 4 * self.depth
        rows = [stack(x) for x in (masses, stiffs, plain, arms) if x is not None]
        both = self.lane_bands(stack(rows))
        lower = both[n : 2 * n, :LANES] + both[:n, LANES:]
        if plain is not None:
            lower = lower + both[2 * n : 3 * n, :LANES]
        out = [
            self.third_axis(a, MASS_BAND) + self.third_axis(b, STIFF_BAND)
            for a, b in zip(unstack(lower, self.depth), unstack(both[:n, :LANES], self.depth))
        ]
        return out if arms is None else (out, both[3 * n :])

    def depth_sum(self, strip, band):
        out = band[0] * strip[0]
        for d in (1, 2, 3):
            out = out + band[d] * strip[d]
        return out

    def corner_table(self, trace, inner=None, arms=None):
        table = jnp.zeros((self.depth, LANES), jnp.float32)
        ends = (0, LANES - 1)
        kinds = 1 if inner is None else KINDS
        for rs in range(2):
            for cs in range(2):
                slot = kinds * (2 * rs + cs)
                values = [(trace[rs], ends[cs])]
                if inner is not None:
                    values.append((inner[rs], ends[cs]))
                    for face, end in ((rs, ends[cs]), (2 + cs, ends[rs])):
                        part = arms[face * self.depth : (face + 1) * self.depth]
                        values.append((part[:, :LANES], end))
                        values.append((part[:, LANES:], end))
                for kind, (value, end) in enumerate(values):
                    shift = (slot + kind - end) % LANES
                    rolled = pltpu.roll(value, shift, 1) if shift else value
                    table = jnp.where(self.lane == slot + kind, rolled, table)
        return table

    def pack(self, table, width):
        count = width // NARROW
        rows = []
        for start in range(0, self.depth, 8):
            for low in range(count):
                total = None
                for i in range(low, 8, count):
                    layer = table[start + i : start + i + 1]
                    part = pltpu.roll(layer, LANES - NARROW * i, 1) if i else layer
                    total = part if total is None else total + part
                rows.append(total)
        return stack(rows) if len(rows) > 1 else rows[0]

    def send(self, payload, groups, packed):
        copies = self.copies
        rows = payload.shape[0] // (self.patches * copies)
        for f in range(4):
            to, at = self.partner(self.me, f) * copies, 0
            for group in groups:
                high = group[f].shape[0]
                for s in range(copies):
                    payload[pl.ds((to + s) * rows + at, high), :] = group[f]
                at += high
        for to in range(self.patches * copies):
            payload[to * rows + at : (to + 1) * rows, :] = packed

    def take(self, recv, patch, lo, count):
        rows = recv.shape[0] // (self.patches * self.copies)
        out = None
        for s in range(self.copies):
            part = recv[pl.ds((patch * self.copies + s) * rows + lo, count), :]
            out = part if out is None else out + part
        return out

    def received(self, recv, count, at=0):
        rows = count * self.depth
        return self.oriented(
            [self.take(recv, self.partner(self.me, f), at, rows) for f in range(4)], count
        )

    def oriented(self, raw, count):
        depth = self.depth
        rows = count * depth
        pieces = jnp.concatenate(self.split(stack(raw)), axis=1)
        turned = jnp.dot(pieces, self.reverse, preferred_element_type=jnp.float32)
        out = []
        for f in range(4):
            flipped = self.flip(self.me, f) == 1
            out.append(jnp.where(flipped, turned[f * rows : (f + 1) * rows], raw[f]))
        return [[out[f][i * depth : (i + 1) * depth] for f in range(4)] for i in range(count)]

    def corner(self, face, side):
        q, f1 = self.partner(self.me, face), self.face_id(self.me, face)
        eq = side ^ self.flip(self.me, face)
        s1 = f1 & 1
        upright = f1 < 2
        f2 = jnp.where(upright, 2 + eq, eq)
        kq = jnp.where(upright, 2 * s1 + eq, 2 * eq + s1)
        tq = jnp.where(upright, 4, 2)
        r, g = self.partner(q, f2), self.face_id(q, f2)
        s2 = s1 ^ self.flip(q, f2)
        flat = g < 2
        k = jnp.where(flat, 2 * (g & 1) + s2, 2 * s2 + (g & 1))
        t = jnp.where(flat, 2, 4)
        g2 = jnp.where(flat, 2 + s2, s2)
        r2, h = self.partner(r, g2), self.face_id(r, g2)
        s4 = (g & 1) ^ self.flip(r, g2)
        k2 = jnp.where(h < 2, 2 * (h & 1) + s4, 2 * s4 + (h & 1))
        return (q, kq, tq), (r, k, t), (r2, k2)

    def corners(self):
        return [[self.corner(f, s) for s in range(2)] for f in range(4)]

    def look(self, recv, at, patch, lane, side, width):
        count = width // NARROW
        shift = (side * (LANES - 1) + LANES - lane) & (LANES - 1)
        known = self.spread.get(id(patch))
        if known is not None:
            return pltpu.roll(known[1], shift, 1)
        packed = self.take(recv, patch, at, self.depth // 8 * count)
        odd = (lax.broadcasted_iota(jnp.int32, (8, LANES), 0) & 1) == 1
        out = []
        for k in range(0, self.depth // 8 * count, count):
            spread = jnp.broadcast_to(packed[k : k + 1], (8, LANES))
            if count == 2:
                spread = jnp.where(odd, packed[k + 1 : k + 2], spread)
            out.append(pltpu.roll(spread, 0, 1, stride=NARROW, stride_axis=0))
        spread = stack(out) if len(out) > 1 else out[0]
        self.spread[id(patch)] = (patch, spread)
        return pltpu.roll(spread, shift, 1)

    def ends(self, low, high):
        return jnp.where(self.first, low, jnp.where(self.last, high, 0.0))

    def other_stiff(self, recv, at, mine, theirs, inner, corners, kinds, width):
        out = []
        edge = self.first | self.last
        for f in range(4):
            across = []
            for s in range(2):
                r, k, t = corners[f][s][1]
                across.append(self.look(recv, at, r, kinds * k, s, width))
            value = inner[f] + PENALTY * (theirs[f] - mine[f])
            far = PENALTY * (theirs[f] - self.ends(*across))
            out.append(value + jnp.where(edge, far, 0.0))
        return out


def stack(values):
    return jnp.concatenate(values, 0)


def unstack(value, depth):
    return [value[f * depth : (f + 1) * depth] for f in range(4)]


def cubic(x, s):
    return x * x * x - x + GRADIENT_ENERGY * s


def start_kernel(sizes, own, payload, *refs):
    body = Body(sizes, refs, sizes[2])
    rows = own.shape[0]
    layer = lax.broadcasted_iota(jnp.int32, (body.depth, LANES), 0)
    low = lax.axis_index("sec") * rows
    here = (layer >= low) & (layer < low + rows)

    def place(value):
        return jnp.where(here, stack([value] * body.slabs), 0.0)

    strips = body.strips(own)
    trace = [s[0] for s in strips]
    inner = body.slab(
        [place(body.depth_sum(s, STIFF_BAND)) for s in strips],
        [place(body.depth_sum(s, MASS_BAND)) for s in strips],
    )
    table = body.corner_table([place(a) for a in trace])
    body.send(payload, [trace, inner], body.pack(table, NARROW))


def fetch_kernel(sizes, partner, face_id, flip, own, payload, *refs):
    here, sems, refs = refs[:4], refs[4], refs[5:]
    sources = (partner, face_id, flip, own)
    copies = [
        pltpu.make_async_copy(source, target, sems.at[i])
        for i, (source, target) in enumerate(zip(sources, here))
    ]
    for copy in copies:
        copy.start()
    for copy in copies:
        copy.wait()
    start_kernel(sizes, here[3], payload, *here[:3], *refs)


def flux_tail(body, layer, mine, other, r0, v1, m1, tr, tv, payload):
    jump = body.jumps(mine, other)
    body.stand(jump, 1)

    def residual(z, stiff, mass):
        body.emit(r0, z, -TIME_STEP * (stiff + body.column(z, 1)), jump, -TIME_STEP, 0)

    body.stiff0(layer, residual)

    def image(z, stiff, mass):
        body.emit(v1, z, stiff, slot=1)
        m1[z] = mass

    body.stiff0(lambda z: r0[z], image, True)
    trace, inner = body.traces(r0, 0), body.traces(v1, 1)
    tr[...], tv[...] = stack(trace), stack(inner)
    body.copies = 1
    body.send(payload, [trace, inner], body.pack(body.corner_table(trace), NARROW))


def middle_kernel(sizes, *refs):
    slabs, refs = refs[: sizes[2]], refs[sizes[2] :]
    c, v0, tc, tv = refs[:4]
    body = Body(sizes, refs[4:])
    count = body.slabs
    rows = body.depth // count
    for k, slab in enumerate(slabs):
        c[pl.ds(lax.rem(lax.axis_index("sec") + k, count) * rows, rows)] = slab[...]

    def image(z, stiff, mass):
        v0[z] = stiff

    body.stiff0(lambda z: c[z], image)
    tc[...], tv[...] = stack(body.traces(c)), stack(body.traces(v0))


def first_kernel(sizes, c, v0, tc, tv0, recv, sc, r0, v1, m1, ts, tr, tv, sides, payload,
                 potential, *refs):
    body = Body(sizes, refs, sizes[2])
    depth, count = body.depth, body.slabs
    rows = depth // count
    high = recv.shape[0] // (body.patches * count)
    raw = []
    for f in range(4):
        q = body.partner(body.me, f)
        parts = [recv[pl.ds((q * count + s) * high, rows), :] for s in range(count)]
        raw.append(stack(parts + [body.take(recv, q, rows, depth)]))
    other, inner = body.oriented(raw, 2)
    mine = unstack(tc, depth)
    jump = body.jumps(mine, other)
    body.stand(jump)

    def make(z):
        body.emit(sc, z, v0[z] + body.column(z), jump)
        potential[z] = cubic(c[z], sc[z])

    mine_s = body.stiff_trace(unstack(tv0, depth), jump)
    other_s = body.other_stiff(recv, rows + depth, mine, other, inner, body.corners(), 1, NARROW)
    ts[...] = stack(mine_s)
    sides[0], sides[1] = stack(other), stack(other_s)
    mine_p = [cubic(x, s) for x, s in zip(mine, mine_s)]
    other_p = [cubic(x, s) for x, s in zip(other, other_s)]
    layer = body.lazy(potential, make)
    flux_tail(body, layer, mine_p, other_p, r0, v1, m1, tr, tv, payload)


def second_kernel(sizes, last, r0, v1, m1, tr, tv, recv, y, v2, m2, ty, tv2, payload, u1, *refs):
    if not last:
        tu, sides, *refs = refs
    body = Body(sizes, refs)
    depth = body.depth
    other, inner = body.received(recv, 2)
    mine = unstack(tr, depth)
    jump = body.jumps(mine, other)
    body.stand(jump)

    def make(z, jump=jump):
        body.emit(u1, z, v1[z] + body.column(z), jump)

    mine_s = body.stiff_trace(unstack(tv, depth), jump)
    other_s = body.other_stiff(
        recv, 2 * depth, mine, other, inner, body.corners(), 1, NARROW
    )
    if not last:
        tu[...] = stack(mine_s)
        sides[0], sides[1] = stack(other), stack(other_s)
    jump = body.jumps(mine_s, other_s)
    body.stand(jump, 1)

    def image(z, stiff, mass):
        value = m1[z] + TWICE * u1[z] + HALF * (stiff + body.column(z, 1))
        body.emit(y, z, value, jump, HALF, 0)

    body.stiff0(body.lazy(u1, make), image)
    sums = [[], [], []]

    def again(z, stiff, mass):
        body.emit(v2, z, stiff, slot=1)
        m2[z] = mass
        a, b = r0[z], y[z]
        for i, product in enumerate((a * a, a * b, b * b)):
            sums[i].append(jnp.sum(product, axis=0, keepdims=True))

    body.stiff0(lambda z: y[z], again, True)
    strips_y, strips = body.strips(y, 0), body.strips(v2, 1)
    trace, inner = [s[0] for s in strips_y], [s[0] for s in strips]
    ty[...], tv2[...] = stack(trace), stack(inner)
    mixed, arms = body.slab(
        [HALF * body.depth_sum(s, STIFF_BAND) for s in strips],
        [HALF * body.depth_sum(s, MASS_BAND) for s in strips],
        [body.depth_sum(s, MASS_BAND) for s in strips_y],
        trace,
    )
    outer = [TWICE * a + b for a, b in zip(inner, mixed)]
    table = body.corner_table(trace, inner, arms)
    for i in range(3):
        total = jnp.sum(stack(sums[i]), axis=1, keepdims=True)
        table = jnp.where(body.lane == SUMS + i, total, table)
    body.send(payload, [trace, inner, outer], body.pack(table, BROAD))


def third_kernel(sizes, last, r0, y, v2, m2, ty, tv2, recv, *refs):
    if last:
        t, base, payload, u2, zf = refs[:5]
        body = Body(sizes, refs[5:])
    else:
        t, base, u2, zf, tt, tu2, tz, sides, payload = refs[:9]
        body = Body(sizes, refs[9:])
    depth, patches = body.depth, body.patches
    at = 3 * depth
    packed = depth * BROAD // LANES
    known = recv[at : at + packed, :]
    for p in range(1, patches):
        known = known + recv[p * (at + packed) + at : (p + 1) * (at + packed), :]
    odd = lax.broadcasted_iota(jnp.int32, (packed, LANES), 0) & 1
    slot = lax.broadcasted_iota(jnp.int32, (packed, LANES), 1) + NARROW * odd
    slot = slot & (BROAD - 1)
    m0, m1, m2s = [
        jnp.sum(jnp.where(slot == SUMS + i, known, 0.0), keepdims=True) for i in range(3)
    ]
    a0 = m0 / m1
    other, inner, outer = body.received(recv, 3)
    corners = body.corners()
    mine = unstack(ty, depth)
    jump = body.jumps(mine, other)
    body.stand(jump)

    def make(z, jump=jump):
        body.emit(u2, z, v2[z] + body.column(z), jump)

    mine_s = body.stiff_trace(unstack(tv2, depth), jump)
    other_s = body.other_stiff(recv, at, mine, other, inner, corners, KINDS, BROAD)
    masses, stiffs, far = [], [], []
    for f in range(4):
        arm_m, arm_k, across = [], [], []
        for s in range(2):
            (q, kq, tq), (r, k, kind), (r2, k2) = corners[f][s]
            look = functools.partial(body.look, recv, at, side=s, width=BROAD)
            arm_m.append(look(q, KINDS * kq + tq) - look(r, KINDS * k + kind))
            arm_k.append(look(q, KINDS * kq + tq + 1) - look(r, KINDS * k + kind + 1))
            value = look(r, KINDS * k)
            across.append(
                look(r, KINDS * k + 1)
                + PENALTY * (value - other[f])
                + PENALTY * (value - look(r2, KINDS * k2))
            )
        theirs = PENALTY * (other[f] - mine[f])
        masses.append(MASS_BAND[0] * theirs + PENALTY * body.ends(*arm_m))
        stiffs.append(STIFF_BAND[0] * theirs + PENALTY * body.ends(*arm_k))
        far.append(body.ends(*across))
    pushed = body.slab(stiffs, masses)
    edge = body.first | body.last
    other_t = []
    for f in range(4):
        again = pushed[f] + PENALTY * (other_s[f] - mine_s[f])
        again = again + jnp.where(edge, PENALTY * (other_s[f] - far[f]), 0.0)
        image = outer[f] + TWICE * (other_s[f] - inner[f]) + HALF * again
        other_t.append(other[f] - a0 * image)
    jump_s = body.jumps(mine_s, other_s)
    body.stand(jump_s, 1)

    def turn(z, stiff, mass):
        image = m2[z] + TWICE * u2[z] + HALF * (stiff + body.column(z, 1))
        body.emit(t, z, y[z] - a0 * image, jump_s, -HALF * a0, 0)

    body.stiff0(body.lazy(u2, make), turn)
    mine_t = body.traces(t, 0)
    jump_t = body.jumps(mine_t, other_t)
    body.stand(jump_t)
    sums = [jnp.zeros((8, LANES), jnp.float32)] * 6

    def image(z, stiff, mass):
        body.emit(zf, z, stiff + body.column(z), jump_t, slot=None if last else 1)
        b, x, s = y[z], t[z], zf[z]
        a = r0[z] - a0 * b
        energy = x * (mass + TWICE * s) + HALF * (s * s)
        for i, product in enumerate((a * a, a * x, a * b, x * x, x * b, energy)):
            sums[i] = sums[i] + jnp.sum(product.reshape(LANES // 8, 8, LANES), axis=0)

    body.stiff0(lambda z: t[z], image, True)
    moments = jnp.zeros((1, LANES), jnp.float32)
    lane = lax.broadcasted_iota(jnp.int32, (1, LANES), 1)
    for i, value in enumerate(sums):
        value = jnp.sum(jnp.sum(value, axis=0, keepdims=True), axis=1, keepdims=True)
        moments = jnp.where(lane == i, value, moments)
    for i, value in enumerate((a0, m0, m1, m2s)):
        base[i : i + 1, :] = jnp.broadcast_to(value, (1, LANES))
    rows = payload.shape[0] // patches
    for to in range(patches):
        payload[to * rows : to * rows + 1, :] = moments
    if not last:
        trace = body.traces(zf, 1)
        tt[...], tu2[...], tz[...] = stack(mine_t), stack(mine_s), stack(trace)
        sides[0], sides[1], sides[2] = stack(other), stack(other_s), stack(other_t)
        for f in range(4):
            payload[pl.ds(body.partner(body.me, f) * rows + 1, depth), :] = trace[f]


def weights(patches, base, recv):
    rows = recv.shape[0] // patches
    total = recv[:1, :]
    for p in range(1, patches):
        total = total + recv[p * rows : p * rows + 1, :]
    a0, m0, m1, m2 = [base[i : i + 1, :1] for i in range(4)]
    rr1, g1, g2, tt, ty, tat = [total[:, i : i + 1] for i in range(6)]
    b0 = rr1 / m0
    a1 = rr1 / (g1 + 2.0 * b0 * g2 + b0 * b0 * m1)
    rr2 = rr1 - 2.0 * a1 * (g1 + b0 * g2) + a1 * a1 * (tt + 2.0 * b0 * ty + b0 * b0 * m2)
    b1 = rr2 / rr1
    shift = a1 * b0 / a0
    c1, c0, c2 = 1.0 + b1 + shift, b1 * b0 - shift, -a1
    a2 = rr2 / (
        c1 * c1 * g1
        + c0 * c0 * m1
        + c2 * c2 * tat
        + 2.0 * (c1 * c0 * g2 + c1 * c2 * tt + c0 * c2 * ty)
    )
    return a0 + a1 * (1.0 + b0) + a2 * (c1 + c0), -a0 * (a1 + a2 * c1), a2 * c2


def next_kernel(sizes, c, r0, y, t, sc, u1, u2, zf, tc, ts, tr, tu, ty, tu2, tt, tz,
                side_c, side_r, side_y, base, recv,
                cn, rn, v1, m1, trn, tvn, payload, potential, *refs):
    body = Body(sizes, refs)
    depth = body.depth
    x = weights(body.patches, base, recv)

    def mix(*values):
        return values[0] + x[0] * values[1] + x[1] * values[2] + x[2] * values[3]

    def make(z):
        cn[z] = mix(c[z], r0[z], y[z], t[z])
        potential[z] = cubic(cn[z], mix(sc[z], u1[z], u2[z], zf[z]))

    (side_z,) = body.received(recv, 1, 1)
    mine = cubic(
        mix(tc[...], tr[...], ty[...], tt[...]), mix(ts[...], tu[...], tu2[...], tz[...])
    )
    other = cubic(
        mix(side_c[0], side_r[0], side_y[0], side_y[2]),
        mix(side_c[1], side_r[1], side_y[1], stack(side_z)),
    )
    layer = body.lazy(potential, make)
    mine, other = unstack(mine, depth), unstack(other, depth)
    flux_tail(body, layer, mine, other, rn, v1, m1, trn, tvn, payload)


def last_kernel(patches, c, r0, y, t, base, recv, out):
    x0, x1, x2 = weights(patches, base, recv)
    rows = out.shape[0]
    low = lax.axis_index("sec") * rows
    for z in range(rows):
        k = low + z
        out[z] = c[k] + x0 * r0[k] + x1 * y[k] + x2 * t[k]


def shards(patches, slabs, concentration, partner, face_id, flip):
    own = concentration[0]
    rows = own.shape[0]
    depth = rows * slabs
    halves = [own]
    for k in range(1, slabs):
        halves.append(lax.ppermute(own, "sec", [((i + k) % slabs, i) for i in range(slabs)]))
    matrices = [jnp.asarray(x) for x in constants()]
    tables = [partner.T, face_id.T, flip.T]
    vmem, smem = pl.BlockSpec(memory_space=pltpu.VMEM), pl.BlockSpec(memory_space=pltpu.SMEM)
    params = pltpu.CompilerParams(vmem_limit_bytes=(4 + depth) << 20)

    def shape(*dims):
        return jax.ShapeDtypeStruct(dims, jnp.float32)

    field, trace, base = shape(depth, LANES, LANES), shape(4 * depth, LANES), shape(8, LANES)

    def sides(count):
        return shape(count, 4 * depth, LANES)

    def load(count):
        return shape(patches * count, LANES)

    shared = [
        pltpu.VMEM((8, LANES + 2 * PAD, LANES), jnp.float32),
        pltpu.VMEM((2, -(-depth // 8), LANES, LANES), jnp.float32),
        pltpu.VMEM((LANES, LANES), jnp.float32),
        pltpu.VMEM((2, -(-depth // 8), LANES, LANES), jnp.float32),
    ]

    def call(kernel, outs, *args, fields=0, consts=matrices, cost=None):
        count, head = len(args), 3 + len(consts)
        inside = [pltpu.VMEM((depth, LANES, LANES), jnp.float32)] * fields
        def run(*refs):
            common, rest = refs[:head], refs[head:]
            cut = len(rest) - len(shared)
            kernel((depth, patches, slabs), *rest[:cut], *common, *rest[cut:])

        return pl.pallas_call(
            run,
            out_shape=outs,
            in_specs=[smem] * 3 + [vmem] * (len(consts) + count),
            out_specs=[vmem] * len(outs),
            scratch_shapes=inside + shared,
            compiler_params=params,
            cost_estimate=cost,
            name=kernel.__name__.strip("<>"),
        )(*tables, *consts, *args)

    def swap(payload, axes="patch", parts=patches):
        rows = payload.shape[0] // parts
        moved = lax.all_to_all(payload.reshape(parts, 1, rows * LANES), axes, 0, 0)
        return moved.reshape(parts * rows, LANES)

    cost = pl.CostEstimate(flops=COST, bytes_accessed=4 * own.size, transcendentals=0)
    narrow, broad = depth * NARROW // LANES, depth * BROAD // LANES
    payload = pl.pallas_call(
        functools.partial(fetch_kernel, (depth, patches, slabs)),
        out_shape=load(slabs * (rows + depth + narrow)),
        in_specs=[pl.BlockSpec(memory_space=pltpu.HBM)] * 4,
        out_specs=vmem,
        scratch_shapes=[pltpu.SMEM((4, patches), jnp.int32)] * 3
        + [pltpu.VMEM(own.shape, jnp.float32), pltpu.SemaphoreType.DMA((4,))]
        + shared,
        compiler_params=params,
        cost_estimate=cost,
        name="start_kernel",
    )(*[pltpu.with_memory_space_constraint(x, pltpu.HBM) for x in (*tables, own)])
    c, v0, tc, tv0 = call(
        middle_kernel,
        [field, field, trace, trace],
        *halves,
        cost=pl.CostEstimate(flops=COST, bytes_accessed=4 * own.size, transcendentals=0),
    )
    sc, r0, v1, m1, ts, tr, tv, side_c, payload = call(
        first_kernel,
        [field] * 4 + [trace] * 3 + [sides(2), load(2 * depth + narrow)],
        c, v0, tc, tv0, swap(payload, ("patch", "sec"), patches * slabs),
        fields=1,
    )
    for step in range(STEPS):
        last = step + 1 == STEPS
        outs = [field] * 3 + [trace] * 2 + [load(3 * depth + broad)]
        y, v2, m2, ty, tv2, payload, *rest = call(
            lambda sizes, *refs, last=last: second_kernel(sizes, last, *refs),
            outs + ([] if last else [field, trace, sides(2)]),
            r0, v1, m1, tr, tv, swap(payload),
            fields=1 if last else 0,
        )
        if not last:
            u1, tu, side_r = rest
        outs = [field, base]
        if last:
            outs += [load(1)]
        else:
            outs += [field] * 2 + [trace] * 3 + [sides(3), load(1 + depth)]
        t, base_now, *rest = call(
            lambda sizes, *refs, last=last: third_kernel(sizes, last, *refs),
            outs,
            r0, y, v2, m2, ty, tv2, swap(payload),
            fields=2 if last else 0,
        )
        if last:
            (payload,) = rest
            break
        u2, zf, tt, tu2, tz, side_y, payload = rest
        c, r0, v1, m1, tr, tv, payload = call(
            next_kernel,
            [field] * 4 + [trace] * 2 + [load(2 * depth + narrow)],
            c, r0, y, t, sc, u1, u2, zf, tc, ts, tr, tu, ty, tu2, tt, tz,
            side_c, side_r, side_y, base_now, swap(payload),
            fields=1,
        )
    out = pl.pallas_call(
        functools.partial(last_kernel, patches),
        out_shape=shape(rows, LANES, LANES),
        in_specs=[vmem] * 6,
        out_specs=vmem,
        compiler_params=params,
    )(c, r0, y, t, base_now, swap(payload))
    return out[None]


def solution(mesh):
    placed = (P("patch", "sec", None, None), P(), P(), P())
    return jax.shard_map(
        functools.partial(shards, mesh.shape["patch"], mesh.shape["sec"]),
        mesh=mesh,
        in_specs=placed,
        out_specs=P("patch", "sec", None, None),
        check_vma=False,
    )
```
